32 devices in a mesh: dp: 8 (over y, x, core), lat: 4 (over z).
Axes of the slice: x: 2, y: 2, z: 4, core: 2. Of those that a mesh axis runs over, the one named last changes fastest.
Arguments:
- media: bfloat16 [4, 16, 1280, 1024], P(None, 'dp', 'lat'), may hold values from -6 to 6
- latents: bfloat16 [4, 16, 64, 1024], P(None, 'dp', 'lat'), may hold values from -6 to 6
- counts: int32 [4, 16], P(None, 'dp'), may hold values from 1 to 5
- cotangent: bfloat16 [4, 16, 64, 1024], P(None, 'dp', 'lat'), may hold values from -6 to 6
- gain_media: bfloat16 [1024], P('dp'), may hold values from 0.25 to 1.75
- bias_media: bfloat16 [1024], P('dp'), may hold values from -3 to 3
- gain_latent: bfloat16 [1024], P('dp'), may hold values from 0.25 to 1.75
- bias_latent: bfloat16 [1024], P('dp'), may hold values from -3 to 3
- gain_ff: bfloat16 [1024], P('dp'), may hold values from 0.25 to 1.75
- bias_ff: bfloat16 [1024], P('dp'), may hold values from -3 to 3
- w_query: bfloat16 [1024, 512], P('dp'), may hold values from -0.375 to 0.375
- w_keyval: bfloat16 [1024, 1024], P('dp'), may hold values from -0.1875 to 0.1875
- w_out: bfloat16 [512, 1024], P('dp'), may hold values from -1 to 1
- w_up: bfloat16 [1024, 4096], P('dp'), may hold values from -0.1875 to 0.1875
- w_down: bfloat16 [4096, 1024], P('dp'), may hold values from -0.09375 to 0.09375
Outputs:
- latents_out: bfloat16 [4, 16, 64, 1024], P(None, 'dp', 'lat')
- media_grad: bfloat16 [4, 16, 1280, 1024], P(None, 'dp', 'lat')
- latent_grad: bfloat16 [4, 16, 64, 1024], P(None, 'dp', 'lat')
- grad_gain_media: float32 [1024], P('dp')
- grad_bias_media: float32 [1024], P('dp')
- grad_gain_latent: float32 [1024], P('dp')
- grad_bias_latent: float32 [1024], P('dp')
- grad_gain_ff: float32 [1024], P('dp')
- grad_bias_ff: float32 [1024], P('dp')
- grad_query: float32 [1024, 512], P('dp')
- grad_keyval: float32 [1024, 1024], P('dp')
- grad_out: float32 [512, 1024], P('dp')
- grad_up: float32 [1024, 4096], P('dp')
- grad_down: float32 [4096, 1024], P('dp')
The draws below stay inside these ranges and needn't reach their ends.
Inputs may be any that keep to these rules, and one draw needn't show every extreme that they name: `counts`: number of images of a sample; its media rows from 256 * count on are padding.
All inputs are finite; a program needn't handle non-finite values.
Results may differ from the reference program's by a relative error of at most 0.017.
Values may be sent and summed in bfloat16 or wider, within the bound.
A program may use at most 248 MiB of HBM per device.

```python
import jax
import jax.numpy as jnp
from jax import lax

D = 1024
HEADS = 8
HEAD = 64
FF = 4096
NLAT = 64
VIS = 256
SLOTS = 5
MICRO = 4
INNER = 512
ROWS = 1280
SAMPLES = 16


def touch_ends(array, own_key, low, top_value):
    place = [jax.random.randint(jax.random.fold_in(own_key, axis), (), 0, length) for axis, length in enumerate(array.shape)]
    widest = array.shape.index(max(array.shape))
    next_to = place[:widest] + [(place[widest] + 1) % array.shape[widest]] + place[widest + 1:]
    return array.at[tuple(place)].set(low).at[tuple(next_to)].set(top_value)


def shard_levels(rng, shape, split, least, top_value):
    level, own = 1.0, jax.random.fold_in(rng, 6)
    for axis_at, shards_of in split:
        steps = jnp.exp(jax.random.uniform(jax.random.fold_in(own, axis_at), (shards_of,), jnp.float32, least / len(split), top_value / len(split)))
        level = level * jnp.repeat(steps, shape[axis_at] // shards_of).reshape([-1 if axis == axis_at else 1 for axis in range(len(shape))])
    return level


def gaussian(own_key, extent, spread, bound, shards=(), kind=jnp.bfloat16):
    level = shard_levels(own_key, extent, shards, -0.22, 0.18) if shards else 1.0
    values = jax.random.normal(own_key, extent, jnp.float32) * spread * level
    return jnp.minimum(jnp.maximum(values, -bound), bound).astype(kind)


def setup_inputs(seed: int = 0) -> dict:
    arg_keys = jax.random.split(jax.random.key(seed), 16)
    media = gaussian(arg_keys[0], (MICRO, SAMPLES, ROWS, D), 1.0, 6.0, ((1, 8), (2, 4)))
    latents = gaussian(arg_keys[1], (MICRO, SAMPLES, NLAT, D), 1.0, 6.0, ((1, 8), (2, 4)))
    counts = touch_ends(jax.random.randint(arg_keys[2], (MICRO, SAMPLES), 1, SLOTS + 1), jax.random.fold_in(arg_keys[2], 1), 1, SLOTS).astype(jnp.int32)
    cotangent = gaussian(arg_keys[3], (MICRO, SAMPLES, NLAT, D), 1.0, 6.0, ((1, 8), (2, 4)))
    gain_media = jnp.clip(1.0 + 0.15 * jax.random.normal(arg_keys[4], (D,), jnp.float32), 0.25, 1.75).astype(jnp.bfloat16)
    bias_media = gaussian(arg_keys[5], (D,), 0.5, 3.0, ((0, 8),))
    gain_latent = jnp.clip(1.0 + 0.15 * jax.random.normal(arg_keys[6], (D,), jnp.float32), 0.25, 1.75).astype(jnp.bfloat16)
    bias_latent = gaussian(arg_keys[7], (D,), 0.5, 3.0, ((0, 8),))
    gain_ff = jnp.clip(1.0 + 0.15 * jax.random.normal(arg_keys[8], (D,), jnp.float32), 0.25, 1.75).astype(jnp.bfloat16)
    bias_ff = gaussian(arg_keys[9], (D,), 0.5, 3.0, ((0, 8),))
    w_query = gaussian(arg_keys[10], (D, INNER), (D // 4) ** -0.5, 0.375, ((0, 8),))
    w_keyval = gaussian(arg_keys[11], (D, 2 * INNER), D ** -0.5, 0.1875, ((0, 8),))
    w_out = gaussian(arg_keys[12], (INNER, D), (INNER // 16) ** -0.5, 1.0, ((0, 8),))
    w_up = gaussian(arg_keys[13], (D, FF), D ** -0.5, 0.1875, ((0, 8),))
    w_down = gaussian(arg_keys[14], (FF, D), FF ** -0.5, 0.09375, ((0, 8),))
    return {"media": media, "latents": latents, "counts": counts, "cotangent": cotangent, "gain_media": gain_media, "bias_media": bias_media, "gain_latent": gain_latent, "bias_latent": bias_latent, "gain_ff": gain_ff, "bias_ff": bias_ff, "w_query": w_query, "w_keyval": w_keyval, "w_out": w_out, "w_up": w_up, "w_down": w_down}


@jax.custom_vjp
def low(v):
    return lax.optimization_barrier(v.astype(jnp.bfloat16)).astype(jnp.float32)

@jax.custom_vjp
def low_back(v):
    return v

def low_keep(v):
    return (low(v), None)

def low_pass(kept, grad):
    return (grad,)

def back_keep(v):
    return (v, None)

def back_low(kept, grad):
    return (low(grad),)
low.defvjp(low_keep, low_pass)
low_back.defvjp(back_keep, back_low)
HIGH = lax.Precision.HIGHEST
EPS = 1e-05

def norm_rows(x, gain, bias):
    mean = lax.optimization_barrier(jnp.mean(x, -1, keepdims=True))
    cent = x - mean
    var = lax.optimization_barrier(jnp.mean(cent * cent, -1, keepdims=True))
    return cent * lax.rsqrt(var + EPS) * gain + bias

def matmul(a, b):
    return jnp.einsum('ij,jk->ik', a, b, precision=HIGH)

def forward(params, media, latents, live):
    gain_m, bias_m, gain_l, bias_l, gain_f, bias_f, w_query, w_keyval, w_out, w_up, w_down = params
    med_norm = low(norm_rows(media, gain_m, bias_m))
    lat_norm = low(norm_rows(latents, gain_l, bias_l))
    query = low_back(low(matmul(lat_norm, w_query) * 0.125))
    kv_media = low_back(low(matmul(med_norm, w_keyval)))
    kv_latent = low_back(low(matmul(lat_norm, w_keyval)))
    keyval = jnp.concatenate([kv_media, kv_latent], 0)
    count = keyval.shape[0]
    keys = keyval[:, :INNER].reshape(count, HEADS, HEAD)
    values = keyval[:, INNER:].reshape(count, HEADS, HEAD)
    heads_q = query.reshape(NLAT, HEADS, HEAD)
    score = low_back(jnp.einsum('qhd,khd->hqk', heads_q, keys, precision=HIGH))
    mask = jnp.concatenate([live, jnp.ones((NLAT,), dtype=bool)], 0)
    score = jnp.where(mask[None, None, :], score, -1e+30)
    prob = low(jax.nn.softmax(score, -1))
    attended = low(jnp.einsum('hqk,khd->qhd', prob, values, precision=HIGH).reshape(NLAT, INNER))
    branch = low_back(matmul(attended, w_out))
    hidden = latents + branch
    ff_norm = low(norm_rows(hidden, gain_f, bias_f))
    up = low_back(matmul(ff_norm, w_up))
    act = low(jax.nn.gelu(up, approximate=False))
    result = low_back(matmul(act, w_down))
    return hidden + result

def reference(media, latents, counts, cotangent, gain_media, bias_media, gain_latent, bias_latent, gain_ff, bias_ff, w_query, w_keyval, w_out, w_up, w_down):
    params = tuple((x.astype(jnp.float32) for x in (gain_media, bias_media, gain_latent, bias_latent, gain_ff, bias_ff, w_query, w_keyval, w_out, w_up, w_down)))
    total = MICRO * SAMPLES
    flat_media = media.reshape(total, ROWS, D)
    flat_lat = latents.reshape(total, NLAT, D)
    flat_cot = cotangent.reshape(total, NLAT, D)
    flat_counts = counts.reshape(total).astype(jnp.int32)
    rows = jnp.arange(ROWS, dtype=jnp.int32)

    def step(acc, item):
        med, lat, cnt, cot = item
        live = rows // VIS < cnt

        def run(pars, med_f, lat_f):
            return forward(pars, med_f, lat_f, live)
        out, pull = jax.vjp(run, params, med.astype(jnp.float32), lat.astype(jnp.float32))
        grad_pars, grad_med, grad_lat = pull(cot.astype(jnp.float32))
        acc = jax.tree.map(lambda a, g: a + g, acc, grad_pars)
        return (acc, (out.astype(jnp.bfloat16), grad_med.astype(jnp.bfloat16), grad_lat.astype(jnp.bfloat16)))
    start = tuple((jnp.zeros(p.shape, jnp.float32) for p in params))
    sums, (outs, med_grads, lat_grads) = lax.scan(step, start, (flat_media, flat_lat, flat_counts, flat_cot))
    return (outs.reshape(MICRO, SAMPLES, NLAT, D), med_grads.reshape(MICRO, SAMPLES, ROWS, D), lat_grads.reshape(MICRO, SAMPLES, NLAT, D), sums[0], sums[1], sums[2], sums[3], sums[4], sums[5], sums[6], sums[7], sums[8], sums[9], sums[10])
```

```python
import functools

import jax
import jax.numpy as jnp
from jax import lax
from jax.experimental import pallas as pl
from jax.experimental.pallas import tpu as pltpu
from jax.sharding import PartitionSpec as P

HEADS = 8
HEAD = 64
VIS = 256
EPS = 1e-05
F32 = jnp.float32
B16 = jnp.bfloat16
MESH = pl.DeviceIdType.MESH
DMA = pltpu.SemaphoreType.DMA


def exchange_kernel(axis, n, modes, *refs):
    count = len(modes)
    ins, outs = refs[:count], refs[count : 2 * count]
    send, recv, own = refs[2 * count :]
    me = lax.axis_index(axis)
    barrier = pltpu.get_barrier_semaphore()
    for k in range(1, n):
        pl.semaphore_signal(
            barrier, inc=1, device_id={axis: lax.rem(me + k, n)}, device_id_type=MESH
        )
    pl.semaphore_wait(barrier, n - 1)
    copies = []
    for k in range(1, n):
        peer = lax.rem(me + k, n)
        for i in range(count):
            source = ins[i] if modes[i] == "gather" else ins[i].at[peer]
            copy = pltpu.make_async_remote_copy(
                source,
                outs[i].at[me],
                send.at[i, k],
                recv.at[i, k],
                device_id={axis: peer},
                device_id_type=MESH,
            )
            copy.start()
            copies.append(copy)
    for i in range(count):
        source = ins[i] if modes[i] == "gather" else ins[i].at[me]
        copy = pltpu.make_async_copy(source, outs[i].at[me], own.at[i])
        copy.start()
        copies.append(copy)
    for copy in copies:
        copy.wait()


class Exchanges:
    def __init__(self, sizes):
        self.sizes = sizes
        self.used = 0

    def __call__(self, axis, arrays, modes):
        n = self.sizes[axis]
        count = len(arrays)
        outs = [
            jax.ShapeDtypeStruct(((n,) + a.shape) if m == "gather" else a.shape, a.dtype)
            for a, m in zip(arrays, modes)
        ]
        self.used += 1
        space = pl.BlockSpec(memory_space=pl.ANY)
        return pl.pallas_call(
            functools.partial(exchange_kernel, axis, n, modes),
            out_shape=outs,
            in_specs=[space] * count,
            out_specs=[space] * count,
            scratch_shapes=[DMA((count, n)), DMA((count, n)), DMA((count,))],
            compiler_params=pltpu.CompilerParams(collective_id=self.used, has_side_effects=True),
            name="exchange_%d" % self.used,
        )(*arrays)


def norm_parts(x):
    mean = jnp.mean(x, -1, keepdims=True)
    cent = x - mean
    factor = lax.rsqrt(jnp.mean(cent * cent, -1, keepdims=True) + EPS)
    return cent * factor, factor


def norm_back(grad, unit, factor, gain):
    scaled = grad * gain
    inner = jnp.mean(scaled * unit, -1, keepdims=True)
    d_input = factor * (scaled - jnp.mean(scaled, -1, keepdims=True) - unit * inner)
    return d_input, jnp.sum(grad * unit, 0), jnp.sum(grad, 0)


def mm(a, b):
    return lax.dot_general(a, b, (((1,), (0,)), ((), ())), preferred_element_type=F32)


def mm_nt(a, b):
    return lax.dot_general(a, b, (((1,), (1,)), ((), ())), preferred_element_type=F32)


def mm_tn(a, b):
    return lax.dot_general(a, b, (((0,), (0,)), ((), ())), preferred_element_type=F32)


def shards(n_dp, n_lat, media, latents, counts, cotangent, g_m, b_m, g_l, b_l, g_f, b_f, wq, wkv, wo, wup, wdown):
    ex = Exchanges({"dp": n_dp, "lat": n_lat})
    micro, per, rows, width = media.shape
    nq = latents.shape[2]
    S = micro * per
    inner = wq.shape[1]
    ff = wup.shape[1]
    ff_part = ff // n_dp
    d_part = width // n_dp
    lat_at = lax.axis_index("lat")
    med = media.reshape(S * rows, width)
    lat = latents.reshape(S * nq, width).astype(F32)
    cot = cotangent.reshape(S * nq, width)
    count = counts.reshape(S)

    small = jnp.stack([g_m, b_m, g_l, b_l, g_f, b_f], 0)
    small_all, wq_all, wkv_all, wo_all = ex("dp", [small, wq, wkv, wo], ["gather"] * 4)
    params = jnp.transpose(small_all, (1, 0, 2)).reshape(6, width).astype(F32)
    wq_all = wq_all.reshape(width, inner)
    wkv_all = wkv_all.reshape(width, 2 * inner)
    wo_all = wo_all.reshape(inner, width)
    wup_cols = jnp.transpose(wup.reshape(d_part, n_dp, ff_part), (1, 0, 2))
    cot_all, wup_s = ex("dp", [cot, wup_cols], ["gather", "swap"])
    cot_all = cot_all.reshape(-1, width)
    wup_s = wup_s.reshape(width, ff_part)

    med_unit, med_factor = norm_parts(med.astype(F32))
    med_norm = (med_unit * params[0] + params[1]).astype(B16)
    lat_unit, lat_factor = norm_parts(lat)
    lat_norm = (lat_unit * params[2] + params[3]).astype(B16)
    query = (mm(lat_norm, wq_all) * 0.125).astype(B16)
    (query_all,) = ex("lat", [query], ["gather"])
    kv_med = mm(med_norm, wkv_all).astype(B16)
    kv_lat = mm(lat_norm, wkv_all).astype(B16)
    keyval = jnp.concatenate(
        [kv_med.reshape(S, rows, 2 * inner), kv_lat.reshape(S, nq, 2 * inner)], 1
    )
    kc = rows + nq
    keys = keyval[:, :, :inner].reshape(S, kc, HEADS, HEAD)
    values = keyval[:, :, inner:].reshape(S, kc, HEADS, HEAD)
    heads_q = query_all.reshape(n_lat, S, nq, HEADS, HEAD)
    slot = (lat_at * rows + lax.iota(jnp.int32, rows)) // VIS
    live = jnp.concatenate(
        [slot[None, :] < count[:, None], jnp.ones((S, nq), dtype=bool)], 1
    )
    score = jnp.einsum("zsqhd,skhd->shzqk", heads_q, keys, preferred_element_type=F32)
    score = jnp.where(live[:, None, None, None, :], score, -1e30)
    top = jnp.max(score, -1)
    p = jnp.exp(score - top[..., None])
    total = jnp.sum(p, -1)
    part = jnp.einsum("shzqk,skhd->zsqhd", p.astype(B16), values, preferred_element_type=F32)
    scale = jnp.transpose(1.0 / total, (2, 0, 3, 1))[..., None]
    part = (part * scale).astype(B16).reshape(n_lat, S * nq, inner)
    stats = jnp.stack([top, total], 0).reshape(2 * S * HEADS, n_lat * nq)
    part_all, stats_all = ex("lat", [part, stats], ["swap", "gather"])
    stats_all = stats_all.reshape(n_lat, 2, S, HEADS, n_lat, nq)
    tops, totals = stats_all[:, 0], stats_all[:, 1]
    top_max = jnp.max(tops, 0)
    weight = totals * jnp.exp(tops - top_max)
    whole = jnp.sum(weight, 0)
    lse = top_max + jnp.log(whole)
    weight = lax.dynamic_index_in_dim(weight / whole, lat_at, 3, keepdims=False)
    weight = jnp.transpose(weight, (0, 1, 3, 2)).reshape(n_lat, S * nq, HEADS, 1)
    attended_f = jnp.sum(part_all.reshape(n_lat, S * nq, HEADS, HEAD).astype(F32) * weight, 0)
    attended = attended_f.reshape(S * nq, inner).astype(B16)

    hidden = lat + mm(attended, wo_all)
    ffn_unit, ffn_factor = norm_parts(hidden)
    ff_norm = (ffn_unit * params[4] + params[5]).astype(B16)
    (ffn_all,) = ex("dp", [ff_norm], ["gather"])
    ffn_all = ffn_all.reshape(-1, width)
    up = mm(ffn_all, wup_s)
    act_f, pull = jax.vjp(lambda v: jax.nn.gelu(v, approximate=False), up)
    act = act_f.astype(B16)
    d_act = mm_nt(cot_all, wdown)
    d_up = pull(d_act)[0].astype(B16)
    out_part = mm(act, wdown).astype(B16).reshape(n_dp, S * nq, width)
    d_ffn_part = mm_nt(d_up, wup_s).astype(B16).reshape(n_dp, S * nq, width)
    d_ffn_all, out_all = ex("dp", [d_ffn_part, out_part], ["swap", "swap"])
    latents_out = (hidden + jnp.sum(out_all.astype(F32), 0)).astype(B16)
    d_ffn = jnp.sum(d_ffn_all.astype(F32), 0)
    grad_down = mm_tn(act, cot_all)
    grad_up = mm_tn(ffn_all, d_up)
    d_h, grad_gf, grad_bf = norm_back(d_ffn, ffn_unit, ffn_factor, params[4])
    d_hidden = cot.astype(F32) + d_h
    d_attn = d_hidden.astype(B16)
    grad_out = mm_tn(attended, d_attn)
    d_att = mm_nt(d_attn, wo_all).astype(B16)
    delta = jnp.sum(
        (d_att.astype(F32) * attended_f.reshape(S * nq, inner)).reshape(S * nq, HEADS, HEAD), -1
    )
    d_att_all, delta_all = ex("lat", [d_att, delta.T], ["gather", "gather"])
    d_att_h = d_att_all.reshape(n_lat, S, nq, HEADS, HEAD)
    delta_h = jnp.transpose(delta_all.reshape(n_lat, HEADS, S, nq), (2, 1, 0, 3))[..., None]
    prob = jnp.exp(score - lse[..., None])
    d_prob = jnp.einsum("zsqhd,skhd->shzqk", d_att_h, values, preferred_element_type=F32)
    d_score = (prob * (d_prob - delta_h)).astype(B16)
    dq_part = jnp.einsum("shzqk,skhd->zsqhd", d_score, keys, preferred_element_type=F32)
    (dq_all,) = ex("lat", [dq_part.astype(B16).reshape(n_lat, S * nq, inner)], ["swap"])
    d_keys = jnp.einsum("shzqk,zsqhd->skhd", d_score, heads_q, preferred_element_type=F32)
    d_values = jnp.einsum(
        "shzqk,zsqhd->skhd", prob.astype(B16), d_att_h, preferred_element_type=F32
    )
    d_kv = jnp.concatenate(
        [d_keys.reshape(S, kc, inner), d_values.reshape(S, kc, inner)], -1
    ).astype(B16)
    d_kv_med = d_kv[:, :rows].reshape(S * rows, 2 * inner)
    d_kv_lat = d_kv[:, rows:].reshape(S * nq, 2 * inner)
    grad_kv = mm_tn(med_norm, d_kv_med) + mm_tn(lat_norm, d_kv_lat)
    d_mnorm = mm_nt(d_kv_med, wkv_all)
    d_media, grad_gm, grad_bm = norm_back(d_mnorm, med_unit, med_factor, params[0])
    dq = (jnp.sum(dq_all.astype(F32), 0) * 0.125).astype(B16)
    grad_q = mm_tn(lat_norm, dq)
    d_lnorm = mm_nt(dq, wq_all) + mm_nt(d_kv_lat, wkv_all)
    d_latn, grad_gl, grad_bl = norm_back(d_lnorm, lat_unit, lat_factor, params[2])
    latent_grad = (d_hidden + d_latn).astype(B16)

    smalls = jnp.stack([grad_gm, grad_bm, grad_gl, grad_bl, grad_gf, grad_bf], 0)
    smalls = jnp.transpose(smalls.reshape(6, n_dp, d_part), (1, 0, 2))
    small_s, q_s, kv_s, o_s, up_s = ex(
        "dp",
        [
            smalls,
            grad_q.astype(B16).reshape(n_dp, d_part, inner),
            grad_kv.astype(B16).reshape(n_dp, d_part, 2 * inner),
            grad_out.astype(B16).reshape(n_dp, inner // n_dp, width),
            grad_up.astype(B16).reshape(n_dp, d_part, ff_part),
        ],
        ["swap"] * 5,
    )
    small_s = jnp.sum(small_s, 0)
    q_s = jnp.sum(q_s.astype(F32), 0)
    kv_s = jnp.sum(kv_s.astype(F32), 0)
    o_s = jnp.sum(o_s.astype(F32), 0)
    up_s = jnp.transpose(up_s, (1, 0, 2)).reshape(d_part, ff)
    pieces = [q_s, kv_s, o_s, up_s, grad_down]
    cut = [x.astype(B16).reshape(n_lat, x.shape[0] // n_lat, x.shape[1]) for x in pieces]
    got = ex("lat", cut + [small_s], ["swap"] * 5 + ["gather"])
    small_s = jnp.sum(got[5], 0)
    summed = [jnp.sum(x.astype(F32), 0).astype(B16) for x in got[:5]]
    full = ex("lat", summed, ["gather"] * 5)
    grads = [x.reshape(y.shape).astype(F32) for x, y in zip(full, pieces)]
    return (
        latents_out.reshape(latents.shape),
        d_media.astype(B16).reshape(media.shape),
        latent_grad.reshape(latents.shape),
        *[small_s[i] for i in range(6)],
        *grads,
    )


def solution(mesh):
    rows4 = P(None, "dp", "lat", None)
    vec = P("dp")
    mat = P("dp", None)
    return jax.shard_map(
        functools.partial(shards, mesh.shape["dp"], mesh.shape["lat"]),
        mesh=mesh,
        in_specs=(rows4, rows4, P(None, "dp"), rows4) + (vec,) * 6 + (mat,) * 5,
        out_specs=(rows4,) * 3 + (vec,) * 6 + (mat,) * 5,
        check_vma=False,
    )
```

```python
import functools
import types

import jax
import jax.numpy as jnp
from jax import lax
from jax.experimental import pallas as pl
from jax.experimental.pallas import tpu as pltpu
from jax.sharding import PartitionSpec as P

HEADS = 8
HEAD = 64
VIS = 256
EPS = 1e-05
F32 = jnp.float32
B16 = jnp.bfloat16
MESH = pl.DeviceIdType.MESH
DMA = pltpu.SemaphoreType.DMA
VMEM_BYTES = 62 << 20


def exchange_kernel(axis, n, modes, *refs):
    count = len(modes)
    ins, outs = refs[:count], refs[count : 2 * count]
    send, recv, own = refs[2 * count :]
    me = lax.axis_index(axis)
    barrier = pltpu.get_barrier_semaphore()
    for k in range(1, n):
        pl.semaphore_signal(
            barrier, inc=1, device_id={axis: lax.rem(me + k, n)}, device_id_type=MESH
        )
    pl.semaphore_wait(barrier, n - 1)
    copies = []
    for k in range(1, n):
        peer = lax.rem(me + k, n)
        for i in range(count):
            source = ins[i] if modes[i] == "gather" else ins[i].at[peer]
            copy = pltpu.make_async_remote_copy(
                source,
                outs[i].at[me],
                send.at[i, k],
                recv.at[i, k],
                device_id={axis: peer},
                device_id_type=MESH,
            )
            copy.start()
            copies.append(copy)
    for i in range(count):
        source = ins[i] if modes[i] == "gather" else ins[i].at[me]
        copy = pltpu.make_async_copy(source, outs[i].at[me], own.at[i])
        copy.start()
        copies.append(copy)
    for copy in copies:
        copy.wait()


class Exchanges:
    def __init__(self, sizes):
        self.sizes = sizes
        self.used = 0

    def __call__(self, axis, arrays, modes):
        n = self.sizes[axis]
        count = len(arrays)
        outs = [
            jax.ShapeDtypeStruct(((n,) + a.shape) if m == "gather" else a.shape, a.dtype)
            for a, m in zip(arrays, modes)
        ]
        self.used += 1
        space = pl.BlockSpec(memory_space=pl.ANY)
        return pl.pallas_call(
            functools.partial(exchange_kernel, axis, n, modes),
            out_shape=outs,
            in_specs=[space] * count,
            out_specs=[space] * count,
            scratch_shapes=[DMA((count, n)), DMA((count, n)), DMA((count,))],
            compiler_params=pltpu.CompilerParams(collective_id=self.used, has_side_effects=True),
            name="exchange_%d" % self.used,
        )(*arrays)


def norm_parts(x):
    mean = jnp.mean(x, -1, keepdims=True)
    cent = x - mean
    factor = lax.rsqrt(jnp.mean(cent * cent, -1, keepdims=True) + EPS)
    return cent * factor, factor


def norm_back(grad, unit, factor, gain):
    scaled = grad * gain
    inner = jnp.mean(scaled * unit, -1, keepdims=True)
    d_input = factor * (scaled - jnp.mean(scaled, -1, keepdims=True) - unit * inner)
    return d_input, jnp.sum(grad * unit, 0), jnp.sum(grad, 0)


def mm(a, b):
    return lax.dot_general(a, b, (((1,), (0,)), ((), ())), preferred_element_type=F32)


def mm_nt(a, b):
    return lax.dot_general(a, b, (((1,), (1,)), ((), ())), preferred_element_type=F32)


def mm_tn(a, b):
    return lax.dot_general(a, b, (((0,), (0,)), ((), ())), preferred_element_type=F32)


def shards(n_dp, n_lat, media, latents, counts, cotangent, g_m, b_m, g_l, b_l, g_f, b_f, wq, wkv, wo, wup, wdown):
    ex = Exchanges({"dp": n_dp, "lat": n_lat})
    micro, per, rows, width = media.shape
    nq = latents.shape[2]
    S = micro * per
    inner = wq.shape[1]
    ff = wup.shape[1]
    ff_part = ff // n_dp
    d_part = width // n_dp
    lat_at = lax.axis_index("lat")
    med = media.reshape(S * rows, width)
    lat = latents.reshape(S * nq, width).astype(F32)
    cot = cotangent.reshape(S * nq, width)
    count = counts.reshape(S)

    small = jnp.stack([g_m, b_m, g_l, b_l, g_f, b_f], 0)
    small_all, wq_all, wkv_all, wo_all = ex("dp", [small, wq, wkv, wo], ["gather"] * 4)
    params = jnp.transpose(small_all, (1, 0, 2)).reshape(6, width).astype(F32)
    wq_all = wq_all.reshape(width, inner)
    wkv_all = wkv_all.reshape(width, 2 * inner)
    wo_all = wo_all.reshape(inner, width)
    wup_cols = jnp.transpose(wup.reshape(d_part, n_dp, ff_part), (1, 0, 2))
    cot_all, wup_s = ex("dp", [cot, wup_cols], ["gather", "swap"])
    cot_all = cot_all.reshape(-1, width)
    wup_s = wup_s.reshape(width, ff_part)

    med_unit, med_factor = norm_parts(med.astype(F32))
    med_norm = (med_unit * params[0] + params[1]).astype(B16)
    lat_unit, lat_factor = norm_parts(lat)
    lat_norm = (lat_unit * params[2] + params[3]).astype(B16)
    query = (mm(lat_norm, wq_all) * 0.125).astype(B16)
    (query_all,) = ex("lat", [query], ["gather"])
    kv_med = mm(med_norm, wkv_all).astype(B16)
    kv_lat = mm(lat_norm, wkv_all).astype(B16)
    keyval = jnp.concatenate(
        [kv_med.reshape(S, rows, 2 * inner), kv_lat.reshape(S, nq, 2 * inner)], 1
    )
    kc = rows + nq
    keys = keyval[:, :, :inner].reshape(S, kc, HEADS, HEAD)
    values = keyval[:, :, inner:].reshape(S, kc, HEADS, HEAD)
    heads_q = query_all.reshape(n_lat, S, nq, HEADS, HEAD)
    slot = (lat_at * rows + lax.iota(jnp.int32, rows)) // VIS
    live = jnp.concatenate(
        [slot[None, :] < count[:, None], jnp.ones((S, nq), dtype=bool)], 1
    )
    score = jnp.einsum("zsqhd,skhd->shzqk", heads_q, keys, preferred_element_type=F32)
    score = jnp.where(live[:, None, None, None, :], score, -1e30)
    top = jnp.max(score, -1)
    p = jnp.exp(score - top[..., None])
    total = jnp.sum(p, -1)
    part = jnp.einsum("shzqk,skhd->zsqhd", p.astype(B16), values, preferred_element_type=F32)
    scale = jnp.transpose(1.0 / total, (2, 0, 3, 1))[..., None]
    part = (part * scale).astype(B16).reshape(n_lat, S * nq, inner)
    stats = jnp.stack([top, total], 0).reshape(2 * S * HEADS, n_lat * nq)
    part_all, stats_all = ex("lat", [part, stats], ["swap", "gather"])
    stats_all = stats_all.reshape(n_lat, 2, S, HEADS, n_lat, nq)
    tops, totals = stats_all[:, 0], stats_all[:, 1]
    top_max = jnp.max(tops, 0)
    weight = totals * jnp.exp(tops - top_max)
    whole = jnp.sum(weight, 0)
    lse = top_max + jnp.log(whole)
    weight = lax.dynamic_index_in_dim(weight / whole, lat_at, 3, keepdims=False)
    weight = jnp.transpose(weight, (0, 1, 3, 2)).reshape(n_lat, S * nq, HEADS, 1)
    attended_f = jnp.sum(part_all.reshape(n_lat, S * nq, HEADS, HEAD).astype(F32) * weight, 0)
    attended = attended_f.reshape(S * nq, inner).astype(B16)

    hidden = lat + mm(attended, wo_all)
    ffn_unit, ffn_factor = norm_parts(hidden)
    ff_norm = (ffn_unit * params[4] + params[5]).astype(B16)
    (ffn_all,) = ex("dp", [ff_norm], ["gather"])
    ffn_all = ffn_all.reshape(-1, width)
    up = mm(ffn_all, wup_s)
    act_f, pull = jax.vjp(lambda v: jax.nn.gelu(v, approximate=False), up)
    act = act_f.astype(B16)
    d_act = mm_nt(cot_all, wdown)
    d_up = pull(d_act)[0].astype(B16)
    out_part = mm(act, wdown).astype(B16).reshape(n_dp, S * nq, width)
    d_ffn_part = mm_nt(d_up, wup_s).astype(B16).reshape(n_dp, S * nq, width)
    d_ffn_all, out_all = ex("dp", [d_ffn_part, out_part], ["swap", "swap"])
    latents_out = (hidden + jnp.sum(out_all.astype(F32), 0)).astype(B16)
    d_ffn = jnp.sum(d_ffn_all.astype(F32), 0)
    grad_down = mm_tn(act, cot_all)
    grad_up = mm_tn(ffn_all, d_up)
    d_h, grad_gf, grad_bf = norm_back(d_ffn, ffn_unit, ffn_factor, params[4])
    d_hidden = cot.astype(F32) + d_h
    d_attn = d_hidden.astype(B16)
    grad_out = mm_tn(attended, d_attn)
    d_att = mm_nt(d_attn, wo_all).astype(B16)
    delta = jnp.sum(
        (d_att.astype(F32) * attended_f.reshape(S * nq, inner)).reshape(S * nq, HEADS, HEAD), -1
    )
    d_att_all, delta_all = ex("lat", [d_att, delta.T], ["gather", "gather"])
    d_att_h = d_att_all.reshape(n_lat, S, nq, HEADS, HEAD)
    delta_h = jnp.transpose(delta_all.reshape(n_lat, HEADS, S, nq), (2, 1, 0, 3))[..., None]
    prob = jnp.exp(score - lse[..., None])
    d_prob = jnp.einsum("zsqhd,skhd->shzqk", d_att_h, values, preferred_element_type=F32)
    d_score = (prob * (d_prob - delta_h)).astype(B16)
    dq_part = jnp.einsum("shzqk,skhd->zsqhd", d_score, keys, preferred_element_type=F32)
    (dq_all,) = ex("lat", [dq_part.astype(B16).reshape(n_lat, S * nq, inner)], ["swap"])
    d_keys = jnp.einsum("shzqk,zsqhd->skhd", d_score, heads_q, preferred_element_type=F32)
    d_values = jnp.einsum(
        "shzqk,zsqhd->skhd", prob.astype(B16), d_att_h, preferred_element_type=F32
    )
    d_kv = jnp.concatenate(
        [d_keys.reshape(S, kc, inner), d_values.reshape(S, kc, inner)], -1
    ).astype(B16)
    d_kv_med = d_kv[:, :rows].reshape(S * rows, 2 * inner)
    d_kv_lat = d_kv[:, rows:].reshape(S * nq, 2 * inner)
    grad_kv = mm_tn(med_norm, d_kv_med) + mm_tn(lat_norm, d_kv_lat)
    d_mnorm = mm_nt(d_kv_med, wkv_all)
    d_media, grad_gm, grad_bm = norm_back(d_mnorm, med_unit, med_factor, params[0])
    dq = (jnp.sum(dq_all.astype(F32), 0) * 0.125).astype(B16)
    grad_q = mm_tn(lat_norm, dq)
    d_lnorm = mm_nt(dq, wq_all) + mm_nt(d_kv_lat, wkv_all)
    d_latn, grad_gl, grad_bl = norm_back(d_lnorm, lat_unit, lat_factor, params[2])
    latent_grad = (d_hidden + d_latn).astype(B16)

    smalls = jnp.stack([grad_gm, grad_bm, grad_gl, grad_bl, grad_gf, grad_bf], 0)
    smalls = jnp.transpose(smalls.reshape(6, n_dp, d_part), (1, 0, 2))
    small_s, q_s, kv_s, o_s, up_s = ex(
        "dp",
        [
            smalls,
            grad_q.astype(B16).reshape(n_dp, d_part, inner),
            grad_kv.astype(B16).reshape(n_dp, d_part, 2 * inner),
            grad_out.astype(B16).reshape(n_dp, inner // n_dp, width),
            grad_up.astype(B16).reshape(n_dp, d_part, ff_part),
        ],
        ["swap"] * 5,
    )
    small_s = jnp.sum(small_s, 0)
    q_s = jnp.sum(q_s.astype(F32), 0)
    kv_s = jnp.sum(kv_s.astype(F32), 0)
    o_s = jnp.sum(o_s.astype(F32), 0)
    up_s = jnp.transpose(up_s, (1, 0, 2)).reshape(d_part, ff)
    pieces = [q_s, kv_s, o_s, up_s, grad_down]
    cut = [x.astype(B16).reshape(n_lat, x.shape[0] // n_lat, x.shape[1]) for x in pieces]
    got = ex("lat", cut + [small_s], ["swap"] * 5 + ["gather"])
    small_s = jnp.sum(got[5], 0)
    summed = [jnp.sum(x.astype(F32), 0).astype(B16) for x in got[:5]]
    full = ex("lat", summed, ["gather"] * 5)
    grads = [x.reshape(y.shape).astype(F32) for x, y in zip(full, pieces)]
    return (
        latents_out.reshape(latents.shape),
        d_media.astype(B16).reshape(media.shape),
        latent_grad.reshape(latents.shape),
        *[small_s[i] for i in range(6)],
        *grads,
    )


NT, NN, TN = (((1,), (1,)), ((), ())), (((1,), (0,)), ((), ())), (((0,), (0,)), ((), ()))


def dot(a, b, form):
    return lax.dot_general(a, b, form, preferred_element_type=F32)


def centred(x):
    mean = jnp.mean(x, -1, keepdims=True)
    cent = x - mean
    factor = lax.rsqrt(jnp.mean(cent * cent, -1, keepdims=True) + EPS)
    return cent * factor, factor


def back(grad, unit, factor, gain):
    scaled = grad * gain
    inner = jnp.mean(scaled * unit, -1, keepdims=True)
    return factor * (scaled - jnp.mean(scaled, -1, keepdims=True) - unit * inner)


def fused_kernel(geo, refs):
    S, R, Q, D, I, NC, NZ = geo
    KR = R + Q
    B = S * Q
    G = 2
    W = I // G
    HG = HEADS // G
    r = refs
    me = lax.axis_index("dp")
    z = lax.axis_index("lat")
    chip = me // 2
    core = lax.rem(me, 2)
    sib = me + 1 - 2 * core
    other = 1 - core

    def chip_to(k):
        return lax.rem(chip + k, NC)

    def chip_from(k):
        return lax.rem(chip + NC - k, NC)

    def z_to(k):
        return lax.rem(z + k, NZ)

    def z_from(k):
        return lax.rem(z + NZ - k, NZ)

    quads = range(1, NC)
    planes = range(1, NZ)
    used = [0, 0]

    def local(src, dst):
        sem = r.lsem.at[used[0]]
        used[0] += 1
        copy = pltpu.make_async_copy(src, dst, sem)
        copy.start()
        return copy

    def remote(src, dst, **where):
        at = used[1]
        used[1] += 1
        copy = pltpu.make_async_remote_copy(
            src, dst, r.ssem.at[at], r.rsem.at[at], device_id=where, device_id_type=MESH
        )
        copy.start()
        return copy

    class Spread:
        def __init__(self, src_for, dst):
            self.dst = dst
            self.far = [remote(src_for(chip_to(k)), dst.at[me], dp=2 * chip_to(k) + core) for k in quads]
            self.near = remote(src_for(chip), dst.at[me], dp=sib)
            self.own = local(src_for(chip), dst.at[me])

        def forward(self):
            self.passed = []
            for k in quads:
                self.far[k - 1].wait_recv()
                slot = self.dst.at[2 * chip_from(k) + core]
                self.passed.append(remote(slot, slot, dp=sib))

        def finish(self):
            self.own.wait()
            self.near.wait()
            for copy in self.far:
                copy.wait_send()
            for copy in self.passed:
                copy.wait()

    def to_quad(src_for, dst):
        return [remote(src_for(chip_to(k)), dst, dp=2 * chip_to(k) + core) for k in quads]

    def to_planes(src_for, dst):
        return [remote(src_for(z_to(k)), dst, lat=z_to(k)) for k in planes]

    def wait_all(copies):
        for copy in copies:
            copy.wait()

    barrier = pltpu.get_barrier_semaphore()
    for k in quads:
        pl.semaphore_signal(barrier, inc=1, device_id={"dp": 2 * chip_to(k) + core}, device_id_type=MESH)
    pl.semaphore_signal(barrier, inc=1, device_id={"dp": sib}, device_id_type=MESH)
    for k in planes:
        pl.semaphore_signal(barrier, inc=1, device_id={"lat": z_to(k)}, device_id_type=MESH)
    pl.semaphore_wait(barrier, NC - 1 + 1 + NZ - 1)

    g_small = Spread(lambda _: r.small, r.small_all)
    g_wq = Spread(lambda _: r.wq, r.wq_all)
    lat_in = local(r.lat, r.lat_v)
    cot_in = local(r.cot, r.cot4.at[chip])
    slots = r.med.shape[0]

    def med_copy(s):
        slot = lax.rem(s, slots)
        return pltpu.make_async_copy(r.media.at[s], r.med.at[slot], r.dsem.at[slot])

    def med_first():
        for s in range(slots):
            med_copy(jnp.int32(s)).start()

    def med_next(s):
        @pl.when(s + slots < S)
        def _():
            med_copy(s + slots).start()

    med_first()
    g_wkv = Spread(lambda _: r.wkv, r.wkv_all)
    g_wo = Spread(lambda _: r.wo, r.wo_all)
    g_small.forward()
    g_small.finish()
    params = r.params
    for d in range(2 * NC):
        span = D // (2 * NC)
        params[:, d * span : (d + 1) * span] = r.small_all[d]

    def param(i):
        return params[i : i + 1, :]

    lat_in.wait()
    unit, _ = centred(r.lat_v[...].astype(F32))
    r.latn[...] = (unit * param(2) + param(3)).astype(B16)
    g_wq.forward()

    rb = 64

    def norm_sample(s, carry):
        slot = lax.rem(s, slots)
        med_copy(s).wait()

        def part(i, inner):
            x = r.med[slot, pl.ds(pl.multiple_of(i * rb, rb), rb), :].astype(F32)
            u, _ = centred(x)
            row = pl.multiple_of(s * KR + i * rb, 16)
            r.X[pl.ds(row, rb), :] = (u * param(0) + param(1)).astype(B16)
            return inner

        lax.fori_loop(0, R // rb, part, 0)
        row = pl.multiple_of(s * KR + R, 16)
        at = pl.multiple_of(s * Q, 16)
        r.X[pl.ds(row, Q), :] = r.latn[pl.ds(at, Q), :]
        med_next(s)
        return carry

    g_wq.finish()
    query = dot(r.latn[...], r.wq_all[...].reshape(D, I), NN) * 0.125
    r.q_all[z] = query.astype(B16).reshape(S, Q, I)
    q_out = to_planes(lambda _: r.q_all.at[z], r.q_all.at[z])
    lax.fori_loop(0, S, norm_sample, 0)
    med_first()
    g_wkv.forward()
    g_wo.forward()
    g_wkv.finish()
    span = r.wup_all.shape[2]

    def up_slice(k):
        return r.wup.at[:, pl.ds(pl.multiple_of(k * span, 128), span)]

    cot_in.wait()
    g_cot = to_quad(lambda _: r.cot, r.cot4.at[chip])
    g_down = remote(r.wdown, r.wdown2.at[core], dp=sib)
    g_down_own = local(r.wdown, r.wdown2.at[core])
    g_up = Spread(up_slice, r.wup_all)

    def keyval(s, carry):
        rows = pl.ds(pl.multiple_of(s * KR, 16), KR)
        r.KV[rows, :] = dot(r.X[rows, :], r.wkv_all[...].reshape(D, 2 * I), NN).astype(B16)
        return carry

    lax.fori_loop(0, S, keyval, 0)
    g_wo.finish()
    wait_all(q_out)

    own_head = (
        lax.broadcasted_iota(jnp.int32, (HG * NZ * Q, W), 0) // (NZ * Q)
        == lax.broadcasted_iota(jnp.int32, (HG * NZ * Q, W), 1) // HEAD
    )
    r.mask[...] = own_head.astype(F32).astype(B16)

    def spread_heads(x):
        return jnp.concatenate([x] * HG, 0) * r.mask[...]

    def take_heads(x):
        low = lax.broadcasted_iota(jnp.int32, (NZ * Q, 2 * HEAD), 1) < HEAD
        cols = []
        for pair in range(HG // 2):
            block = x[:, pair * 2 * HEAD : (pair + 1) * 2 * HEAD]
            n = NZ * Q
            cols.append(
                jnp.where(low, block[2 * pair * n : (2 * pair + 1) * n], block[(2 * pair + 1) * n : (2 * pair + 2) * n])
            )
        return jnp.concatenate(cols, 1)

    def scores(s, g, qbig):
        rows = pl.ds(pl.multiple_of(s * KR, 16), KR)
        raw = dot(r.KV[rows, g * W : (g + 1) * W], qbig, NT)
        row = lax.broadcasted_iota(jnp.int32, raw.shape, 0)
        live = jnp.logical_or(row >= R, row + z * R < r.counts[s] * VIS)
        return jnp.where(live, raw, -1e30)

    def queries(s, g):
        return spread_heads(r.q_all[:, s, :, g * W : (g + 1) * W].reshape(NZ * Q, W))

    def stats(s, carry):
        for g in range(G):
            score = scores(s, g, queries(s, g))
            top = jnp.max(score, 0, keepdims=True)
            total = jnp.sum(jnp.exp(score - top), 0, keepdims=True)
            r.lse[z, pl.ds(s * G + g, 1), :] = top + jnp.log(total)
        return carry

    lax.fori_loop(0, S, stats, 0)
    wait_all(to_planes(lambda _: r.lse.at[z], r.lse.at[z]))
    every = r.lse[...]
    top = jnp.max(every, 0)
    r.lse_all[...] = top + jnp.log(jnp.sum(jnp.exp(every - top[None]), 0))

    def attend(s, carry):
        rows = pl.ds(pl.multiple_of(s * KR, 16), KR)
        for g in range(G):
            score = scores(s, g, queries(s, g))
            prob = jnp.exp(score - r.lse_all[pl.ds(s * G + g, 1), :])
            part = dot(prob.astype(B16), r.KV[rows, I + g * W : I + (g + 1) * W], TN)
            r.o_send[:, s, :, g * W : (g + 1) * W] = take_heads(part).astype(B16).reshape(NZ, Q, W)
        return carry

    lax.fori_loop(0, S, attend, 0)
    o_out = to_planes(lambda k: r.o_send.at[k], r.o_recv.at[z])
    g_up.forward()
    wait_all(g_cot)
    g_down.wait()
    g_down_own.wait()

    def act_grad(b, carry):
        r.d_act[b] = dot(r.cot4[b], r.wdown2[...].reshape(span, D), NT)
        return carry

    lax.fori_loop(0, NC, act_grad, 0)
    g_up.finish()
    wait_all(o_out)
    att = r.o_send[z].astype(F32)
    for k in planes:
        att = att + r.o_recv[z_from(k)].astype(F32)
    att = att.reshape(B, I)
    r.att_f[...] = att
    r.att[...] = att.astype(B16)
    hidden = r.lat_v[...].astype(F32) + dot(r.att[...], r.wo_all[...].reshape(I, D), NN)
    r.hidden[...] = hidden
    unit, _ = centred(hidden)
    r.ffn4[chip] = (unit * param(4) + param(5)).astype(B16)
    f_out = to_quad(lambda _: r.ffn4.at[chip], r.ffn4.at[chip])

    def feed(b):
        r.up[...] = dot(r.ffn4[b], r.wup_all[...].reshape(D, span), NN)

        def gelu_part(i, carry):
            rows = pl.ds(pl.multiple_of(i * 32, 32), 32)
            x = r.up[rows, :]
            cdf = 0.5 * (1.0 + lax.erf(x * 0.7071067811865476))
            pdf = jnp.exp(-0.5 * x * x) * 0.3989422804014327
            r.act[b, rows, :] = (x * cdf).astype(B16)
            r.d_up[b, rows, :] = (r.d_act[b, rows, :] * (cdf + x * pdf)).astype(B16)
            return carry

        lax.fori_loop(0, B // 32, gelu_part, 0)
        r.df_send[b] = dot(r.d_up[b], r.wup_all[...].reshape(D, span), NT).astype(B16)

    feed(chip)
    df_out = []
    for k in quads:
        f_out[k - 1].wait_recv()
        b = chip_from(k)
        feed(b)
        df_out.append(remote(r.df_send.at[b], r.df_recv.at[chip], dp=2 * b + core))

    def down(i, carry):
        r.out_send[i] = dot(r.act[i], r.wdown2[...].reshape(span, D), NN).astype(B16)
        return carry

    lax.fori_loop(0, NC, down, 0)
    out_out = to_quad(lambda k: r.out_send.at[k], r.out_recv.at[chip])

    half = span // 2
    act2 = r.act

    def grad_down(i, carry):
        at = pl.multiple_of(i * 256, 256)
        value = dot(
            act2[:, :, pl.ds(at, 256)].reshape(NC * B, 256), r.cot4[...].reshape(NC * B, D), TN
        )
        r.gd[i // (half // 256), pl.ds(pl.multiple_of(lax.rem(i * 256, half), 256), 256), :] = value.astype(B16)
        return carry

    lax.fori_loop(0, span // 256, grad_down, 0)
    gd_out = remote(r.gd.at[other], r.gd_recv, dp=sib)
    dw = D // NC
    hw = dw // 2

    def grad_up(i, carry):
        at = pl.multiple_of(i * dw, dw)
        value = dot(
            r.ffn4[:, :, pl.ds(at, dw)].reshape(NC * B, dw), r.d_up[...].reshape(NC * B, span), TN
        ).astype(B16)
        r.gu[0, i] = value[:hw]
        r.gu[1, i] = value[hw:]
        return carry

    lax.fori_loop(0, NC, grad_up, 0)
    gu_out = remote(r.gu.at[other], r.gu_recv, dp=sib)

    for copy in f_out:
        copy.wait_send()
    wait_all(df_out)
    d_ffn = r.df_send[chip].astype(F32)
    for k in quads:
        d_ffn = d_ffn + r.df_recv[chip_to(k)].astype(F32)
    unit, factor = centred(r.hidden[...])
    sums = r.sums
    sums[4:5, :] = jnp.sum(d_ffn * unit, 0, keepdims=True)
    sums[5:6, :] = jnp.sum(d_ffn, 0, keepdims=True)
    d_hidden = r.cot4[chip].astype(F32) + back(d_ffn, unit, factor, param(4))
    r.d_hidden[...] = d_hidden
    r.d_attn[...] = d_hidden.astype(B16)
    d_att = dot(r.d_attn[...], r.wo_all[...].reshape(I, D), NT).astype(B16)
    weighed = d_att.astype(F32) * r.att_f[...]
    lane = lax.broadcasted_iota(jnp.int32, (B, 128), 1)
    delta = jnp.zeros((B, 128), F32)
    low_lane = lax.broadcasted_iota(jnp.int32, (B, 128), 1) < HEAD
    for h in range(HEADS):
        block = weighed[:, (h // 2) * 128 : (h // 2) * 128 + 128]
        keep = low_lane if h % 2 == 0 else jnp.logical_not(low_lane)
        one = jnp.sum(jnp.where(keep, block, 0.0), -1, keepdims=True)
        delta = jnp.where(jnp.logical_or(lane == h, lane == HEADS + h), -one, delta)
    coarse = delta.astype(B16).astype(F32)
    ext = jnp.where(lane < HEADS, coarse, delta - coarse).astype(B16)
    r.d_ext[z, :, :, 0:I] = d_att.reshape(S, Q, I)
    r.d_ext[z, :, :, I : I + 128] = ext.reshape(S, Q, 128)
    d_out = to_planes(lambda _: r.d_ext.at[z], r.d_ext.at[z])

    ow = I // NC
    oh = ow // 2
    for i in range(NC):
        value = dot(r.att[:, i * ow : (i + 1) * ow], r.d_attn[...], TN).astype(B16)
        r.go[0, i] = value[:oh]
        r.go[1, i] = value[oh:]
    go_out = remote(r.go.at[other], r.go_recv, dp=sib)

    wait_all(out_out)
    out = r.hidden[...] + r.out_send[chip].astype(F32)
    for k in quads:
        out = out + r.out_recv[chip_to(k)].astype(F32)
    r.stage[0] = out.astype(B16)
    put_out = local(r.stage.at[0], r.latents_out)

    def add_pair(dst, a, b, n):
        def body(i, carry):
            dst[i] = (a[i].astype(F32) + b[i].astype(F32)).astype(B16)
            return carry

        lax.fori_loop(0, n, body, 0)

    gd_out.wait()
    piece = half // NZ
    for j in range(NZ):
        rows = slice(j * piece, (j + 1) * piece)
        r.gd_sum[j] = (r.gd[core, rows, :].astype(F32) + r.gd_recv[rows, :].astype(F32)).astype(B16)
    gz_out = to_planes(lambda k: r.gd_sum.at[k], r.gz_recv.at[0, z])
    gu_out.wait()
    add_pair(r.gu_sum, r.gu.at[core], r.gu_recv, NC)
    gq_out = to_quad(lambda k: r.gu_sum.at[k], r.gu_quad.at[chip])
    wait_all(d_out)

    ones = jnp.ones((KR, 128), B16)
    lane_e = lax.broadcasted_iota(jnp.int32, (HG * NZ * Q, 128), 1)
    head_e = lax.broadcasted_iota(jnp.int32, (HG * NZ * Q, 128), 0) // (NZ * Q)
    for g in range(G):
        r.mask_e[g] = (
            jnp.logical_or(lane_e == head_e + g * HG, lane_e == head_e + g * HG + HEADS).astype(F32).astype(B16)
        )

    def attend_back(s, carry):
        rows = pl.ds(pl.multiple_of(s * KR, 16), KR)
        for g in range(G):
            qbig = queries(s, g)
            score = scores(s, g, qbig)
            prob = jnp.exp(score - r.lse_all[pl.ds(s * G + g, 1), :])
            dbig = spread_heads(r.d_ext[:, s, :, g * W : (g + 1) * W].reshape(NZ * Q, W))
            minus = r.d_ext[:, s, :, I : I + 128].reshape(NZ * Q, 128)
            minus = jnp.concatenate([minus] * HG, 0) * r.mask_e[g]
            d_prob = dot(r.KV[rows, I + g * W : I + (g + 1) * W], dbig, NT) + dot(ones, minus, NT)
            d_score = (prob * d_prob).astype(B16)
            dq = dot(d_score, r.KV[rows, g * W : (g + 1) * W], TN)
            r.dq_send[:, s, :, g * W : (g + 1) * W] = take_heads(dq).astype(B16).reshape(NZ, Q, W)
            r.KV[rows, g * W : (g + 1) * W] = dot(d_score, qbig, NN).astype(B16)
            r.KV[rows, I + g * W : I + (g + 1) * W] = dot(prob.astype(B16), dbig, NN).astype(B16)
        return carry

    lax.fori_loop(0, S, attend_back, 0)
    dq_out = to_planes(lambda k: r.dq_send.at[k], r.dq_recv.at[z])

    wait_all(gq_out)
    r.gu_quad[chip] = r.gu_sum[chip]
    gz_out += to_planes(lambda k: r.gu_quad.at[k], r.gz_recv.at[1, z])

    def grad_kv(i, carry):
        at = pl.multiple_of(i * dw, dw)
        value = dot(r.X[:, pl.ds(at, dw)], r.KV[...], TN).astype(B16)
        r.gk[0, i] = value[:hw]
        r.gk[1, i] = value[hw:]
        return carry

    lax.fori_loop(0, NC, grad_kv, 0)
    gk_out = remote(r.gk.at[other], r.gk_recv, dp=sib)

    wait_all(dq_out)
    dq = r.dq_send[z].astype(F32)
    for k in planes:
        dq = dq + r.dq_recv[z_from(k)].astype(F32)
    r.dq[...] = (dq.reshape(B, I) * 0.125).astype(B16)
    for i in range(NC):
        value = dot(r.latn[:, i * dw : (i + 1) * dw], r.dq[...], TN).astype(B16)
        r.gq[0, i] = value[:hw]
        r.gq[1, i] = value[hw:]
    gqs_out = remote(r.gq.at[other], r.gq_recv, dp=sib)
    gk_out.wait()
    go_out.wait()
    add_pair(r.gk_sum, r.gk.at[core], r.gk_recv, NC)
    add_pair(r.go_sum, r.go.at[core], r.go_recv, NC)
    quad_out = to_quad(lambda k: r.gk_sum.at[k], r.gk_quad.at[chip])
    quad_out += to_quad(lambda k: r.go_sum.at[k], r.go_quad.at[chip])
    gqs_out.wait()
    add_pair(r.gq_sum, r.gq.at[core], r.gq_recv, NC)
    quad_out += to_quad(lambda k: r.gq_sum.at[k], r.gq_quad.at[chip])

    wait_all(gz_out)
    for a, own in enumerate([r.gd_sum, r.gu_quad]):
        total = own[z].astype(F32)
        for k in planes:
            total = total + r.gz_recv[a, z_from(k)].astype(F32)
        r.gz_sum[a] = total.astype(B16)
    last = []
    for a, out in enumerate([r.gdown, r.gup]):
        last.append(local(r.gz_sum.at[a], out.at[z]))
        last += to_planes(lambda _: r.gz_sum.at[a], out.at[z])

    sums[0:1, :] = jnp.zeros((1, D), F32)
    sums[1:2, :] = jnp.zeros((1, D), F32)
    sums[6:8, :] = jnp.zeros((2, D), F32)

    def media_back(s, carry):
        slot = lax.rem(s, 2)
        held = lax.rem(s, slots)
        rows = pl.ds(pl.multiple_of(s * KR, 16), KR)
        med_copy(s).wait()
        r.dn[...] = dot(r.KV[rows, :], r.wkv_all[...].reshape(D, 2 * I), NT)
        r.d_lat[pl.ds(pl.multiple_of(s * Q, 8), Q), :] = r.dn[R:, :]

        @pl.when(s >= 2)
        def _():
            pltpu.make_async_copy(r.mg.at[slot], r.media_grad.at[s - 2], r.msem.at[slot]).wait()

        def part(i, inner):
            block = pl.ds(pl.multiple_of(i * rb, rb), rb)
            unit, factor = centred(r.med[held, block, :].astype(F32))
            grad = r.dn[block, :]
            sums[0:1, :] += jnp.sum(grad * unit, 0, keepdims=True)
            sums[1:2, :] += jnp.sum(grad, 0, keepdims=True)
            r.mg[slot, block, :] = back(grad, unit, factor, param(0)).astype(B16)
            return inner

        lax.fori_loop(0, R // rb, part, 0)
        pltpu.make_async_copy(r.mg.at[slot], r.media_grad.at[s], r.msem.at[slot]).start()
        med_next(s)
        return carry

    lax.fori_loop(0, S, media_back, 0)

    d_latn = r.d_lat[...] + dot(r.dq[...], r.wq_all[...].reshape(D, I), NT)
    unit, factor = centred(r.lat_v[...].astype(F32))
    sums[2:3, :] = jnp.sum(d_latn * unit, 0, keepdims=True)
    sums[3:4, :] = jnp.sum(d_latn, 0, keepdims=True)
    r.stage[1] = (r.d_hidden[...] + back(d_latn, unit, factor, param(2))).astype(B16)
    put_lat = local(r.stage.at[1], r.latent_grad)

    sp = D // (2 * NC)
    for t in range(NC):
        for cc in range(2):
            d = 2 * t + cc
            r.sm[cc, t] = sums[:, d * sp : (d + 1) * sp]
    sm_out = remote(r.sm.at[other], r.sm_recv, dp=sib)
    sm_out.wait()
    r.sm_sum[...] = r.sm[core] + r.sm_recv[...]
    quad_out += to_quad(lambda k: r.sm_sum.at[k], r.sm_quad.at[chip])
    wait_all(quad_out)

    def quad_total(own, got):
        total = own[chip].astype(F32)
        for k in quads:
            total = total + got[chip_to(k)].astype(F32)
        return total

    r.sm_z[z] = quad_total(r.sm_sum, r.sm_quad)
    zs_out = to_planes(lambda _: r.sm_z.at[z], r.sm_z.at[z])
    thirds = [
        (r.gk_sum, r.gk_quad, r.gk_z, r.gk_zr, r.gk_f, r.gkv),
        (r.gq_sum, r.gq_quad, r.gq_z, r.gq_zr, r.gq_f, r.gquery),
        (r.go_sum, r.go_quad, r.go_z, r.go_zr, r.go_f, r.gout),
    ]
    for own, got, split, far, _, _ in thirds:
        total = quad_total(own, got).astype(B16)
        rows = total.shape[0] // NZ
        for j in range(NZ):
            split[j] = total[j * rows : (j + 1) * rows]
        zs_out += to_planes(lambda k: split.at[k], far.at[z])
    wait_all(zs_out)
    r.sm_all[...] = jnp.sum(r.sm_z[...], 0)
    last.append(local(r.sm_all, r.gsmall))
    for _, _, split, far, whole, out in thirds:
        total = split[z].astype(F32)
        for k in planes:
            total = total + far[z_from(k)].astype(F32)
        whole[...] = total.astype(B16)
        last.append(local(whole, out.at[z]))
        last += to_planes(lambda _: whole, out.at[z])
    for slot in range(2):
        pltpu.make_async_copy(
            r.mg.at[slot], r.media_grad.at[S - 2 + slot], r.msem.at[slot]
        ).wait()
    put_out.wait()
    put_lat.wait()
    wait_all(last)
    assert used[1] <= r.rsem.shape[0] and used[0] <= r.lsem.shape[0]


def fused(n_dp, n_lat, media, latents, counts, cotangent, g_m, b_m, g_l, b_l, g_f, b_f, wq, wkv, wo, wup, wdown):
    micro, per, R, D = media.shape
    Q = latents.shape[2]
    S = micro * per
    B = S * Q
    I = wq.shape[1]
    NC = n_dp // 2
    NZ = n_lat
    KR = R + Q
    span = wup.shape[1] // NC
    dp_rows = D // n_dp
    small = jnp.stack([g_m, b_m, g_l, b_l, g_f, b_f], 0).astype(F32)
    small = jnp.pad(small, ((0, 2), (0, 0)))
    hbm = pl.BlockSpec(memory_space=pl.ANY)
    ins = dict(
        media=media.reshape(S, R, D),
        lat=latents.reshape(B, D),
        cot=cotangent.reshape(B, D),
        small=small,
        wq=wq,
        wkv=wkv,
        wo=wo,
        wup=wup,
        wdown=wdown,
        counts=counts.reshape(S),
    )
    in_specs = [hbm] * 9 + [pl.BlockSpec(memory_space=pltpu.SMEM)]
    outs = dict(
        latents_out=((B, D), B16),
        media_grad=((S, R, D), B16),
        latent_grad=((B, D), B16),
        gsmall=((8, dp_rows), F32),
        gquery=((NZ, dp_rows // NZ, I), B16),
        gkv=((NZ, dp_rows // NZ, 2 * I), B16),
        gout=((NZ, I // n_dp // NZ, D), B16),
        gup=((NC, dp_rows, span), B16),
        gdown=((NZ, span // 2 // NZ, D), B16),
    )
    kv_rows = S * KR
    o_rows = I // n_dp
    buffers = dict(
        med=((4, R, D), B16),
        X=((kv_rows, D), B16),
        KV=((kv_rows, 2 * I), B16),
        small_all=((n_dp, 8, dp_rows), F32),
        params=((8, D), F32),
        wq_all=((n_dp, dp_rows, I), B16),
        wkv_all=((n_dp, dp_rows, 2 * I), B16),
        wo_all=((n_dp, o_rows, D), B16),
        wup_all=((n_dp, dp_rows, span), B16),
        wdown2=((2, span // 2, D), B16),
        lat_v=((B, D), B16),
        latn=((B, D), B16),
        cot4=((NC, B, D), B16),
        q_all=((NZ, S, Q, I), B16),
        lse=((NZ, 2 * S, NZ * Q * HEADS // 2), F32),
        lse_all=((2 * S, NZ * Q * HEADS // 2), F32),
        mask=((NZ * Q * HEADS // 2, I // 2), B16),
        mask_e=((2, NZ * Q * HEADS // 2, 128), B16),
        o_send=((NZ, S, Q, I), B16),
        o_recv=((NZ, S, Q, I), B16),
        att_f=((B, I), F32),
        att=((B, I), B16),
        hidden=((B, D), F32),
        ffn4=((NC, B, D), B16),
        d_act=((NC, B, span), F32),
        up=((B, span), F32),
        act=((NC, B, span), B16),
        d_up=((NC, B, span), B16),
        df_send=((NC, B, D), B16),
        df_recv=((NC, B, D), B16),
        out_send=((NC, B, D), B16),
        out_recv=((NC, B, D), B16),
        gd=((2, span // 2, D), B16),
        gd_recv=((span // 2, D), B16),
        gd_sum=((NZ, span // 2 // NZ, D), B16),
        gu=((2, NC, dp_rows, span), B16),
        gu_recv=((NC, dp_rows, span), B16),
        gu_sum=((NC, dp_rows, span), B16),
        gu_quad=((NC, dp_rows, span), B16),
        gz_recv=((2, NZ, dp_rows, span), B16),
        gz_sum=((2, dp_rows, span), B16),
        d_hidden=((B, D), F32),
        d_attn=((B, D), B16),
        d_ext=((NZ, S, Q, I + 128), B16),
        dq_send=((NZ, S, Q, I), B16),
        dq_recv=((NZ, S, Q, I), B16),
        dq=((B, I), B16),
        d_lat=((B, D), F32),
        dn=((KR, D), F32),
        mg=((2, R, D), B16),
        stage=((2, B, D), B16),
        sums=((8, D), F32),
        sm=((2, NC, 8, dp_rows), F32),
        sm_recv=((NC, 8, dp_rows), F32),
        sm_sum=((NC, 8, dp_rows), F32),
        sm_quad=((NC, 8, dp_rows), F32),
        sm_z=((NZ, 8, dp_rows), F32),
        sm_all=((8, dp_rows), F32),
    )
    for letter, rows, cols in (("k", dp_rows, 2 * I), ("q", dp_rows, I), ("o", o_rows, D)):
        name = "g" + letter
        buffers[name] = ((2, NC, rows, cols), B16)
        for tail in ("_recv", "_sum", "_quad"):
            buffers[name + tail] = ((NC, rows, cols), B16)
        for tail in ("_z", "_zr"):
            buffers[name + tail] = ((NZ, rows // NZ, cols), B16)
        buffers[name + "_f"] = ((rows // NZ, cols), B16)
    same = dict(gk="gu", gu_sum="act", gd_sum="d_up", gk_sum="df_send", dq_send="o_send", d_lat="up")
    for name in same:
        del buffers[name]
    names = list(ins) + list(outs) + list(buffers) + ["lsem", "ssem", "rsem", "msem", "dsem"]
    geo = (S, R, Q, D, I, NC, NZ)

    def body(*refs):
        table = dict(zip(names, refs))
        for name, base in same.items():
            table[name] = table[base]
        fused_kernel(geo, types.SimpleNamespace(**table))

    got = pl.pallas_call(
        body,
        out_shape=[jax.ShapeDtypeStruct(s, d) for s, d in outs.values()],
        in_specs=in_specs,
        out_specs=[hbm] * len(outs),
        scratch_shapes=[pltpu.VMEM(s, d) for s, d in buffers.values()]
        + [DMA((28,)), DMA((120,)), DMA((120,)), DMA((2,)), DMA((4,))],
        compiler_params=pltpu.CompilerParams(
            collective_id=1, has_side_effects=True, vmem_limit_bytes=VMEM_BYTES
        ),
        name="resampler",
    )(*ins.values())
    out = types.SimpleNamespace(**dict(zip(outs, got)))
    grad_up = jnp.transpose(out.gup, (1, 0, 2))
    return (
        out.latents_out.reshape(latents.shape),
        out.media_grad.reshape(media.shape),
        out.latent_grad.reshape(latents.shape),
        *[out.gsmall[i] for i in range(6)],
        out.gquery.reshape(wq.shape).astype(F32),
        out.gkv.reshape(wkv.shape).astype(F32),
        out.gout.reshape(wo.shape).astype(F32),
        grad_up.reshape(wup.shape).astype(F32),
        out.gdown.reshape(wdown.shape).astype(F32),
    )


def solution(mesh):
    rows4 = P(None, "dp", "lat", None)
    vec = P("dp")
    mat = P("dp", None)
    n_dp, n_lat = mesh.shape["dp"], mesh.shape["lat"]
    body = fused if n_dp == 2 * n_lat else shards
    return jax.shard_map(
        functools.partial(body, n_dp, n_lat),
        mesh=mesh,
        in_specs=(rows4, rows4, P(None, "dp"), rows4) + (vec,) * 6 + (mat,) * 5,
        out_specs=(rows4,) * 3 + (vec,) * 6 + (mat,) * 5,
        check_vma=False,
    )
```

```python
import functools
import types

import jax
import jax.numpy as jnp
from jax import lax
from jax.experimental import pallas as pl
from jax.experimental.pallas import tpu as pltpu
from jax.sharding import PartitionSpec as P

HEADS = 8
HEAD = 64
VIS = 256
EPS = 1e-05
F32 = jnp.float32
B16 = jnp.bfloat16
MESH = pl.DeviceIdType.MESH
DMA = pltpu.SemaphoreType.DMA
VMEM_BYTES = 62 << 20


def exchange_kernel(axis, n, modes, *refs):
    count = len(modes)
    ins, outs = refs[:count], refs[count : 2 * count]
    send, recv, own = refs[2 * count :]
    me = lax.axis_index(axis)
    barrier = pltpu.get_barrier_semaphore()
    for k in range(1, n):
        pl.semaphore_signal(
            barrier, inc=1, device_id={axis: lax.rem(me + k, n)}, device_id_type=MESH
        )
    pl.semaphore_wait(barrier, n - 1)
    copies = []
    for k in range(1, n):
        peer = lax.rem(me + k, n)
        for i in range(count):
            source = ins[i] if modes[i] == "gather" else ins[i].at[peer]
            copy = pltpu.make_async_remote_copy(
                source,
                outs[i].at[me],
                send.at[i, k],
                recv.at[i, k],
                device_id={axis: peer},
                device_id_type=MESH,
            )
            copy.start()
            copies.append(copy)
    for i in range(count):
        source = ins[i] if modes[i] == "gather" else ins[i].at[me]
        copy = pltpu.make_async_copy(source, outs[i].at[me], own.at[i])
        copy.start()
        copies.append(copy)
    for copy in copies:
        copy.wait()


class Exchanges:
    def __init__(self, sizes):
        self.sizes = sizes
        self.used = 0

    def __call__(self, axis, arrays, modes):
        n = self.sizes[axis]
        count = len(arrays)
        outs = [
            jax.ShapeDtypeStruct(((n,) + a.shape) if m == "gather" else a.shape, a.dtype)
            for a, m in zip(arrays, modes)
        ]
        self.used += 1
        space = pl.BlockSpec(memory_space=pl.ANY)
        return pl.pallas_call(
            functools.partial(exchange_kernel, axis, n, modes),
            out_shape=outs,
            in_specs=[space] * count,
            out_specs=[space] * count,
            scratch_shapes=[DMA((count, n)), DMA((count, n)), DMA((count,))],
            compiler_params=pltpu.CompilerParams(collective_id=self.used, has_side_effects=True),
            name="exchange_%d" % self.used,
        )(*arrays)


def norm_parts(x):
    mean = jnp.mean(x, -1, keepdims=True)
    cent = x - mean
    factor = lax.rsqrt(jnp.mean(cent * cent, -1, keepdims=True) + EPS)
    return cent * factor, factor


def norm_back(grad, unit, factor, gain):
    scaled = grad * gain
    inner = jnp.mean(scaled * unit, -1, keepdims=True)
    d_input = factor * (scaled - jnp.mean(scaled, -1, keepdims=True) - unit * inner)
    return d_input, jnp.sum(grad * unit, 0), jnp.sum(grad, 0)


def mm(a, b):
    return lax.dot_general(a, b, (((1,), (0,)), ((), ())), preferred_element_type=F32)


def mm_nt(a, b):
    return lax.dot_general(a, b, (((1,), (1,)), ((), ())), preferred_element_type=F32)


def mm_tn(a, b):
    return lax.dot_general(a, b, (((0,), (0,)), ((), ())), preferred_element_type=F32)


def shards(n_dp, n_lat, media, latents, counts, cotangent, g_m, b_m, g_l, b_l, g_f, b_f, wq, wkv, wo, wup, wdown):
    ex = Exchanges({"dp": n_dp, "lat": n_lat})
    micro, per, rows, width = media.shape
    nq = latents.shape[2]
    S = micro * per
    inner = wq.shape[1]
    ff = wup.shape[1]
    ff_part = ff // n_dp
    d_part = width // n_dp
    lat_at = lax.axis_index("lat")
    med = media.reshape(S * rows, width)
    lat = latents.reshape(S * nq, width).astype(F32)
    cot = cotangent.reshape(S * nq, width)
    count = counts.reshape(S)

    small = jnp.stack([g_m, b_m, g_l, b_l, g_f, b_f], 0)
    small_all, wq_all, wkv_all, wo_all = ex("dp", [small, wq, wkv, wo], ["gather"] * 4)
    params = jnp.transpose(small_all, (1, 0, 2)).reshape(6, width).astype(F32)
    wq_all = wq_all.reshape(width, inner)
    wkv_all = wkv_all.reshape(width, 2 * inner)
    wo_all = wo_all.reshape(inner, width)
    wup_cols = jnp.transpose(wup.reshape(d_part, n_dp, ff_part), (1, 0, 2))
    cot_all, wup_s = ex("dp", [cot, wup_cols], ["gather", "swap"])
    cot_all = cot_all.reshape(-1, width)
    wup_s = wup_s.reshape(width, ff_part)

    med_unit, med_factor = norm_parts(med.astype(F32))
    med_norm = (med_unit * params[0] + params[1]).astype(B16)
    lat_unit, lat_factor = norm_parts(lat)
    lat_norm = (lat_unit * params[2] + params[3]).astype(B16)
    query = (mm(lat_norm, wq_all) * 0.125).astype(B16)
    (query_all,) = ex("lat", [query], ["gather"])
    kv_med = mm(med_norm, wkv_all).astype(B16)
    kv_lat = mm(lat_norm, wkv_all).astype(B16)
    keyval = jnp.concatenate(
        [kv_med.reshape(S, rows, 2 * inner), kv_lat.reshape(S, nq, 2 * inner)], 1
    )
    kc = rows + nq
    keys = keyval[:, :, :inner].reshape(S, kc, HEADS, HEAD)
    values = keyval[:, :, inner:].reshape(S, kc, HEADS, HEAD)
    heads_q = query_all.reshape(n_lat, S, nq, HEADS, HEAD)
    slot = (lat_at * rows + lax.iota(jnp.int32, rows)) // VIS
    live = jnp.concatenate(
        [slot[None, :] < count[:, None], jnp.ones((S, nq), dtype=bool)], 1
    )
    score = jnp.einsum("zsqhd,skhd->shzqk", heads_q, keys, preferred_element_type=F32)
    score = jnp.where(live[:, None, None, None, :], score, -1e30)
    top = jnp.max(score, -1)
    p = jnp.exp(score - top[..., None])
    total = jnp.sum(p, -1)
    part = jnp.einsum("shzqk,skhd->zsqhd", p.astype(B16), values, preferred_element_type=F32)
    scale = jnp.transpose(1.0 / total, (2, 0, 3, 1))[..., None]
    part = (part * scale).astype(B16).reshape(n_lat, S * nq, inner)
    stats = jnp.stack([top, total], 0).reshape(2 * S * HEADS, n_lat * nq)
    part_all, stats_all = ex("lat", [part, stats], ["swap", "gather"])
    stats_all = stats_all.reshape(n_lat, 2, S, HEADS, n_lat, nq)
    tops, totals = stats_all[:, 0], stats_all[:, 1]
    top_max = jnp.max(tops, 0)
    weight = totals * jnp.exp(tops - top_max)
    whole = jnp.sum(weight, 0)
    lse = top_max + jnp.log(whole)
    weight = lax.dynamic_index_in_dim(weight / whole, lat_at, 3, keepdims=False)
    weight = jnp.transpose(weight, (0, 1, 3, 2)).reshape(n_lat, S * nq, HEADS, 1)
    attended_f = jnp.sum(part_all.reshape(n_lat, S * nq, HEADS, HEAD).astype(F32) * weight, 0)
    attended = attended_f.reshape(S * nq, inner).astype(B16)

    hidden = lat + mm(attended, wo_all)
    ffn_unit, ffn_factor = norm_parts(hidden)
    ff_norm = (ffn_unit * params[4] + params[5]).astype(B16)
    (ffn_all,) = ex("dp", [ff_norm], ["gather"])
    ffn_all = ffn_all.reshape(-1, width)
    up = mm(ffn_all, wup_s)
    act_f, pull = jax.vjp(lambda v: jax.nn.gelu(v, approximate=False), up)
    act = act_f.astype(B16)
    d_act = mm_nt(cot_all, wdown)
    d_up = pull(d_act)[0].astype(B16)
    out_part = mm(act, wdown).astype(B16).reshape(n_dp, S * nq, width)
    d_ffn_part = mm_nt(d_up, wup_s).astype(B16).reshape(n_dp, S * nq, width)
    d_ffn_all, out_all = ex("dp", [d_ffn_part, out_part], ["swap", "swap"])
    latents_out = (hidden + jnp.sum(out_all.astype(F32), 0)).astype(B16)
    d_ffn = jnp.sum(d_ffn_all.astype(F32), 0)
    grad_down = mm_tn(act, cot_all)
    grad_up = mm_tn(ffn_all, d_up)
    d_h, grad_gf, grad_bf = norm_back(d_ffn, ffn_unit, ffn_factor, params[4])
    d_hidden = cot.astype(F32) + d_h
    d_attn = d_hidden.astype(B16)
    grad_out = mm_tn(attended, d_attn)
    d_att = mm_nt(d_attn, wo_all).astype(B16)
    delta = jnp.sum(
        (d_att.astype(F32) * attended_f.reshape(S * nq, inner)).reshape(S * nq, HEADS, HEAD), -1
    )
    d_att_all, delta_all = ex("lat", [d_att, delta.T], ["gather", "gather"])
    d_att_h = d_att_all.reshape(n_lat, S, nq, HEADS, HEAD)
    delta_h = jnp.transpose(delta_all.reshape(n_lat, HEADS, S, nq), (2, 1, 0, 3))[..., None]
    prob = jnp.exp(score - lse[..., None])
    d_prob = jnp.einsum("zsqhd,skhd->shzqk", d_att_h, values, preferred_element_type=F32)
    d_score = (prob * (d_prob - delta_h)).astype(B16)
    dq_part = jnp.einsum("shzqk,skhd->zsqhd", d_score, keys, preferred_element_type=F32)
    (dq_all,) = ex("lat", [dq_part.astype(B16).reshape(n_lat, S * nq, inner)], ["swap"])
    d_keys = jnp.einsum("shzqk,zsqhd->skhd", d_score, heads_q, preferred_element_type=F32)
    d_values = jnp.einsum(
        "shzqk,zsqhd->skhd", prob.astype(B16), d_att_h, preferred_element_type=F32
    )
    d_kv = jnp.concatenate(
        [d_keys.reshape(S, kc, inner), d_values.reshape(S, kc, inner)], -1
    ).astype(B16)
    d_kv_med = d_kv[:, :rows].reshape(S * rows, 2 * inner)
    d_kv_lat = d_kv[:, rows:].reshape(S * nq, 2 * inner)
    grad_kv = mm_tn(med_norm, d_kv_med) + mm_tn(lat_norm, d_kv_lat)
    d_mnorm = mm_nt(d_kv_med, wkv_all)
    d_media, grad_gm, grad_bm = norm_back(d_mnorm, med_unit, med_factor, params[0])
    dq = (jnp.sum(dq_all.astype(F32), 0) * 0.125).astype(B16)
    grad_q = mm_tn(lat_norm, dq)
    d_lnorm = mm_nt(dq, wq_all) + mm_nt(d_kv_lat, wkv_all)
    d_latn, grad_gl, grad_bl = norm_back(d_lnorm, lat_unit, lat_factor, params[2])
    latent_grad = (d_hidden + d_latn).astype(B16)

    smalls = jnp.stack([grad_gm, grad_bm, grad_gl, grad_bl, grad_gf, grad_bf], 0)
    smalls = jnp.transpose(smalls.reshape(6, n_dp, d_part), (1, 0, 2))
    small_s, q_s, kv_s, o_s, up_s = ex(
        "dp",
        [
            smalls,
            grad_q.astype(B16).reshape(n_dp, d_part, inner),
            grad_kv.astype(B16).reshape(n_dp, d_part, 2 * inner),
            grad_out.astype(B16).reshape(n_dp, inner // n_dp, width),
            grad_up.astype(B16).reshape(n_dp, d_part, ff_part),
        ],
        ["swap"] * 5,
    )
    small_s = jnp.sum(small_s, 0)
    q_s = jnp.sum(q_s.astype(F32), 0)
    kv_s = jnp.sum(kv_s.astype(F32), 0)
    o_s = jnp.sum(o_s.astype(F32), 0)
    up_s = jnp.transpose(up_s, (1, 0, 2)).reshape(d_part, ff)
    pieces = [q_s, kv_s, o_s, up_s, grad_down]
    cut = [x.astype(B16).reshape(n_lat, x.shape[0] // n_lat, x.shape[1]) for x in pieces]
    got = ex("lat", cut + [small_s], ["swap"] * 5 + ["gather"])
    small_s = jnp.sum(got[5], 0)
    summed = [jnp.sum(x.astype(F32), 0).astype(B16) for x in got[:5]]
    full = ex("lat", summed, ["gather"] * 5)
    grads = [x.reshape(y.shape).astype(F32) for x, y in zip(full, pieces)]
    return (
        latents_out.reshape(latents.shape),
        d_media.astype(B16).reshape(media.shape),
        latent_grad.reshape(latents.shape),
        *[small_s[i] for i in range(6)],
        *grads,
    )


NORM_EARLY = 3
UP_EARLY = 4
HOP1, HOP2 = 2, 4
HOPS_ATT = ((1, 3), (6, 4))
HOPS_KV = ((1, 5),)
HOPS_Q = (6, 7)
HOPS_MED = ((2, 8), (5, 9))
MED_SPLIT = 4
HOP_END = 10

NT, NN, TN = (((1,), (1,)), ((), ())), (((1,), (0,)), ((), ())), (((0,), (0,)), ((), ()))


def dot(a, b, form):
    return lax.dot_general(a, b, form, preferred_element_type=F32)


def centred(x):
    mean = jnp.mean(x, -1, keepdims=True)
    cent = x - mean
    factor = lax.rsqrt(jnp.mean(cent * cent, -1, keepdims=True) + EPS)
    return cent * factor, factor


def back(grad, unit, factor, gain):
    scaled = grad * gain
    inner = jnp.mean(scaled * unit, -1, keepdims=True)
    return factor * (scaled - jnp.mean(scaled, -1, keepdims=True) - unit * inner)


def fused_kernel(geo, refs):
    S, R, Q, D, I, NC, NZ = geo
    KR = R + Q
    B = S * Q
    G = 2
    W = I // G
    HG = HEADS // G
    r = refs
    me = lax.axis_index("dp")
    z = lax.axis_index("lat")
    chip = me // 2
    core = lax.rem(me, 2)
    sib = me + 1 - 2 * core
    other = 1 - core

    def chip_to(k):
        return lax.rem(chip + k, NC)

    def chip_from(k):
        return lax.rem(chip + NC - k, NC)

    def z_to(k):
        return lax.rem(z + k, NZ)

    def z_from(k):
        return lax.rem(z + NZ - k, NZ)

    quads = range(1, NC)
    planes = range(1, NZ)
    used = [0, 0]

    def local(src, dst):
        sem = r.lsem.at[used[0]]
        used[0] += 1
        copy = pltpu.make_async_copy(src, dst, sem)
        copy.start()
        return copy

    def remote(src, dst, **where):
        at = used[1]
        used[1] += 1
        copy = pltpu.make_async_remote_copy(
            src, dst, r.ssem.at[at], r.rsem.at[at], device_id=where, device_id_type=MESH
        )
        copy.start()
        return copy

    class Planned:
        def __init__(self, make):
            at = used[1]
            used[1] += 1

            def build():
                src, dst, where = make()
                return pltpu.make_async_remote_copy(
                    src, dst, r.ssem.at[at], r.rsem.at[at], device_id=where, device_id_type=MESH
                )

            self.build = build

        def start(self):
            self.build().start()

        def wait(self):
            self.build().wait()

        def wait_send(self):
            self.build().wait_send()

        def wait_recv(self):
            self.build().wait_recv()

    class Spread:
        def __init__(self, src_for, dst_at):
            self.dst_at = dst_at
            self.far = [remote(src_for(chip_to(k)), dst_at(me), dp=2 * chip_to(k) + core) for k in quads]
            self.near = remote(src_for(chip), dst_at(me), dp=sib)
            self.own = local(src_for(chip), dst_at(me))

        def forward(self):
            self.passed = []
            for k in quads:
                self.far[k - 1].wait_recv()
                slot = self.dst_at(2 * chip_from(k) + core)
                self.passed.append(remote(slot, slot, dp=sib))

        def finish(self):
            self.own.wait()
            self.near.wait()
            for copy in self.far:
                copy.wait_send()
            for copy in self.passed:
                copy.wait()

    def to_quad(src_for, dst):
        return [remote(src_for(chip_to(k)), dst, dp=2 * chip_to(k) + core) for k in quads]

    def to_planes(src_for, dst):
        return [remote(src_for(z_to(k)), dst, lat=z_to(k)) for k in planes]

    def wait_all(copies):
        for copy in copies:
            copy.wait()

    class Meet:
        def __init__(self, own, got, cross, out, root):
            self.own, self.got, self.crossed, self.out, self.root = own, got, cross, out, root
            peer = 3 - root
            self.up = Planned(lambda: (own, got, {"lat": 1 + z // 2}))
            self.over = Planned(lambda: (own, cross, {"lat": root}))
            self.near = Planned(lambda: (own, out, {"lat": 3 * (root - 1)}))
            self.back = Planned(lambda: (own, out, {"lat": peer}))
            self.far = Planned(lambda: (out, out, {"lat": 3 * (peer - 1)}))
            self.lsem = r.lsem.at[used[0]]
            used[0] += 1

        def send(self):
            @pl.when(jnp.logical_or(z == 0, z == NZ - 1))
            def _():
                self.up.start()

        def merge(self):
            @pl.when(z == 3 - self.root)
            def _():
                self.up.wait_recv()
                self.own[...] = (self.own[...].astype(F32) + self.got[...].astype(F32)).astype(B16)
                self.over.start()

        def total(self):
            @pl.when(z == self.root)
            def _():
                self.up.wait_recv()
                both = self.own[...].astype(F32) + self.got[...].astype(F32)
                self.over.wait_recv()
                self.own[...] = (both + self.crossed[...].astype(F32)).astype(B16)
                self.near.start()
                self.back.start()
                pltpu.make_async_copy(self.own, self.out, self.lsem).start()

        def relay(self):
            @pl.when(z == 3 - self.root)
            def _():
                self.back.wait_recv()
                self.far.start()

        def finish(self):
            root, peer = self.root, 3 - self.root

            @pl.when(jnp.logical_or(z == 0, z == NZ - 1))
            def _():
                self.up.wait_send()

            @pl.when(z == 3 * (root - 1))
            def _():
                self.near.wait_recv()

            @pl.when(z == 3 * (peer - 1))
            def _():
                self.far.wait_recv()

            @pl.when(z == peer)
            def _():
                self.over.wait_send()
                self.far.wait_send()

            @pl.when(z == root)
            def _():
                self.near.wait_send()
                self.back.wait_send()
                pltpu.make_async_copy(self.own, self.out, self.lsem).wait()

    barrier = pltpu.get_barrier_semaphore()
    for k in quads:
        pl.semaphore_signal(barrier, inc=1, device_id={"dp": 2 * chip_to(k) + core}, device_id_type=MESH)
    pl.semaphore_signal(barrier, inc=1, device_id={"dp": sib}, device_id_type=MESH)
    for k in planes:
        pl.semaphore_signal(barrier, inc=1, device_id={"lat": z_to(k)}, device_id_type=MESH)
    pl.semaphore_wait(barrier, NC - 1 + 1 + NZ - 1)

    def whole(ref):
        return lambda _: ref

    def rows_at(ref):
        return lambda d: ref.at[d]

    def cols_at(ref, at, size):
        return lambda d: ref.at[d, :, at : at + size]

    g_small = Spread(whole(r.small), rows_at(r.small_all))
    g_wq = Spread(whole(r.wq), rows_at(r.wq_all))
    lat_in = local(r.lat, r.lat_v)
    cot_in = local(r.cot, r.cot4.at[chip])
    slots = r.med.shape[0]

    def med_copy(s):
        slot = lax.rem(s, slots)
        return pltpu.make_async_copy(r.media.at[s], r.med.at[slot], r.dsem.at[slot])

    def med_first():
        for s in range(slots):
            med_copy(jnp.int32(s)).start()

    def med_next(s):
        @pl.when(s + slots < S)
        def _():
            med_copy(s + slots).start()

    med_first()
    g_small.forward()
    g_small.finish()
    params = r.params
    for d in range(2 * NC):
        span = D // (2 * NC)
        params[0:6, d * span : (d + 1) * span] = r.small_all[d].astype(F32)

    def param(i):
        return params[i : i + 1, :]

    lat_in.wait()
    unit, _ = centred(r.lat_v[...].astype(F32))
    r.latn[...] = (unit * param(2) + param(3)).astype(B16)
    rb = 64

    def norm_sample(s, carry):
        slot = lax.rem(s, slots)
        med_copy(s).wait()

        def part(i, inner):
            x = r.med[slot, pl.ds(pl.multiple_of(i * rb, rb), rb), :].astype(F32)
            u, _ = centred(x)
            row = pl.multiple_of(s * KR + i * rb, 16)
            r.X[pl.ds(row, rb), :] = (u * param(0) + param(1)).astype(B16)
            return inner

        lax.fori_loop(0, R // rb, part, 0)
        row = pl.multiple_of(s * KR + R, 16)
        at = pl.multiple_of(s * Q, 16)
        r.X[pl.ds(row, Q), :] = r.latn[pl.ds(at, Q), :]
        med_next(s)
        return carry

    early = NORM_EARLY
    lax.fori_loop(0, early, norm_sample, 0)
    g_wq.forward()
    g_key = Spread(lambda _: r.wkv.at[:, 0:I], cols_at(r.wkv_all, 0, I))
    g_wq.finish()
    query = dot(r.latn[...], r.wq_all[...].reshape(D, I), NN) * 0.125
    r.q_all[z] = query.astype(B16).reshape(S, Q, I)
    q_out = to_planes(lambda _: r.q_all.at[z], r.q_all.at[z])
    lax.fori_loop(early, S, norm_sample, 0)
    med_first()
    g_key.forward()
    g_val = Spread(lambda _: r.wkv.at[:, I : 2 * I], cols_at(r.wkv_all, I, I))
    g_wo = Spread(whole(r.wo), rows_at(r.wo_all))
    g_key.finish()
    span = r.wup_all.shape[2]

    def up_slice(k):
        return r.wup.at[:, pl.ds(pl.multiple_of(k * span, 128), span)]

    def key_cols(s, carry):
        rows = pl.ds(pl.multiple_of(s * KR, 16), KR)
        r.KV[rows, 0:I] = dot(r.X[rows, :], r.wkv_all[:, :, 0:I].reshape(D, I), NN).astype(B16)
        return carry

    def value_cols(s, carry):
        rows = pl.ds(pl.multiple_of(s * KR, 16), KR)
        r.KV[rows, I : 2 * I] = dot(r.X[rows, :], r.wkv_all[:, :, I : 2 * I].reshape(D, I), NN).astype(B16)
        return carry

    lax.fori_loop(0, S, key_cols, 0)
    g_val.forward()
    g_val.finish()
    cot_in.wait()
    g_cot = to_quad(lambda _: r.cot, r.cot4.at[chip])
    g_down = remote(r.wdown, r.wdown2.at[core], dp=sib)
    g_down_own = local(r.wdown, r.wdown2.at[core])
    g_up = Spread(up_slice, rows_at(r.wup_all))
    lax.fori_loop(0, S, value_cols, 0)
    g_wo.forward()
    g_wo.finish()
    wait_all(q_out)

    own_head = (
        lax.broadcasted_iota(jnp.int32, (HG * NZ * Q, W), 0) // (NZ * Q)
        == lax.broadcasted_iota(jnp.int32, (HG * NZ * Q, W), 1) // HEAD
    )
    r.mask[...] = own_head.astype(F32).astype(B16)

    def spread_heads(x):
        return jnp.concatenate([x] * HG, 0) * r.mask[...]

    def take_heads(x):
        low = lax.broadcasted_iota(jnp.int32, (NZ * Q, 2 * HEAD), 1) < HEAD
        cols = []
        for pair in range(HG // 2):
            block = x[:, pair * 2 * HEAD : (pair + 1) * 2 * HEAD]
            n = NZ * Q
            cols.append(
                jnp.where(low, block[2 * pair * n : (2 * pair + 1) * n], block[(2 * pair + 1) * n : (2 * pair + 2) * n])
            )
        return jnp.concatenate(cols, 1)

    def scores(s, g, qbig):
        rows = pl.ds(pl.multiple_of(s * KR, 16), KR)
        raw = dot(r.KV[rows, g * W : (g + 1) * W], qbig, NT)
        row = lax.broadcasted_iota(jnp.int32, raw.shape, 0)
        live = jnp.logical_or(row >= R, row + z * R < r.counts[s // r.counts.shape[1], lax.rem(s, r.counts.shape[1])] * VIS)
        return jnp.where(live, raw, -1e30)

    def queries(s, g):
        return spread_heads(r.q_all[:, s, :, g * W : (g + 1) * W].reshape(NZ * Q, W))

    def attend(s, carry):
        rows = pl.ds(pl.multiple_of(s * KR, 16), KR)
        for g in range(G):
            score = scores(s, g, queries(s, g))
            top = jnp.max(score, 0, keepdims=True)
            grown = jnp.exp(score - top)
            total = jnp.sum(grown, 0, keepdims=True)
            r.lse[z, pl.ds(g * S + s, 1), :] = top + jnp.log(total)
            prob = (grown * (1.0 / total)).astype(B16)
            part = dot(prob, r.KV[rows, I + g * W : I + (g + 1) * W], TN)
            r.o_send[:, s, :, g * W : (g + 1) * W] = take_heads(part).astype(B16).reshape(NZ, Q, W)
        return carry

    lax.fori_loop(0, S, attend, 0)
    lse_out = to_planes(lambda _: r.lse.at[z], r.lse.at[z])
    o_out = to_planes(lambda k: r.o_send.at[k], r.o_recv.at[z])
    g_up.forward()
    wait_all(g_cot)
    g_down.wait()
    g_down_own.wait()

    def act_grad(b, carry):
        r.d_act[b] = dot(r.cot4[b], r.wdown2[...].reshape(span, D), NT)
        return carry

    lax.fori_loop(0, NC, act_grad, 0)
    g_up.finish()
    wait_all(lse_out)
    every = r.lse[...]
    top = jnp.max(every, 0)
    lse_all = top + jnp.log(jnp.sum(jnp.exp(every - top[None]), 0))
    r.lse_all[...] = lse_all
    r.lse[...] = jnp.exp(every - lse_all[None])
    pick = (
        lax.rem(lax.broadcasted_iota(jnp.int32, (B, HG * NZ * Q), 1), NZ * Q)
        == lax.rem(lax.broadcasted_iota(jnp.int32, (B, HG * NZ * Q), 0), Q) + z * Q
    )
    for k in range(NZ):
        store = r.hidden if k < 2 else r.d_hidden
        for g in range(G):
            lanes = jnp.broadcast_to(
                r.lse[z_from(k), g * S : (g + 1) * S, :][:, None, :], (S, Q, HG * NZ * Q)
            ).reshape(B, HG * NZ * Q)
            lanes = jnp.where(pick, lanes, 0.0)
            coarse = lanes.astype(B16)
            fine = (lanes - coarse.astype(F32)).astype(B16)
            at = (k % 2) * I + g * W
            store[:, at : at + W] = dot(coarse, r.mask[...], NN) + dot(fine, r.mask[...], NN)
    wait_all(o_out)
    att = r.hidden[:, 0:I] * r.o_send[z].astype(F32).reshape(B, I)
    for k in planes:
        store = r.hidden if k < 2 else r.d_hidden
        at = (k % 2) * I
        att = att + store[:, at : at + I] * r.o_recv[z_from(k)].astype(F32).reshape(B, I)
    r.att_f[...] = att
    r.att[...] = att.astype(B16)
    hidden = r.lat_v[...].astype(F32) + dot(r.att[...], r.wo_all[...].reshape(I, D), NN)
    r.hidden[...] = hidden
    unit, _ = centred(hidden)
    r.ffn4[chip] = (unit * param(4) + param(5)).astype(B16)
    f_out = to_quad(lambda _: r.ffn4.at[chip], r.ffn4.at[chip])

    def feed(b):
        r.up[...] = dot(r.ffn4[b], r.wup_all[...].reshape(D, span), NN)

        def gelu_part(i, carry):
            rows = pl.ds(pl.multiple_of(i * 32, 32), 32)
            x = r.up[rows, :]
            cdf = 0.5 * (1.0 + lax.erf(x * 0.7071067811865476))
            pdf = jnp.exp(-0.5 * x * x) * 0.3989422804014327
            r.act[b, rows, :] = (x * cdf).astype(B16)
            r.d_up[b, rows, :] = (r.d_act[b, rows, :] * (cdf + x * pdf)).astype(B16)
            return carry

        lax.fori_loop(0, B // 32, gelu_part, 0)
        r.df_send[b] = dot(r.d_up[b], r.wup_all[...].reshape(D, span), NT).astype(B16)

    feed(chip)
    df_out = []
    for k in quads:
        f_out[k - 1].wait_recv()
        b = chip_from(k)
        feed(b)
        df_out.append(remote(r.df_send.at[b], r.df_recv.at[chip], dp=2 * b + core))

    half = span // 2
    act2 = r.act

    def grad_down(i, carry):
        at = pl.multiple_of(i * 256, 256)
        value = dot(
            act2[:, :, pl.ds(at, 256)].reshape(NC * B, 256), r.cot4[...].reshape(NC * B, D), TN
        )
        r.gd[i // (half // 256), pl.ds(pl.multiple_of(lax.rem(i * 256, half), 256), 256), :] = value.astype(B16)
        return carry

    lax.fori_loop(0, span // 256, grad_down, 0)
    gd_out = remote(r.gd.at[other], r.gd_recv, dp=sib)
    dw = D // NC
    hw = dw // 2

    def grad_up(i, carry):
        at = pl.multiple_of(i * dw, dw)
        value = dot(
            r.ffn4[:, :, pl.ds(at, dw)].reshape(NC * B, dw), r.d_up[...].reshape(NC * B, span), TN
        ).astype(B16)
        r.gu[0, i] = value[:hw]
        r.gu[1, i] = value[hw:]
        return carry

    lax.fori_loop(0, NC, grad_up, 0)
    gu_out = remote(r.gu.at[other], r.gu_recv, dp=sib)

    def down(i, carry):
        r.out_send[i] = dot(r.act[i], r.wdown2[...].reshape(span, D), NN).astype(B16)
        return carry

    lax.fori_loop(0, NC, down, 0)
    piece = half // NZ
    gd_out.wait()
    for j in range(NZ):
        rows = slice(j * piece, (j + 1) * piece)
        r.gd_sum[j] = (r.gd[core, rows, :].astype(F32) + r.gd_recv[rows, :].astype(F32)).astype(B16)

    meets = [
        Meet(r.gd_sum.at[j], r.z_got.at[j], r.z_cross.at[j // 2], r.gdown.at[j * piece : (j + 1) * piece, :], 1 + j % 2)
        for j in range(NZ)
    ]
    meets += [
        Meet(r.gu_quad.at[j], r.z_got.at[NZ + j], r.z_cross.at[(NZ + j) // 2], r.gup.at[:, j * span : (j + 1) * span], 1 + j % 2)
        for j in range(NC)
    ]
    for part_, got_, cross_, out_ in (
        (r.go_t, r.go_got, r.go_cross, r.gout),
        (r.gk_t, r.gk_got, r.gk_cross, r.gkv),
        (r.gq_t, r.gq_got, r.gq_cross, r.gquery),
    ):
        rows = part_.shape[1]
        meets += [
            Meet(part_.at[j], got_.at[j], cross_, out_.at[j * rows : (j + 1) * rows, :], 1 + j) for j in range(2)
        ]

    def hop(n):
        if 0 <= n < len(meets):
            meets[n].merge()
        if 0 <= n - HOP1 < len(meets):
            meets[n - HOP1].total()
        if 0 <= n - HOP2 < len(meets):
            meets[n - HOP2].relay()

    for n in range(UP_EARLY):
        meets[n].send()
    gu_out.wait()

    for copy in f_out:
        copy.wait_send()
    wait_all(df_out)
    d_ffn = r.df_send[chip].astype(F32)
    for k in quads:
        d_ffn = d_ffn + r.df_recv[chip_to(k)].astype(F32)
    unit, factor = centred(r.hidden[...])
    sums = r.sums
    sums[4:5, :] = jnp.sum(d_ffn * unit, 0, keepdims=True)
    sums[5:6, :] = jnp.sum(d_ffn, 0, keepdims=True)
    d_hidden = r.cot4[chip].astype(F32) + back(d_ffn, unit, factor, param(4))
    r.d_hidden[...] = d_hidden
    r.d_attn[...] = d_hidden.astype(B16)
    d_att = dot(r.d_attn[...], r.wo_all[...].reshape(I, D), NT).astype(B16)
    weighed = d_att.astype(F32) * r.att_f[...]
    lane = lax.broadcasted_iota(jnp.int32, (B, 128), 1)
    delta = jnp.zeros((B, 128), F32)
    low_lane = lax.broadcasted_iota(jnp.int32, (B, 128), 1) < HEAD
    for h in range(HEADS):
        block = weighed[:, (h // 2) * 128 : (h // 2) * 128 + 128]
        keep = low_lane if h % 2 == 0 else jnp.logical_not(low_lane)
        one = jnp.sum(jnp.where(keep, block, 0.0), -1, keepdims=True)
        delta = jnp.where(jnp.logical_or(lane == h, lane == HEADS + h), -one, delta)
    coarse = delta.astype(B16).astype(F32)
    ext = jnp.where(lane < HEADS, coarse, delta - coarse).astype(B16)
    r.d_ext[z, :, :, 0:I] = d_att.reshape(S, Q, I)
    r.d_ext[z, :, :, I : I + 128] = ext.reshape(S, Q, 128)
    d_out = to_planes(lambda _: r.d_ext.at[z], r.d_ext.at[z])

    ow = I // NC
    oh = ow // 2
    for i in range(NC):
        value = dot(r.att[:, i * ow : (i + 1) * ow], r.d_attn[...], TN).astype(B16)
        r.go[0, i] = value[:oh]
        r.go[1, i] = value[oh:]
    go_out = remote(r.go.at[other], r.go_recv, dp=sib)

    def add_pair(dst, a, b, n):
        def body(i, carry):
            dst[i] = (a[i].astype(F32) + b[i].astype(F32)).astype(B16)
            return carry

        lax.fori_loop(0, n, body, 0)

    add_pair(r.gu_sum, r.gu.at[core], r.gu_recv, NC)
    guq_out = to_quad(lambda k: r.gu_sum.at[k], r.gu_quad.at[chip])
    out_out = to_quad(lambda k: r.out_send.at[k], r.out_recv.at[chip])
    go_out.wait()
    add_pair(r.go_sum, r.go.at[core], r.go_recv, NC)
    goq_out = to_quad(lambda k: r.go_sum.at[k], r.go_quad.at[chip])
    for n in range(UP_EARLY, NZ):
        meets[n].send()
    hop(0)
    hop(1)
    wait_all(guq_out)
    r.gu_quad[chip] = r.gu_sum[chip]
    for n in range(NZ, NZ + NC):
        meets[n].send()

    def quad_total(own, got):
        total = own[chip].astype(F32)
        for k in quads:
            total = total + got[chip_to(k)].astype(F32)
        return total

    def split_total(dst, own, got):
        total = quad_total(own, got).astype(B16)
        rows = total.shape[0] // 2
        for j in range(2):
            dst[j] = total[j * rows : (j + 1) * rows]

    wait_all(goq_out)
    split_total(r.go_t, r.go_sum, r.go_quad)
    for n in (8, 9):
        meets[n].send()
    hop(2)
    wait_all(d_out)

    ones = jnp.ones((KR, 128), B16)
    lane_e = lax.broadcasted_iota(jnp.int32, (HG * NZ * Q, 128), 1)
    head_e = lax.broadcasted_iota(jnp.int32, (HG * NZ * Q, 128), 0) // (NZ * Q)
    for g in range(G):
        r.mask_e[g] = (
            jnp.logical_or(lane_e == head_e + g * HG, lane_e == head_e + g * HG + HEADS).astype(F32).astype(B16)
        )

    def attend_back(s, carry):
        rows = pl.ds(pl.multiple_of(s * KR, 16), KR)
        for g in range(G):
            qbig = queries(s, g)
            score = scores(s, g, qbig)
            prob = jnp.exp(score - r.lse_all[pl.ds(g * S + s, 1), :])
            dbig = spread_heads(r.d_ext[:, s, :, g * W : (g + 1) * W].reshape(NZ * Q, W))
            minus = r.d_ext[:, s, :, I : I + 128].reshape(NZ * Q, 128)
            minus = jnp.concatenate([minus] * HG, 0) * r.mask_e[g]
            d_prob = dot(r.KV[rows, I + g * W : I + (g + 1) * W], dbig, NT) + dot(ones, minus, NT)
            d_score = (prob * d_prob).astype(B16)
            dq = dot(d_score, r.KV[rows, g * W : (g + 1) * W], TN)
            r.dq_send[:, s, :, g * W : (g + 1) * W] = take_heads(dq).astype(B16).reshape(NZ, Q, W)
            r.KV[rows, g * W : (g + 1) * W] = dot(d_score, qbig, NN).astype(B16)
            r.KV[rows, I + g * W : I + (g + 1) * W] = dot(prob.astype(B16), dbig, NN).astype(B16)
        for at, n in HOPS_ATT:

            @pl.when(s == at)
            def _():
                hop(n)

        return carry

    lax.fori_loop(0, S, attend_back, 0)
    dq_out = to_planes(lambda k: r.dq_send.at[k], r.dq_recv.at[z])

    def grad_kv(i, carry):
        at = pl.multiple_of(i * dw, dw)
        value = dot(r.X[:, pl.ds(at, dw)], r.KV[...], TN).astype(B16)
        r.gk[0, i] = value[:hw]
        r.gk[1, i] = value[hw:]
        for at, n in HOPS_KV:

            @pl.when(i == at)
            def _():
                hop(n)

        return carry

    lax.fori_loop(0, NC, grad_kv, 0)
    gk_out = remote(r.gk.at[other], r.gk_recv, dp=sib)

    wait_all(dq_out)
    dq = r.dq_send[z].astype(F32)
    for k in planes:
        dq = dq + r.dq_recv[z_from(k)].astype(F32)
    r.dq[...] = (dq.reshape(B, I) * 0.125).astype(B16)
    for i in range(NC):
        value = dot(r.latn[:, i * dw : (i + 1) * dw], r.dq[...], TN).astype(B16)
        r.gq[0, i] = value[:hw]
        r.gq[1, i] = value[hw:]
    gqs_out = remote(r.gq.at[other], r.gq_recv, dp=sib)
    gk_out.wait()
    add_pair(r.gk_sum, r.gk.at[core], r.gk_recv, NC)
    gkq_out = to_quad(lambda k: r.gk_sum.at[k], r.gk_quad.at[chip])
    gqs_out.wait()
    add_pair(r.gq_sum, r.gq.at[core], r.gq_recv, NC)
    gqq_out = to_quad(lambda k: r.gq_sum.at[k], r.gq_quad.at[chip])
    for n in HOPS_Q:
        hop(n)

    sums[0:1, :] = jnp.zeros((1, D), F32)
    sums[1:2, :] = jnp.zeros((1, D), F32)
    sums[6:8, :] = jnp.zeros((2, D), F32)

    def media_back(s, carry):
        slot = lax.rem(s, 2)
        held = lax.rem(s, slots)
        rows = pl.ds(pl.multiple_of(s * KR, 16), KR)
        med_copy(s).wait()
        r.dn[...] = dot(r.KV[rows, :], r.wkv_all[...].reshape(D, 2 * I), NT)
        r.d_lat[pl.ds(pl.multiple_of(s * Q, 8), Q), :] = r.dn[R:, :]

        @pl.when(s >= 2)
        def _():
            pltpu.make_async_copy(r.mg.at[slot], r.media_grad.at[s - 2], r.msem.at[slot]).wait()

        def part(i, inner):
            block = pl.ds(pl.multiple_of(i * rb, rb), rb)
            unit, factor = centred(r.med[held, block, :].astype(F32))
            grad = r.dn[block, :]
            sums[0:1, :] += jnp.sum(grad * unit, 0, keepdims=True)
            sums[1:2, :] += jnp.sum(grad, 0, keepdims=True)
            r.mg[slot, block, :] = back(grad, unit, factor, param(0)).astype(B16)
            return inner

        lax.fori_loop(0, R // rb, part, 0)
        pltpu.make_async_copy(r.mg.at[slot], r.media_grad.at[s], r.msem.at[slot]).start()
        med_next(s)
        for at, n in HOPS_MED:

            @pl.when(s == at)
            def _():
                hop(n)

        return carry

    lax.fori_loop(0, MED_SPLIT, media_back, 0)
    wait_all(gkq_out)
    split_total(r.gk_t, r.gk_sum, r.gk_quad)
    wait_all(gqq_out)
    split_total(r.gq_t, r.gq_sum, r.gq_quad)
    for n in range(10, 14):
        meets[n].send()
    lax.fori_loop(MED_SPLIT, S, media_back, 0)

    d_latn = r.d_lat[...] + dot(r.dq[...], r.wq_all[...].reshape(D, I), NT)
    unit, factor = centred(r.lat_v[...].astype(F32))
    sums[2:3, :] = jnp.sum(d_latn * unit, 0, keepdims=True)
    sums[3:4, :] = jnp.sum(d_latn, 0, keepdims=True)
    r.stage[1] = (r.d_hidden[...] + back(d_latn, unit, factor, param(2))).astype(B16)
    put_lat = local(r.stage.at[1], r.latent_grad)

    sp = D // (2 * NC)
    for t in range(NC):
        for cc in range(2):
            d = 2 * t + cc
            r.sm[cc, t] = sums[:, d * sp : (d + 1) * sp]
    sm_out = remote(r.sm.at[other], r.sm_recv, dp=sib)
    hop(HOP_END)
    sm_out.wait()
    r.sm_sum[...] = r.sm[core] + r.sm_recv[...]
    smq_out = to_quad(lambda k: r.sm_sum.at[k], r.sm_quad.at[chip])
    hop(HOP_END + 1)
    wait_all(smq_out)
    r.sm_z[z] = quad_total(r.sm_sum, r.sm_quad)
    zs_out = to_planes(lambda _: r.sm_z.at[z], r.sm_z.at[z])
    hop(HOP_END + 2)
    wait_all(out_out)
    out = r.hidden[...] + r.out_send[chip].astype(F32)
    for k in quads:
        out = out + r.out_recv[chip_to(k)].astype(F32)
    r.stage[0] = out.astype(B16)
    put_out = local(r.stage.at[0], r.latents_out)
    for n in range(HOP_END + 3, len(meets) + HOP2):
        hop(n)
    wait_all(zs_out)
    r.sm_all[...] = jnp.sum(r.sm_z[...], 0)
    put_small = local(r.sm_all, r.gsmall)
    for meet in meets:
        meet.finish()
    put_small.wait()
    for slot in range(2):
        pltpu.make_async_copy(
            r.mg.at[slot], r.media_grad.at[S - 2 + slot], r.msem.at[slot]
        ).wait()
    put_out.wait()
    put_lat.wait()
    assert used[1] <= r.rsem.shape[0] and used[0] <= r.lsem.shape[0]


def fused(n_dp, n_lat, media, latents, counts, cotangent, g_m, b_m, g_l, b_l, g_f, b_f, wq, wkv, wo, wup, wdown):
    micro, per, R, D = media.shape
    Q = latents.shape[2]
    S = micro * per
    B = S * Q
    I = wq.shape[1]
    NC = n_dp // 2
    NZ = n_lat
    KR = R + Q
    span = wup.shape[1] // NC
    dp_rows = D // n_dp
    small = jnp.stack([g_m, b_m, g_l, b_l, g_f, b_f], 0)
    hbm = pl.BlockSpec(memory_space=pl.ANY)
    ins = dict(
        media=media.reshape(S, R, D),
        lat=latents.reshape(B, D),
        cot=cotangent.reshape(B, D),
        small=small,
        wq=wq,
        wkv=wkv,
        wo=wo,
        wup=wup,
        wdown=wdown,
        counts=counts,
    )
    in_specs = [hbm] * 9 + [pl.BlockSpec(memory_space=pltpu.SMEM)]
    outs = dict(
        latents_out=((B, D), B16),
        media_grad=((S, R, D), B16),
        latent_grad=((B, D), B16),
        gsmall=((8, dp_rows), F32),
        gquery=((dp_rows, I), B16),
        gkv=((dp_rows, 2 * I), B16),
        gout=((I // n_dp, D), B16),
        gup=((dp_rows, NC * span), B16),
        gdown=((span // 2, D), B16),
    )
    kv_rows = S * KR
    o_rows = I // n_dp
    buffers = dict(
        med=((4, R, D), B16),
        X=((kv_rows, D), B16),
        KV=((kv_rows, 2 * I), B16),
        small_all=((n_dp, 6, dp_rows), B16),
        params=((8, D), F32),
        wq_all=((n_dp, dp_rows, I), B16),
        wkv_all=((n_dp, dp_rows, 2 * I), B16),
        wo_all=((n_dp, o_rows, D), B16),
        wup_all=((n_dp, dp_rows, span), B16),
        wdown2=((2, span // 2, D), B16),
        lat_v=((B, D), B16),
        latn=((B, D), B16),
        cot4=((NC, B, D), B16),
        q_all=((NZ, S, Q, I), B16),
        lse=((NZ, 2 * S, NZ * Q * HEADS // 2), F32),
        lse_all=((2 * S, NZ * Q * HEADS // 2), F32),
        mask=((NZ * Q * HEADS // 2, I // 2), B16),
        mask_e=((2, NZ * Q * HEADS // 2, 128), B16),
        o_send=((NZ, S, Q, I), B16),
        o_recv=((NZ, S, Q, I), B16),
        att_f=((B, I), F32),
        att=((B, I), B16),
        hidden=((B, D), F32),
        ffn4=((NC, B, D), B16),
        d_act=((NC, B, span), F32),
        up=((B, span), F32),
        act=((NC, B, span), B16),
        d_up=((NC, B, span), B16),
        df_send=((NC, B, D), B16),
        df_recv=((NC, B, D), B16),
        out_send=((NC, B, D), B16),
        out_recv=((NC, B, D), B16),
        gd=((2, span // 2, D), B16),
        gd_recv=((span // 2, D), B16),
        gd_sum=((NZ, span // 2 // NZ, D), B16),
        gu=((2, NC, dp_rows, span), B16),
        gu_recv=((NC, dp_rows, span), B16),
        gu_sum=((NC, dp_rows, span), B16),
        gu_quad=((NC, dp_rows, span), B16),
        z_got=((2 * NZ, dp_rows, span), B16),
        z_cross=((NZ, dp_rows, span), B16),
        d_hidden=((B, D), F32),
        d_attn=((B, D), B16),
        d_ext=((NZ, S, Q, I + 128), B16),
        dq_send=((NZ, S, Q, I), B16),
        dq_recv=((NZ, S, Q, I), B16),
        dq=((B, I), B16),
        d_lat=((B, D), F32),
        dn=((KR, D), F32),
        mg=((2, R, D), B16),
        stage=((2, B, D), B16),
        sums=((8, D), F32),
        sm=((2, NC, 8, dp_rows), F32),
        sm_recv=((NC, 8, dp_rows), F32),
        sm_sum=((NC, 8, dp_rows), F32),
        sm_quad=((NC, 8, dp_rows), F32),
        sm_z=((NZ, 8, dp_rows), F32),
        sm_all=((8, dp_rows), F32),
    )
    for letter, rows, cols in (("k", dp_rows, 2 * I), ("q", dp_rows, I), ("o", o_rows, D)):
        name = "g" + letter
        buffers[name] = ((2, NC, rows, cols), B16)
        for tail in ("_recv", "_sum", "_quad"):
            buffers[name + tail] = ((NC, rows, cols), B16)
        buffers[name + "_t"] = ((2, rows // 2, cols), B16)
        buffers[name + "_got"] = ((2, rows // 2, cols), B16)
        buffers[name + "_cross"] = ((rows // 2, cols), B16)
    same = dict(gk="gu", gu_sum="act", gd_sum="d_up", gk_sum="df_send", dq_send="o_send", d_lat="up")
    for name in same:
        del buffers[name]
    names = list(ins) + list(outs) + list(buffers) + ["lsem", "ssem", "rsem", "msem", "dsem"]
    geo = (S, R, Q, D, I, NC, NZ)

    def body(*refs):
        table = dict(zip(names, refs))
        for name, base in same.items():
            table[name] = table[base]
        fused_kernel(geo, types.SimpleNamespace(**table))

    got = pl.pallas_call(
        body,
        out_shape=[jax.ShapeDtypeStruct(s, d) for s, d in outs.values()],
        in_specs=in_specs,
        out_specs=[hbm] * len(outs),
        scratch_shapes=[pltpu.VMEM(s, d) for s, d in buffers.values()]
        + [DMA((40,)), DMA((176,)), DMA((176,)), DMA((2,)), DMA((4,))],
        compiler_params=pltpu.CompilerParams(
            collective_id=1, has_side_effects=True, vmem_limit_bytes=VMEM_BYTES
        ),
        name="resampler",
    )(*ins.values())
    done = finish(got)
    return (
        done[0].reshape(latents.shape),
        done[1].reshape(media.shape),
        done[2].reshape(latents.shape),
        *done[3:9],
        *done[9:],
    )


def finish_kernel(*refs):
    ins, outs = refs[:9], refs[9:23]
    stage, casts = refs[23:32], refs[32:37]
    sem_in, sem_out = refs[37:]
    parts = ins[1].shape[0]

    def media(s, load):
        if load:
            return pltpu.make_async_copy(ins[1].at[s], stage[1].at[s], sem_in.at[9 + s])
        return pltpu.make_async_copy(stage[1].at[s], outs[1].at[s], sem_out.at[9 + s])

    loads = [pltpu.make_async_copy(ins[i], stage[i], sem_in.at[i]) for i in range(9) if i != 1]
    order = [7, 6, 3, 4, 5, 0, 1, 2]
    for s in range(parts // 2):
        media(s, True).start()
    for i in order[:2]:
        loads[i].start()
    for s in range(parts // 2, parts):
        media(s, True).start()
    for i in order[2:]:
        loads[i].start()
    for s in range(parts // 2):
        media(s, True).wait()
        media(s, False).start()
    stores = []

    def cast_one(i):
        loads[3 + i].wait()
        rows = stage[4 + i].shape[0]
        step = 32

        def cast(k, carry):
            block = pl.ds(pl.multiple_of(k * step, step), step)
            casts[i][block, :] = stage[4 + i][block, :].astype(F32)
            return carry

        lax.fori_loop(0, rows // step, cast, 0)
        copy = pltpu.make_async_copy(casts[i], outs[9 + i], sem_out.at[3 + i])
        copy.start()
        stores.append(copy)

    cast_one(4)
    cast_one(3)
    for s in range(parts // 2, parts):
        media(s, True).wait()
        media(s, False).start()
    for i in range(3):
        cast_one(i)
    for at, i in enumerate((0, 2)):
        loads[at].wait()
        copy = pltpu.make_async_copy(stage[i], outs[i], sem_out.at[i])
        copy.start()
        stores.append(copy)
    loads[2].wait()
    for i in range(6):
        outs[3 + i][...] = stage[3][i]
    for s in range(parts):
        media(s, False).wait()
    for copy in stores:
        copy.wait()


def finish(got):
    hbm = pl.BlockSpec(memory_space=pl.ANY)
    vmem = pl.BlockSpec(memory_space=pltpu.VMEM)
    shapes = [jax.ShapeDtypeStruct(x.shape, x.dtype) for x in got[:3]]
    shapes += [jax.ShapeDtypeStruct((got[3].shape[1],), F32)] * 6
    shapes += [jax.ShapeDtypeStruct(x.shape, F32) for x in got[4:]]
    return pl.pallas_call(
        finish_kernel,
        out_shape=shapes,
        in_specs=[hbm] * 9,
        out_specs=[hbm] * 3 + [vmem] * 6 + [hbm] * 5,
        scratch_shapes=[pltpu.VMEM(x.shape, x.dtype) for x in got]
        + [pltpu.VMEM(x.shape, F32) for x in got[4:]]
        + [DMA((9 + got[1].shape[0],))] * 2,
        compiler_params=pltpu.CompilerParams(vmem_limit_bytes=VMEM_BYTES),
        name="casts",
    )(*got)


def solution(mesh):
    rows4 = P(None, "dp", "lat", None)
    vec = P("dp")
    mat = P("dp", None)
    n_dp, n_lat = mesh.shape["dp"], mesh.shape["lat"]
    body = fused if (n_dp, n_lat) == (8, 4) else shards
    return jax.shard_map(
        functools.partial(body, n_dp, n_lat),
        mesh=mesh,
        in_specs=(rows4, rows4, P(None, "dp"), rows4) + (vec,) * 6 + (mat,) * 5,
        out_specs=(rows4,) * 3 + (vec,) * 6 + (mat,) * 5,
        check_vma=False,
    )
```

```python
import functools
import types

import jax
import jax.numpy as jnp
from jax import lax
from jax.experimental import pallas as pl
from jax.experimental.pallas import tpu as pltpu
from jax.sharding import PartitionSpec as P

HEADS = 8
HEAD = 64
VIS = 256
EPS = 1e-05
F32 = jnp.float32
B16 = jnp.bfloat16
MESH = pl.DeviceIdType.MESH
DMA = pltpu.SemaphoreType.DMA
VMEM_BYTES = 62 << 20


def exchange_kernel(axis, n, modes, *refs):
    count = len(modes)
    ins, outs = refs[:count], refs[count : 2 * count]
    send, recv, own = refs[2 * count :]
    me = lax.axis_index(axis)
    barrier = pltpu.get_barrier_semaphore()
    for k in range(1, n):
        pl.semaphore_signal(
            barrier, inc=1, device_id={axis: lax.rem(me + k, n)}, device_id_type=MESH
        )
    pl.semaphore_wait(barrier, n - 1)
    copies = []
    for k in range(1, n):
        peer = lax.rem(me + k, n)
        for i in range(count):
            source = ins[i] if modes[i] == "gather" else ins[i].at[peer]
            copy = pltpu.make_async_remote_copy(
                source,
                outs[i].at[me],
                send.at[i, k],
                recv.at[i, k],
                device_id={axis: peer},
                device_id_type=MESH,
            )
            copy.start()
            copies.append(copy)
    for i in range(count):
        source = ins[i] if modes[i] == "gather" else ins[i].at[me]
        copy = pltpu.make_async_copy(source, outs[i].at[me], own.at[i])
        copy.start()
        copies.append(copy)
    for copy in copies:
        copy.wait()


class Exchanges:
    def __init__(self, sizes):
        self.sizes = sizes
        self.used = 0

    def __call__(self, axis, arrays, modes):
        n = self.sizes[axis]
        count = len(arrays)
        outs = [
            jax.ShapeDtypeStruct(((n,) + a.shape) if m == "gather" else a.shape, a.dtype)
            for a, m in zip(arrays, modes)
        ]
        self.used += 1
        space = pl.BlockSpec(memory_space=pl.ANY)
        return pl.pallas_call(
            functools.partial(exchange_kernel, axis, n, modes),
            out_shape=outs,
            in_specs=[space] * count,
            out_specs=[space] * count,
            scratch_shapes=[DMA((count, n)), DMA((count, n)), DMA((count,))],
            compiler_params=pltpu.CompilerParams(collective_id=self.used, has_side_effects=True),
            name="exchange_%d" % self.used,
        )(*arrays)


def norm_parts(x):
    mean = jnp.mean(x, -1, keepdims=True)
    cent = x - mean
    factor = lax.rsqrt(jnp.mean(cent * cent, -1, keepdims=True) + EPS)
    return cent * factor, factor


def norm_back(grad, unit, factor, gain):
    scaled = grad * gain
    inner = jnp.mean(scaled * unit, -1, keepdims=True)
    d_input = factor * (scaled - jnp.mean(scaled, -1, keepdims=True) - unit * inner)
    return d_input, jnp.sum(grad * unit, 0), jnp.sum(grad, 0)


def mm(a, b):
    return lax.dot_general(a, b, (((1,), (0,)), ((), ())), preferred_element_type=F32)


def mm_nt(a, b):
    return lax.dot_general(a, b, (((1,), (1,)), ((), ())), preferred_element_type=F32)


def mm_tn(a, b):
    return lax.dot_general(a, b, (((0,), (0,)), ((), ())), preferred_element_type=F32)


def shards(n_dp, n_lat, media, latents, counts, cotangent, g_m, b_m, g_l, b_l, g_f, b_f, wq, wkv, wo, wup, wdown):
    ex = Exchanges({"dp": n_dp, "lat": n_lat})
    micro, per, rows, width = media.shape
    nq = latents.shape[2]
    S = micro * per
    inner = wq.shape[1]
    ff = wup.shape[1]
    ff_part = ff // n_dp
    d_part = width // n_dp
    lat_at = lax.axis_index("lat")
    med = media.reshape(S * rows, width)
    lat = latents.reshape(S * nq, width).astype(F32)
    cot = cotangent.reshape(S * nq, width)
    count = counts.reshape(S)

    small = jnp.stack([g_m, b_m, g_l, b_l, g_f, b_f], 0)
    small_all, wq_all, wkv_all, wo_all = ex("dp", [small, wq, wkv, wo], ["gather"] * 4)
    params = jnp.transpose(small_all, (1, 0, 2)).reshape(6, width).astype(F32)
    wq_all = wq_all.reshape(width, inner)
    wkv_all = wkv_all.reshape(width, 2 * inner)
    wo_all = wo_all.reshape(inner, width)
    wup_cols = jnp.transpose(wup.reshape(d_part, n_dp, ff_part), (1, 0, 2))
    cot_all, wup_s = ex("dp", [cot, wup_cols], ["gather", "swap"])
    cot_all = cot_all.reshape(-1, width)
    wup_s = wup_s.reshape(width, ff_part)

    med_unit, med_factor = norm_parts(med.astype(F32))
    med_norm = (med_unit * params[0] + params[1]).astype(B16)
    lat_unit, lat_factor = norm_parts(lat)
    lat_norm = (lat_unit * params[2] + params[3]).astype(B16)
    query = (mm(lat_norm, wq_all) * 0.125).astype(B16)
    (query_all,) = ex("lat", [query], ["gather"])
    kv_med = mm(med_norm, wkv_all).astype(B16)
    kv_lat = mm(lat_norm, wkv_all).astype(B16)
    keyval = jnp.concatenate(
        [kv_med.reshape(S, rows, 2 * inner), kv_lat.reshape(S, nq, 2 * inner)], 1
    )
    kc = rows + nq
    keys = keyval[:, :, :inner].reshape(S, kc, HEADS, HEAD)
    values = keyval[:, :, inner:].reshape(S, kc, HEADS, HEAD)
    heads_q = query_all.reshape(n_lat, S, nq, HEADS, HEAD)
    slot = (lat_at * rows + lax.iota(jnp.int32, rows)) // VIS
    live = jnp.concatenate(
        [slot[None, :] < count[:, None], jnp.ones((S, nq), dtype=bool)], 1
    )
    score = jnp.einsum("zsqhd,skhd->shzqk", heads_q, keys, preferred_element_type=F32)
    score = jnp.where(live[:, None, None, None, :], score, -1e30)
    top = jnp.max(score, -1)
    p = jnp.exp(score - top[..., None])
    total = jnp.sum(p, -1)
    part = jnp.einsum("shzqk,skhd->zsqhd", p.astype(B16), values, preferred_element_type=F32)
    scale = jnp.transpose(1.0 / total, (2, 0, 3, 1))[..., None]
    part = (part * scale).astype(B16).reshape(n_lat, S * nq, inner)
    stats = jnp.stack([top, total], 0).reshape(2 * S * HEADS, n_lat * nq)
    part_all, stats_all = ex("lat", [part, stats], ["swap", "gather"])
    stats_all = stats_all.reshape(n_lat, 2, S, HEADS, n_lat, nq)
    tops, totals = stats_all[:, 0], stats_all[:, 1]
    top_max = jnp.max(tops, 0)
    weight = totals * jnp.exp(tops - top_max)
    whole = jnp.sum(weight, 0)
    lse = top_max + jnp.log(whole)
    weight = lax.dynamic_index_in_dim(weight / whole, lat_at, 3, keepdims=False)
    weight = jnp.transpose(weight, (0, 1, 3, 2)).reshape(n_lat, S * nq, HEADS, 1)
    attended_f = jnp.sum(part_all.reshape(n_lat, S * nq, HEADS, HEAD).astype(F32) * weight, 0)
    attended = attended_f.reshape(S * nq, inner).astype(B16)

    hidden = lat + mm(attended, wo_all)
    ffn_unit, ffn_factor = norm_parts(hidden)
    ff_norm = (ffn_unit * params[4] + params[5]).astype(B16)
    (ffn_all,) = ex("dp", [ff_norm], ["gather"])
    ffn_all = ffn_all.reshape(-1, width)
    up = mm(ffn_all, wup_s)
    act_f, pull = jax.vjp(lambda v: jax.nn.gelu(v, approximate=False), up)
    act = act_f.astype(B16)
    d_act = mm_nt(cot_all, wdown)
    d_up = pull(d_act)[0].astype(B16)
    out_part = mm(act, wdown).astype(B16).reshape(n_dp, S * nq, width)
    d_ffn_part = mm_nt(d_up, wup_s).astype(B16).reshape(n_dp, S * nq, width)
    d_ffn_all, out_all = ex("dp", [d_ffn_part, out_part], ["swap", "swap"])
    latents_out = (hidden + jnp.sum(out_all.astype(F32), 0)).astype(B16)
    d_ffn = jnp.sum(d_ffn_all.astype(F32), 0)
    grad_down = mm_tn(act, cot_all)
    grad_up = mm_tn(ffn_all, d_up)
    d_h, grad_gf, grad_bf = norm_back(d_ffn, ffn_unit, ffn_factor, params[4])
    d_hidden = cot.astype(F32) + d_h
    d_attn = d_hidden.astype(B16)
    grad_out = mm_tn(attended, d_attn)
    d_att = mm_nt(d_attn, wo_all).astype(B16)
    delta = jnp.sum(
        (d_att.astype(F32) * attended_f.reshape(S * nq, inner)).reshape(S * nq, HEADS, HEAD), -1
    )
    d_att_all, delta_all = ex("lat", [d_att, delta.T], ["gather", "gather"])
    d_att_h = d_att_all.reshape(n_lat, S, nq, HEADS, HEAD)
    delta_h = jnp.transpose(delta_all.reshape(n_lat, HEADS, S, nq), (2, 1, 0, 3))[..., None]
    prob = jnp.exp(score - lse[..., None])
    d_prob = jnp.einsum("zsqhd,skhd->shzqk", d_att_h, values, preferred_element_type=F32)
    d_score = (prob * (d_prob - delta_h)).astype(B16)
    dq_part = jnp.einsum("shzqk,skhd->zsqhd", d_score, keys, preferred_element_type=F32)
    (dq_all,) = ex("lat", [dq_part.astype(B16).reshape(n_lat, S * nq, inner)], ["swap"])
    d_keys = jnp.einsum("shzqk,zsqhd->skhd", d_score, heads_q, preferred_element_type=F32)
    d_values = jnp.einsum(
        "shzqk,zsqhd->skhd", prob.astype(B16), d_att_h, preferred_element_type=F32
    )
    d_kv = jnp.concatenate(
        [d_keys.reshape(S, kc, inner), d_values.reshape(S, kc, inner)], -1
    ).astype(B16)
    d_kv_med = d_kv[:, :rows].reshape(S * rows, 2 * inner)
    d_kv_lat = d_kv[:, rows:].reshape(S * nq, 2 * inner)
    grad_kv = mm_tn(med_norm, d_kv_med) + mm_tn(lat_norm, d_kv_lat)
    d_mnorm = mm_nt(d_kv_med, wkv_all)
    d_media, grad_gm, grad_bm = norm_back(d_mnorm, med_unit, med_factor, params[0])
    dq = (jnp.sum(dq_all.astype(F32), 0) * 0.125).astype(B16)
    grad_q = mm_tn(lat_norm, dq)
    d_lnorm = mm_nt(dq, wq_all) + mm_nt(d_kv_lat, wkv_all)
    d_latn, grad_gl, grad_bl = norm_back(d_lnorm, lat_unit, lat_factor, params[2])
    latent_grad = (d_hidden + d_latn).astype(B16)

    smalls = jnp.stack([grad_gm, grad_bm, grad_gl, grad_bl, grad_gf, grad_bf], 0)
    smalls = jnp.transpose(smalls.reshape(6, n_dp, d_part), (1, 0, 2))
    small_s, q_s, kv_s, o_s, up_s = ex(
        "dp",
        [
            smalls,
            grad_q.astype(B16).reshape(n_dp, d_part, inner),
            grad_kv.astype(B16).reshape(n_dp, d_part, 2 * inner),
            grad_out.astype(B16).reshape(n_dp, inner // n_dp, width),
            grad_up.astype(B16).reshape(n_dp, d_part, ff_part),
        ],
        ["swap"] * 5,
    )
    small_s = jnp.sum(small_s, 0)
    q_s = jnp.sum(q_s.astype(F32), 0)
    kv_s = jnp.sum(kv_s.astype(F32), 0)
    o_s = jnp.sum(o_s.astype(F32), 0)
    up_s = jnp.transpose(up_s, (1, 0, 2)).reshape(d_part, ff)
    pieces = [q_s, kv_s, o_s, up_s, grad_down]
    cut = [x.astype(B16).reshape(n_lat, x.shape[0] // n_lat, x.shape[1]) for x in pieces]
    got = ex("lat", cut + [small_s], ["swap"] * 5 + ["gather"])
    small_s = jnp.sum(got[5], 0)
    summed = [jnp.sum(x.astype(F32), 0).astype(B16) for x in got[:5]]
    full = ex("lat", summed, ["gather"] * 5)
    grads = [x.reshape(y.shape).astype(F32) for x, y in zip(full, pieces)]
    return (
        latents_out.reshape(latents.shape),
        d_media.astype(B16).reshape(media.shape),
        latent_grad.reshape(latents.shape),
        *[small_s[i] for i in range(6)],
        *grads,
    )


ROWS_STEP = 160
NORMS = (3, 6)
UP_EARLY = 4
HOP1, HOP2 = 2, 4
HOPS_DEXT = (0, 1)
HOPS_MID = (2,)
HOPS_ATT = ()
HOPS_KV = ((1, 3), (3, 4))
HOPS_Q = (5, 6)
HOPS_MED = ((1, 7), (4, 8), (6, 9))
MED_SPLIT = 4
HOP_END = 10

NT, NN, TN = (((1,), (1,)), ((), ())), (((1,), (0,)), ((), ())), (((0,), (0,)), ((), ()))


def dot(a, b, form):
    return lax.dot_general(a, b, form, preferred_element_type=F32)


def centred(x):
    mean = jnp.mean(x, -1, keepdims=True)
    cent = x - mean
    factor = lax.rsqrt(jnp.mean(cent * cent, -1, keepdims=True) + EPS)
    return cent * factor, factor


def back(grad, unit, factor, gain):
    scaled = grad * gain
    inner = jnp.mean(scaled * unit, -1, keepdims=True)
    return factor * (scaled - jnp.mean(scaled, -1, keepdims=True) - unit * inner)


def fused_kernel(geo, refs):
    S, R, Q, D, I, NC, NZ = geo
    KR = R + Q
    B = S * Q
    G = 2
    W = I // G
    HG = HEADS // G
    r = refs
    me = lax.axis_index("dp")
    z = lax.axis_index("lat")
    chip = me // 2
    core = lax.rem(me, 2)
    sib = me + 1 - 2 * core
    other = 1 - core

    def chip_to(k):
        return lax.rem(chip + k, NC)

    def chip_from(k):
        return lax.rem(chip + NC - k, NC)

    def z_to(k):
        return lax.rem(z + k, NZ)

    def z_from(k):
        return lax.rem(z + NZ - k, NZ)

    quads = range(1, NC)
    planes = range(1, NZ)
    used = [0, 0]

    def local(src, dst):
        sem = r.lsem.at[used[0]]
        used[0] += 1
        copy = pltpu.make_async_copy(src, dst, sem)
        copy.start()
        return copy

    def remote(src, dst, **where):
        at = used[1]
        used[1] += 1
        copy = pltpu.make_async_remote_copy(
            src, dst, r.ssem.at[at], r.rsem.at[at], device_id=where, device_id_type=MESH
        )
        copy.start()
        return copy

    class Planned:
        def __init__(self, make):
            at = used[1]
            used[1] += 1

            def build():
                src, dst, where = make()
                return pltpu.make_async_remote_copy(
                    src, dst, r.ssem.at[at], r.rsem.at[at], device_id=where, device_id_type=MESH
                )

            self.build = build

        def start(self):
            self.build().start()

        def wait(self):
            self.build().wait()

        def wait_send(self):
            self.build().wait_send()

        def wait_recv(self):
            self.build().wait_recv()

    class Spread:
        def __init__(self, src_for, dst_at):
            self.dst_at = dst_at
            self.far = [remote(src_for(chip_to(k)), dst_at(me), dp=2 * chip_to(k) + core) for k in quads]
            self.near = remote(src_for(chip), dst_at(me), dp=sib)
            self.own = local(src_for(chip), dst_at(me))

        def forward(self):
            self.passed = []
            for k in quads:
                self.far[k - 1].wait_recv()
                slot = self.dst_at(2 * chip_from(k) + core)
                self.passed.append(remote(slot, slot, dp=sib))

        def finish(self):
            self.own.wait()
            self.near.wait()
            for copy in self.far:
                copy.wait_send()
            for copy in self.passed:
                copy.wait()

    side = chip + 1 - 2 * lax.rem(chip, 2)
    ahead = chip + 2 - 4 * (chip // 2)
    cross = 3 - chip

    class Relay(Spread):
        def __init__(self, src_for, dst_at):
            self.dst_at = dst_at
            self.own = local(src_for(chip), dst_at(me))
            self.far = [remote(src_for(t), dst_at(me), dp=2 * t + core) for t in (side, ahead)]
            self.near = remote(src_for(chip), dst_at(me), dp=sib)
            self.half = dst_at(me).shape[0] // 2

        def forward(self):
            self.passed = []
            h = self.half
            for k, (source, target, at) in enumerate(((side, ahead, 0), (ahead, side, h))):
                self.far[k].wait_recv()
                slot = self.dst_at(2 * source + core)
                part = slot.at[at : at + h]
                self.passed.append(remote(part, part, dp=2 * target + core))
                self.passed.append(remote(slot, slot, dp=sib))

        def forward2(self):
            h = self.half
            self.late = []
            slot = self.dst_at(2 * cross + core)
            for k, at in ((0, 0), (2, h)):
                self.passed[k].wait_recv()
                part = slot.at[at : at + h]
                self.late.append(remote(part, part, dp=sib))

        def finish(self):
            self.own.wait()
            self.near.wait()
            for copy in self.far:
                copy.wait_send()
            for k in (0, 2):
                self.passed[k].wait_send()
            for copy in (self.passed[1], self.passed[3], *self.late):
                copy.wait()

    def to_quad(src_for, dst):
        return [remote(src_for(chip_to(k)), dst, dp=2 * chip_to(k) + core) for k in quads]

    def to_planes(src_for, dst):
        return [remote(src_for(z_to(k)), dst, lat=z_to(k)) for k in planes]

    def wait_all(copies):
        for copy in copies:
            copy.wait()

    class Meet:
        def __init__(self, own, got, cross, out, root):
            self.own, self.got, self.crossed, self.out, self.root = own, got, cross, out, root
            peer = 3 - root
            self.up = Planned(lambda: (own, got, {"lat": 1 + z // 2}))
            self.over = Planned(lambda: (own, cross, {"lat": root}))
            self.near = Planned(lambda: (own, out, {"lat": 3 * (root - 1)}))
            self.back = Planned(lambda: (own, out, {"lat": peer}))
            self.far = Planned(lambda: (out, out, {"lat": 3 * (peer - 1)}))
            self.lsem = r.lsem.at[used[0]]
            used[0] += 1

        def send(self):
            @pl.when(jnp.logical_or(z == 0, z == NZ - 1))
            def _():
                self.up.start()

        def merge(self):
            @pl.when(z == 3 - self.root)
            def _():
                self.up.wait_recv()
                self.own[...] = (self.own[...].astype(F32) + self.got[...].astype(F32)).astype(B16)
                self.over.start()

        def total(self):
            @pl.when(z == self.root)
            def _():
                self.up.wait_recv()
                both = self.own[...].astype(F32) + self.got[...].astype(F32)
                self.over.wait_recv()
                self.own[...] = (both + self.crossed[...].astype(F32)).astype(B16)
                self.near.start()
                self.back.start()
                pltpu.make_async_copy(self.own, self.out, self.lsem).start()

        def relay(self):
            @pl.when(z == 3 - self.root)
            def _():
                self.back.wait_recv()
                self.far.start()

        def finish(self):
            root, peer = self.root, 3 - self.root

            @pl.when(jnp.logical_or(z == 0, z == NZ - 1))
            def _():
                self.up.wait_send()

            @pl.when(z == 3 * (root - 1))
            def _():
                self.near.wait_recv()

            @pl.when(z == 3 * (peer - 1))
            def _():
                self.far.wait_recv()

            @pl.when(z == peer)
            def _():
                self.over.wait_send()
                self.far.wait_send()

            @pl.when(z == root)
            def _():
                self.near.wait_send()
                self.back.wait_send()
                pltpu.make_async_copy(self.own, self.out, self.lsem).wait()

    barrier = pltpu.get_barrier_semaphore()
    for k in quads:
        pl.semaphore_signal(barrier, inc=1, device_id={"dp": 2 * chip_to(k) + core}, device_id_type=MESH)
    pl.semaphore_signal(barrier, inc=1, device_id={"dp": sib}, device_id_type=MESH)
    for k in planes:
        pl.semaphore_signal(barrier, inc=1, device_id={"lat": z_to(k)}, device_id_type=MESH)
    pl.semaphore_wait(barrier, NC - 1 + 1 + NZ - 1)

    def whole(ref):
        return lambda _: ref

    def rows_at(ref):
        return lambda d: ref.at[d]

    def cols_at(ref, at, size):
        return lambda d: ref.at[d, :, at : at + size]

    part_rows = D // (2 * NC)
    per_slot = NC

    def up_at(d):
        at = pl.multiple_of(lax.rem(d, per_slot) * part_rows, part_rows)
        return r.ffw.at[2 + d // per_slot, pl.ds(at, part_rows)]

    span = r.wup.shape[1] // NC

    def down_matrix():
        return r.ffw[0:2].reshape(span, D)

    def up_matrix():
        return r.ffw[2:4].reshape(D, span)

    g_small = Spread(whole(r.small), rows_at(r.small_all))
    g_wq = Spread(whole(r.wq), rows_at(r.wq_all))
    lat_in = local(r.lat, r.lat_v)
    cot_in = local(r.cot, r.cot4.at[chip])
    slots = r.med.shape[0]

    def med_copy(s):
        slot = lax.rem(s, slots)
        return pltpu.make_async_copy(r.media.at[s], r.med.at[slot], r.dsem.at[slot])

    def med_first():
        for s in range(slots):
            med_copy(jnp.int32(s)).start()

    def med_next(s):
        @pl.when(s + slots < S)
        def _():
            med_copy(s + slots).start()

    med_first()
    g_small.forward()
    g_small.finish()
    params = r.params
    for d in range(2 * NC):
        params[0:6, d * part_rows : (d + 1) * part_rows] = r.small_all[d].astype(F32)

    def param(i):
        return params[i : i + 1, :]

    lat_in.wait()
    unit, _ = centred(r.lat_v[...].astype(F32))
    r.latn[...] = (unit * param(2) + param(3)).astype(B16)
    rb = ROWS_STEP

    def norm_sample(s, carry):
        slot = lax.rem(s, slots)
        med_copy(s).wait()

        def part(i, inner):
            x = r.med[slot, pl.ds(pl.multiple_of(i * rb, rb), rb), :].astype(F32)
            u, _ = centred(x)
            row = pl.multiple_of(s * KR + i * rb, 16)
            r.X[pl.ds(row, rb), :] = (u * param(0) + param(1)).astype(B16)
            return inner

        lax.fori_loop(0, R // rb, part, 0)
        row = pl.multiple_of(s * KR + R, 16)
        at = pl.multiple_of(s * Q, 16)
        r.X[pl.ds(row, Q), :] = r.latn[pl.ds(at, Q), :]
        med_next(s)
        return carry

    def up_slice(k):
        return r.wup.at[:, pl.ds(pl.multiple_of(k * span, 128), span)]

    def key_cols(s, carry):
        rows = pl.ds(pl.multiple_of(s * KR, 16), KR)
        r.KV[rows, 0:I] = dot(r.X[rows, :], r.wkv_all[:, :, 0:I].reshape(D, I), NN).astype(B16)
        return carry

    def value_cols(s, carry):
        rows = pl.ds(pl.multiple_of(s * KR, 16), KR)
        r.KV[rows, I : 2 * I] = dot(r.X[rows, :], r.wkv_all[:, :, I : 2 * I].reshape(D, I), NN).astype(B16)
        return carry

    first, second = NORMS
    lax.fori_loop(0, first, norm_sample, 0)
    g_key = Relay(lambda _: r.wkv.at[:, 0:I], cols_at(r.wkv_all, 0, I))
    g_wq.forward()
    g_val = Relay(lambda _: r.wkv.at[:, I : 2 * I], cols_at(r.wkv_all, I, I))
    g_wq.finish()
    query = dot(r.latn[...], r.wq_all[...].reshape(D, I), NN) * 0.125
    r.q_all[z] = query.astype(B16).reshape(S, Q, I)
    q_out = to_planes(lambda _: r.q_all.at[z], r.q_all.at[z])
    lax.fori_loop(first, second, norm_sample, 0)
    g_key.forward()
    g_wo = Relay(whole(r.wo), rows_at(r.wo_all))
    lax.fori_loop(second, S, norm_sample, 0)
    med_first()
    g_key.forward2()
    g_val.forward()
    g_up = Spread(up_slice, up_at)
    g_key.finish()
    lax.fori_loop(0, S, key_cols, 0)
    g_val.forward2()
    g_wo.forward()
    g_down = remote(r.wdown, r.ffw.at[core], dp=sib)
    g_down_own = local(r.wdown, r.ffw.at[core])
    g_val.finish()
    lax.fori_loop(0, S, value_cols, 0)
    g_wo.forward2()
    cot_in.wait()
    g_cot = to_quad(lambda _: r.cot, r.cot4.at[chip])
    wait_all(q_out)

    own_head = (
        lax.broadcasted_iota(jnp.int32, (HG * NZ * Q, W), 0) // (NZ * Q)
        == lax.broadcasted_iota(jnp.int32, (HG * NZ * Q, W), 1) // HEAD
    )
    r.mask[...] = own_head.astype(F32).astype(B16)

    def spread_heads(x):
        return jnp.concatenate([x] * HG, 0) * r.mask[...]

    def take_heads(x):
        low = lax.broadcasted_iota(jnp.int32, (NZ * Q, 2 * HEAD), 1) < HEAD
        cols = []
        for pair in range(HG // 2):
            block = x[:, pair * 2 * HEAD : (pair + 1) * 2 * HEAD]
            n = NZ * Q
            cols.append(
                jnp.where(low, block[2 * pair * n : (2 * pair + 1) * n], block[(2 * pair + 1) * n : (2 * pair + 2) * n])
            )
        return jnp.concatenate(cols, 1)

    def scores(s, g, qbig):
        rows = pl.ds(pl.multiple_of(s * KR, 16), KR)
        raw = dot(r.KV[rows, g * W : (g + 1) * W], qbig, NT)
        row = lax.broadcasted_iota(jnp.int32, raw.shape, 0)
        live = jnp.logical_or(row >= R, row + z * R < r.counts[s // r.counts.shape[1], lax.rem(s, r.counts.shape[1])] * VIS)
        return jnp.where(live, raw, -1e30)

    def queries(s, g):
        return spread_heads(r.q_all[:, s, :, g * W : (g + 1) * W].reshape(NZ * Q, W))

    def attend(s, carry):
        rows = pl.ds(pl.multiple_of(s * KR, 16), KR)
        for g in range(G):
            score = scores(s, g, queries(s, g))
            top = jnp.max(score, 0, keepdims=True)
            grown = jnp.exp(score - top)
            total = jnp.sum(grown, 0, keepdims=True)
            r.lse[z, pl.ds(g * S + s, 1), :] = top + jnp.log(total)
            prob = (grown * (1.0 / total)).astype(B16)
            part = dot(prob, r.KV[rows, I + g * W : I + (g + 1) * W], TN)
            r.o_send[:, s, :, g * W : (g + 1) * W] = take_heads(part).astype(B16).reshape(NZ, Q, W)

        @pl.when(s == S // 2)
        def _():
            for copy in o_out[: NZ - 1]:
                copy.start()

        return carry

    def half(n):
        return slice(n * (S // 2), (n + 1) * (S // 2))

    def plan(make):
        return [Planned(functools.partial(make, k, n)) for n in range(2) for k in planes]

    o_out = plan(lambda k, n: (r.o_send.at[z_to(k), half(n)], r.o_recv.at[z, half(n)], {"lat": z_to(k)}))
    lax.fori_loop(0, S, attend, 0)
    lse_out = to_planes(lambda _: r.lse.at[z], r.lse.at[z])
    for copy in o_out[NZ - 1 :]:
        copy.start()
    wait_all(lse_out)
    every = r.lse[...]
    top = jnp.max(every, 0)
    lse_all = top + jnp.log(jnp.sum(jnp.exp(every - top[None]), 0))
    r.lse_all[...] = lse_all
    r.lse[...] = jnp.exp(every - lse_all[None])
    pick = (
        lax.rem(lax.broadcasted_iota(jnp.int32, (B, HG * NZ * Q), 1), NZ * Q)
        == lax.rem(lax.broadcasted_iota(jnp.int32, (B, HG * NZ * Q), 0), Q) + z * Q
    )
    for k in range(NZ):
        store = r.hidden if k < 2 else r.d_hidden
        for g in range(G):
            lanes = jnp.broadcast_to(
                r.lse[z_from(k), g * S : (g + 1) * S, :][:, None, :], (S, Q, HG * NZ * Q)
            ).reshape(B, HG * NZ * Q)
            lanes = jnp.where(pick, lanes, 0.0)
            coarse = lanes.astype(B16)
            fine = (lanes - coarse.astype(F32)).astype(B16)
            at = (k % 2) * I + g * W
            store[:, at : at + W] = dot(coarse, r.mask[...], NN) + dot(fine, r.mask[...], NN)
    g_up.forward()
    g_wo.finish()
    wait_all(o_out)
    att = r.hidden[:, 0:I] * r.o_send[z].astype(F32).reshape(B, I)
    for k in planes:
        store = r.hidden if k < 2 else r.d_hidden
        at = (k % 2) * I
        att = att + store[:, at : at + I] * r.o_recv[z_from(k)].astype(F32).reshape(B, I)
    r.att_f[...] = att
    r.att[...] = att.astype(B16)
    hidden = r.lat_v[...].astype(F32) + dot(r.att[...], r.wo_all[...].reshape(I, D), NN)
    r.hidden[...] = hidden
    unit, _ = centred(hidden)
    r.ffn4[chip] = (unit * param(4) + param(5)).astype(B16)
    f_out = to_quad(lambda _: r.ffn4.at[chip], r.ffn4.at[chip])

    def act_grad(b, carry):
        r.d_act[b] = dot(r.cot4[b], down_matrix(), NT)
        return carry

    wait_all(g_cot)
    g_down.wait()
    g_down_own.wait()
    g_up.finish()
    lax.fori_loop(0, NC, act_grad, 0)

    def feed(b):
        r.up[...] = dot(r.ffn4[b], up_matrix(), NN)

        def gelu_part(i, carry):
            rows = pl.ds(pl.multiple_of(i * 32, 32), 32)
            x = r.up[rows, :]
            cdf = 0.5 * (1.0 + lax.erf(x * 0.7071067811865476))
            pdf = jnp.exp(-0.5 * x * x) * 0.3989422804014327
            r.act[b, rows, :] = (x * cdf).astype(B16)
            r.d_up[b, rows, :] = (r.d_act[b, rows, :] * (cdf + x * pdf)).astype(B16)
            return carry

        lax.fori_loop(0, B // 32, gelu_part, 0)
        r.df_send[b] = dot(r.d_up[b], up_matrix(), NT).astype(B16)

    feed(chip)
    df_out = []
    for k in quads:
        f_out[k - 1].wait_recv()
        b = chip_from(k)
        feed(b)
        df_out.append(remote(r.df_send.at[b], r.df_recv.at[chip], dp=2 * b + core))

    own_span = span // 2
    act2 = r.act

    def grad_down(i, carry):
        at = pl.multiple_of(i * 256, 256)
        value = dot(
            act2[:, :, pl.ds(at, 256)].reshape(NC * B, 256), r.cot4[...].reshape(NC * B, D), TN
        )
        r.gd[i // (own_span // 256), pl.ds(pl.multiple_of(lax.rem(i * 256, own_span), 256), 256), :] = value.astype(B16)
        return carry

    lax.fori_loop(0, span // 256, grad_down, 0)
    gd_out = remote(r.gd.at[other], r.gd_recv, dp=sib)
    dw = D // NC
    hw = dw // 2

    def grad_up(i, carry):
        at = pl.multiple_of(i * dw, dw)
        value = dot(
            r.ffn4[:, :, pl.ds(at, dw)].reshape(NC * B, dw), r.d_up[...].reshape(NC * B, span), TN
        ).astype(B16)
        r.gu[0, i] = value[:hw]
        r.gu[1, i] = value[hw:]
        return carry

    lax.fori_loop(0, NC, grad_up, 0)
    gu_out = remote(r.gu.at[other], r.gu_recv, dp=sib)

    def down(i, carry):
        r.out_send[i] = dot(r.act[i], down_matrix(), NN).astype(B16)
        return carry

    lax.fori_loop(0, NC, down, 0)
    piece = own_span // NZ
    gd_out.wait()
    for j in range(NZ):
        rows = slice(j * piece, (j + 1) * piece)
        r.gd_sum[j] = (r.gd[core, rows, :].astype(F32) + r.gd_recv[rows, :].astype(F32)).astype(B16)

    meets = [
        Meet(r.gd_sum.at[j], r.z_got.at[j], r.z_cross.at[j // 2], r.gdown.at[j * piece : (j + 1) * piece, :], 1 + j % 2)
        for j in range(NZ)
    ]
    meets += [
        Meet(r.gu_quad.at[j], r.z_got.at[NZ + j], r.z_cross.at[(NZ + j) // 2], r.gup.at[:, j * span : (j + 1) * span], 1 + j % 2)
        for j in range(NC)
    ]
    for part_, got_, cross_, out_ in (
        (r.go_t, r.go_got, r.go_cross, r.gout),
        (r.gk_t, r.gk_got, r.gk_cross, r.gkv),
        (r.gq_t, r.gq_got, r.gq_cross, r.gquery),
    ):
        rows = part_.shape[1]
        meets += [
            Meet(part_.at[j], got_.at[j], cross_, out_.at[j * rows : (j + 1) * rows, :], 1 + j) for j in range(2)
        ]

    def hop(n):
        if 0 <= n < len(meets):
            meets[n].merge()
        if 0 <= n - HOP1 < len(meets):
            meets[n - HOP1].total()
        if 0 <= n - HOP2 < len(meets):
            meets[n - HOP2].relay()

    for n in range(UP_EARLY):
        meets[n].send()
    gu_out.wait()

    for copy in f_out:
        copy.wait_send()
    wait_all(df_out)
    d_ffn = r.df_send[chip].astype(F32)
    for k in quads:
        d_ffn = d_ffn + r.df_recv[chip_to(k)].astype(F32)
    unit, factor = centred(r.hidden[...])
    sums = r.sums
    sums[4:5, :] = jnp.sum(d_ffn * unit, 0, keepdims=True)
    sums[5:6, :] = jnp.sum(d_ffn, 0, keepdims=True)
    d_hidden = r.cot4[chip].astype(F32) + back(d_ffn, unit, factor, param(4))
    r.d_hidden[...] = d_hidden
    r.d_attn[...] = d_hidden.astype(B16)
    d_att = dot(r.d_attn[...], r.wo_all[...].reshape(I, D), NT).astype(B16)
    weighed = d_att.astype(F32) * r.att_f[...]
    lane = lax.broadcasted_iota(jnp.int32, (B, 128), 1)
    delta = jnp.zeros((B, 128), F32)
    low_lane = lax.broadcasted_iota(jnp.int32, (B, 128), 1) < HEAD
    for h in range(HEADS):
        block = weighed[:, (h // 2) * 128 : (h // 2) * 128 + 128]
        keep = low_lane if h % 2 == 0 else jnp.logical_not(low_lane)
        one = jnp.sum(jnp.where(keep, block, 0.0), -1, keepdims=True)
        delta = jnp.where(jnp.logical_or(lane == h, lane == HEADS + h), -one, delta)
    coarse = delta.astype(B16).astype(F32)
    ext = jnp.where(lane < HEADS, coarse, delta - coarse).astype(B16)
    r.d_ext[z, :, :, 0:I] = d_att.reshape(S, Q, I)
    r.d_ext[z, :, :, I : I + 128] = ext.reshape(S, Q, 128)
    d_out = plan(lambda k, n: (r.d_ext.at[z, half(n)], r.d_ext.at[z, half(n)], {"lat": z_to(k)}))
    for copy in d_out:
        copy.start()

    ow = I // NC
    oh = ow // 2
    for i in range(NC):
        value = dot(r.att[:, i * ow : (i + 1) * ow], r.d_attn[...], TN).astype(B16)
        r.go[0, i] = value[:oh]
        r.go[1, i] = value[oh:]
    go_out = remote(r.go.at[other], r.go_recv, dp=sib)

    def add_pair(dst, a, b, n):
        def body(i, carry):
            dst[i] = (a[i].astype(F32) + b[i].astype(F32)).astype(B16)
            return carry

        lax.fori_loop(0, n, body, 0)

    add_pair(r.gu_sum, r.gu.at[core], r.gu_recv, NC)
    guq_out = to_quad(lambda k: r.gu_sum.at[k], r.gu_quad.at[chip])
    for n in range(UP_EARLY, NZ):
        meets[n].send()

    def prob_at(s, g):
        lanes = pl.ds(pl.multiple_of(lax.rem(s, 2) * I + g * W, W), W)
        return r.ffw.at[s // 2, 0:KR, lanes]

    def probs(s, carry):
        for g in range(G):
            score = scores(s, g, queries(s, g))
            prob_at(s, g)[...] = jnp.exp(score - r.lse_all[pl.ds(g * S + s, 1), :]).astype(B16)
        return carry

    lax.fori_loop(0, S, probs, 0)
    go_out.wait()
    add_pair(r.go_sum, r.go.at[core], r.go_recv, NC)

    def quad_total(own, got):
        total = own[chip].astype(F32)
        for k in quads:
            total = total + got[chip_to(k)].astype(F32)
        return total

    def split_total(dst, own, got):
        total = quad_total(own, got).astype(B16)
        rows = total.shape[0] // 2
        for j in range(2):
            dst[j] = total[j * rows : (j + 1) * rows]

    for n in HOPS_DEXT:
        hop(n)
    wait_all(d_out[: NZ - 1])

    ones = jnp.ones((KR, 128), B16)
    lane_e = lax.broadcasted_iota(jnp.int32, (HG * NZ * Q, 128), 1)
    head_e = lax.broadcasted_iota(jnp.int32, (HG * NZ * Q, 128), 0) // (NZ * Q)
    for g in range(G):
        r.mask_e[g] = (
            jnp.logical_or(lane_e == head_e + g * HG, lane_e == head_e + g * HG + HEADS).astype(F32).astype(B16)
        )

    dq_out = plan(lambda k, n: (r.dq_send.at[z_to(k), half(n)], r.dq_recv.at[z, half(n)], {"lat": z_to(k)}))

    def attend_back(s, carry):
        rows = pl.ds(pl.multiple_of(s * KR, 16), KR)

        for g in range(G):
            qbig = queries(s, g)
            prob = prob_at(s, g)[...]
            dbig = spread_heads(r.d_ext[:, s, :, g * W : (g + 1) * W].reshape(NZ * Q, W))
            minus = r.d_ext[:, s, :, I : I + 128].reshape(NZ * Q, 128)
            minus = jnp.concatenate([minus] * HG, 0) * r.mask_e[g]
            d_prob = dot(r.KV[rows, I + g * W : I + (g + 1) * W], dbig, NT) + dot(ones, minus, NT)
            d_score = (prob.astype(F32) * d_prob).astype(B16)
            dq = dot(d_score, r.KV[rows, g * W : (g + 1) * W], TN)
            r.dq_send[:, s, :, g * W : (g + 1) * W] = take_heads(dq).astype(B16).reshape(NZ, Q, W)
            r.KV[rows, g * W : (g + 1) * W] = dot(d_score, qbig, NN).astype(B16)
            r.KV[rows, I + g * W : I + (g + 1) * W] = dot(prob, dbig, NN).astype(B16)
        return carry

    lax.fori_loop(0, S // 2, attend_back, 0)
    for copy in dq_out[: NZ - 1]:
        copy.start()
    goq_out = to_quad(lambda k: r.go_sum.at[k], r.go_quad.at[chip])
    out_out = to_quad(lambda k: r.out_send.at[k], r.out_recv.at[chip])
    for n in HOPS_MID:
        hop(n)
    wait_all(d_out[NZ - 1 :])
    lax.fori_loop(S // 2, S, attend_back, 0)
    for copy in dq_out[NZ - 1 :]:
        copy.start()
    wait_all(guq_out)
    r.gu_quad[chip] = r.gu_sum[chip]
    for n in range(NZ, NZ + NC):
        meets[n].send()
    for n in HOPS_ATT:
        hop(n)

    def kv_chip(i):
        return lax.rem(chip + 1 + i, NC)

    def kv_pair(i):
        return pltpu.make_async_remote_copy(
            r.gk.at[other, kv_chip(i)],
            r.gk_recv.at[kv_chip(i)],
            r.ksem.at[0, i],
            r.ksem.at[1, i],
            device_id={"dp": sib},
            device_id_type=MESH,
        )

    def kv_quad(i):
        return pltpu.make_async_remote_copy(
            r.gk_sum.at[kv_chip(i)],
            r.gk_quad.at[chip],
            r.ksem.at[2, i],
            r.ksem.at[3, i],
            device_id={"dp": 2 * kv_chip(i) + core},
            device_id_type=MESH,
        )

    def kv_add(i):
        kv_pair(i).wait()
        b = kv_chip(i)
        r.gk_sum[b] = (r.gk[core, b].astype(F32) + r.gk_recv[b].astype(F32)).astype(B16)

    def grad_kv(i, carry):
        b = kv_chip(i)
        value = dot(r.X[:, pl.ds(pl.multiple_of(b * dw, dw), dw)], r.KV[...], TN).astype(B16)
        r.gk[0, b] = value[:hw]
        r.gk[1, b] = value[hw:]
        kv_pair(i).start()

        @pl.when(i >= 1)
        def _():
            kv_add(i - 1)
            kv_quad(i - 1).start()

        for at, n in HOPS_KV:

            @pl.when(i == at)
            def _():
                hop(n)

        return carry

    lax.fori_loop(0, NC, grad_kv, 0)

    wait_all(goq_out)
    split_total(r.go_t, r.go_sum, r.go_quad)
    for n in (8, 9):
        meets[n].send()
    wait_all(dq_out)
    dq = r.dq_send[z].astype(F32)
    for k in planes:
        dq = dq + r.dq_recv[z_from(k)].astype(F32)
    r.dq[...] = (dq.reshape(B, I) * 0.125).astype(B16)
    for i in range(NC):
        value = dot(r.latn[:, i * dw : (i + 1) * dw], r.dq[...], TN).astype(B16)
        r.gq[0, i] = value[:hw]
        r.gq[1, i] = value[hw:]
    gqs_out = remote(r.gq.at[other], r.gq_recv, dp=sib)
    kv_add(NC - 1)
    gqs_out.wait()
    add_pair(r.gq_sum, r.gq.at[core], r.gq_recv, NC)
    gqq_out = to_quad(lambda k: r.gq_sum.at[k], r.gq_quad.at[chip])
    for n in HOPS_Q:
        hop(n)

    sums[0:1, :] = jnp.zeros((1, D), F32)
    sums[1:2, :] = jnp.zeros((1, D), F32)
    sums[6:8, :] = jnp.zeros((2, D), F32)

    def media_back(s, carry):
        slot = lax.rem(s, 2)
        held = lax.rem(s, slots)
        rows = pl.ds(pl.multiple_of(s * KR, 16), KR)
        med_copy(s).wait()
        r.dn[...] = dot(r.KV[rows, :], r.wkv_all[...].reshape(D, 2 * I), NT)
        r.d_lat[pl.ds(pl.multiple_of(s * Q, 8), Q), :] = r.dn[R:, :]

        @pl.when(s >= 2)
        def _():
            pltpu.make_async_copy(r.mg.at[slot], r.media_grad.at[s - 2], r.msem.at[slot]).wait()

        def part(i, inner):
            block = pl.ds(pl.multiple_of(i * rb, rb), rb)
            unit, factor = centred(r.med[held, block, :].astype(F32))
            grad = r.dn[block, :]
            sums[0:1, :] += jnp.sum(grad * unit, 0, keepdims=True)
            sums[1:2, :] += jnp.sum(grad, 0, keepdims=True)
            r.mg[slot, block, :] = back(grad, unit, factor, param(0)).astype(B16)
            return inner

        lax.fori_loop(0, R // rb, part, 0)
        pltpu.make_async_copy(r.mg.at[slot], r.media_grad.at[s], r.msem.at[slot]).start()
        med_next(s)
        for at, n in HOPS_MED:

            @pl.when(s == at)
            def _():
                hop(n)

        return carry

    lax.fori_loop(0, MED_SPLIT, media_back, 0)
    for i in range(NC - 1):
        kv_quad(i).wait()
    split_total(r.gk_t, r.gk_sum, r.gk_quad)
    wait_all(gqq_out)
    split_total(r.gq_t, r.gq_sum, r.gq_quad)
    for n in range(10, 14):
        meets[n].send()
    lax.fori_loop(MED_SPLIT, S, media_back, 0)

    d_latn = r.d_lat[...] + dot(r.dq[...], r.wq_all[...].reshape(D, I), NT)
    unit, factor = centred(r.lat_v[...].astype(F32))
    sums[2:3, :] = jnp.sum(d_latn * unit, 0, keepdims=True)
    sums[3:4, :] = jnp.sum(d_latn, 0, keepdims=True)
    r.stage[1] = (r.d_hidden[...] + back(d_latn, unit, factor, param(2))).astype(B16)
    put_lat = local(r.stage.at[1], r.latent_grad)

    sp = D // (2 * NC)
    for t in range(NC):
        for cc in range(2):
            d = 2 * t + cc
            r.sm[cc, t] = sums[:, d * sp : (d + 1) * sp]
    sm_out = remote(r.sm.at[other], r.sm_recv, dp=sib)
    hop(HOP_END)
    sm_out.wait()
    r.sm_sum[...] = r.sm[core] + r.sm_recv[...]
    smq_out = to_quad(lambda k: r.sm_sum.at[k], r.sm_quad.at[chip])
    hop(HOP_END + 1)
    wait_all(smq_out)
    r.sm_z[z] = quad_total(r.sm_sum, r.sm_quad)
    zs_out = to_planes(lambda _: r.sm_z.at[z], r.sm_z.at[z])
    hop(HOP_END + 2)
    wait_all(out_out)
    out = r.hidden[...] + r.out_send[chip].astype(F32)
    for k in quads:
        out = out + r.out_recv[chip_to(k)].astype(F32)
    r.stage[0] = out.astype(B16)
    put_out = local(r.stage.at[0], r.latents_out)
    for n in range(HOP_END + 3, len(meets) + HOP2):
        hop(n)
    wait_all(zs_out)
    r.sm_all[...] = jnp.sum(r.sm_z[...], 0)
    put_small = local(r.sm_all, r.gsmall)
    for meet in meets:
        meet.finish()
    put_small.wait()
    for slot in range(2):
        pltpu.make_async_copy(
            r.mg.at[slot], r.media_grad.at[S - 2 + slot], r.msem.at[slot]
        ).wait()
    put_out.wait()
    put_lat.wait()
    assert used[1] <= r.rsem.shape[0] and used[0] <= r.lsem.shape[0]


def fused(n_dp, n_lat, media, latents, counts, cotangent, g_m, b_m, g_l, b_l, g_f, b_f, wq, wkv, wo, wup, wdown):
    micro, per, R, D = media.shape
    Q = latents.shape[2]
    S = micro * per
    B = S * Q
    I = wq.shape[1]
    NC = n_dp // 2
    NZ = n_lat
    KR = R + Q
    span = wup.shape[1] // NC
    dp_rows = D // n_dp
    small = jnp.stack([g_m, b_m, g_l, b_l, g_f, b_f], 0)
    hbm = pl.BlockSpec(memory_space=pl.ANY)
    ins = dict(
        media=media.reshape(S, R, D),
        lat=latents.reshape(B, D),
        cot=cotangent.reshape(B, D),
        small=small,
        wq=wq,
        wkv=wkv,
        wo=wo,
        wup=wup,
        wdown=wdown,
        counts=counts,
    )
    in_specs = [hbm] * 9 + [pl.BlockSpec(memory_space=pltpu.SMEM)]
    outs = dict(
        latents_out=((B, D), B16),
        media_grad=((S, R, D), B16),
        latent_grad=((B, D), B16),
        gsmall=((8, dp_rows), F32),
        gquery=((dp_rows, I), B16),
        gkv=((dp_rows, 2 * I), B16),
        gout=((I // n_dp, D), B16),
        gup=((dp_rows, NC * span), B16),
        gdown=((span // 2, D), B16),
    )
    kv_rows = S * KR
    o_rows = I // n_dp
    buffers = dict(
        med=((4, R, D), B16),
        X=((kv_rows, D), B16),
        KV=((kv_rows, 2 * I), B16),
        small_all=((n_dp, 6, dp_rows), B16),
        params=((8, D), F32),
        wq_all=((n_dp, dp_rows, I), B16),
        wkv_all=((n_dp, dp_rows, 2 * I), B16),
        wo_all=((n_dp, o_rows, D), B16),
        ffw=((4, span // 2, D), B16),
        lat_v=((B, D), B16),
        latn=((B, D), B16),
        cot4=((NC, B, D), B16),
        q_all=((NZ, S, Q, I), B16),
        lse=((NZ, 2 * S, NZ * Q * HEADS // 2), F32),
        lse_all=((2 * S, NZ * Q * HEADS // 2), F32),
        mask=((NZ * Q * HEADS // 2, I // 2), B16),
        mask_e=((2, NZ * Q * HEADS // 2, 128), B16),
        o_send=((NZ, S, Q, I), B16),
        o_recv=((NZ, S, Q, I), B16),
        att_f=((B, I), F32),
        att=((B, I), B16),
        hidden=((B, D), F32),
        ffn4=((NC, B, D), B16),
        d_act=((NC, B, span), F32),
        up=((B, span), F32),
        act=((NC, B, span), B16),
        d_up=((NC, B, span), B16),
        df_send=((NC, B, D), B16),
        df_recv=((NC, B, D), B16),
        out_send=((NC, B, D), B16),
        out_recv=((NC, B, D), B16),
        gd=((2, span // 2, D), B16),
        gd_recv=((span // 2, D), B16),
        gd_sum=((NZ, span // 2 // NZ, D), B16),
        gu=((2, NC, dp_rows, span), B16),
        gu_recv=((NC, dp_rows, span), B16),
        gu_sum=((NC, dp_rows, span), B16),
        gu_quad=((NC, dp_rows, span), B16),
        z_got=((2 * NZ, dp_rows, span), B16),
        z_cross=((NZ, dp_rows, span), B16),
        d_hidden=((B, D), F32),
        d_attn=((B, D), B16),
        d_ext=((NZ, S, Q, I + 128), B16),
        dq_send=((NZ, S, Q, I), B16),
        dq_recv=((NZ, S, Q, I), B16),
        dq=((B, I), B16),
        d_lat=((B, D), F32),
        dn=((KR, D), F32),
        mg=((2, R, D), B16),
        stage=((2, B, D), B16),
        sums=((8, D), F32),
        sm=((2, NC, 8, dp_rows), F32),
        sm_recv=((NC, 8, dp_rows), F32),
        sm_sum=((NC, 8, dp_rows), F32),
        sm_quad=((NC, 8, dp_rows), F32),
        sm_z=((NZ, 8, dp_rows), F32),
        sm_all=((8, dp_rows), F32),
    )
    for letter, rows, cols in (("k", dp_rows, 2 * I), ("q", dp_rows, I), ("o", o_rows, D)):
        name = "g" + letter
        buffers[name] = ((2, NC, rows, cols), B16)
        for tail in ("_recv", "_sum", "_quad"):
            buffers[name + tail] = ((NC, rows, cols), B16)
        buffers[name + "_t"] = ((2, rows // 2, cols), B16)
        buffers[name + "_got"] = ((2, rows // 2, cols), B16)
        buffers[name + "_cross"] = ((rows // 2, cols), B16)
    same = dict(gk="gu", gu_sum="act", gd_sum="d_up", gk_sum="df_send", dq_send="o_send", d_lat="up")
    for name in same:
        del buffers[name]
    names = list(ins) + list(outs) + list(buffers) + ["lsem", "ssem", "rsem", "msem", "dsem", "ksem"]
    geo = (S, R, Q, D, I, NC, NZ)

    def body(*refs):
        table = dict(zip(names, refs))
        for name, base in same.items():
            table[name] = table[base]
        fused_kernel(geo, types.SimpleNamespace(**table))

    got = pl.pallas_call(
        body,
        out_shape=[jax.ShapeDtypeStruct(s, d) for s, d in outs.values()],
        in_specs=in_specs,
        out_specs=[hbm] * len(outs),
        scratch_shapes=[pltpu.VMEM(s, d) for s, d in buffers.values()]
        + [DMA((40,)), DMA((192,)), DMA((192,)), DMA((2,)), DMA((4,)), DMA((4, 4))],
        compiler_params=pltpu.CompilerParams(
            collective_id=1, has_side_effects=True, vmem_limit_bytes=VMEM_BYTES
        ),
        name="resampler",
    )(*ins.values())
    done = finish(got)
    return (
        done[0].reshape(latents.shape),
        done[1].reshape(media.shape),
        done[2].reshape(latents.shape),
        *done[3:9],
        *done[9:],
    )


def finish_kernel(*refs):
    ins, outs = refs[:9], refs[9:23]
    stage, casts = refs[23:32], refs[32:37]
    sem_in, sem_out = refs[37:]
    parts = ins[1].shape[0]

    def media(s, load):
        if load:
            return pltpu.make_async_copy(ins[1].at[s], stage[1].at[s], sem_in.at[9 + s])
        return pltpu.make_async_copy(stage[1].at[s], outs[1].at[s], sem_out.at[9 + s])

    loads = [pltpu.make_async_copy(ins[i], stage[i], sem_in.at[i]) for i in range(9) if i != 1]
    order = [7, 6, 3, 4, 5, 0, 1, 2]
    for s in range(parts // 2):
        media(s, True).start()
    for i in order[:2]:
        loads[i].start()
    for s in range(parts // 2, parts):
        media(s, True).start()
    for i in order[2:]:
        loads[i].start()
    for s in range(parts // 2):
        media(s, True).wait()
        media(s, False).start()
    stores = []

    def cast_one(i):
        loads[3 + i].wait()
        rows = stage[4 + i].shape[0]
        step = 32

        def cast(k, carry):
            block = pl.ds(pl.multiple_of(k * step, step), step)
            casts[i][block, :] = stage[4 + i][block, :].astype(F32)
            return carry

        lax.fori_loop(0, rows // step, cast, 0)
        copy = pltpu.make_async_copy(casts[i], outs[9 + i], sem_out.at[3 + i])
        copy.start()
        stores.append(copy)

    cast_one(4)
    cast_one(3)
    for s in range(parts // 2, parts):
        media(s, True).wait()
        media(s, False).start()
    for i in range(3):
        cast_one(i)
    for at, i in enumerate((0, 2)):
        loads[at].wait()
        copy = pltpu.make_async_copy(stage[i], outs[i], sem_out.at[i])
        copy.start()
        stores.append(copy)
    loads[2].wait()
    for i in range(6):
        outs[3 + i][...] = stage[3][i]
    for s in range(parts):
        media(s, False).wait()
    for copy in stores:
        copy.wait()


def finish(got):
    hbm = pl.BlockSpec(memory_space=pl.ANY)
    vmem = pl.BlockSpec(memory_space=pltpu.VMEM)
    shapes = [jax.ShapeDtypeStruct(x.shape, x.dtype) for x in got[:3]]
    shapes += [jax.ShapeDtypeStruct((got[3].shape[1],), F32)] * 6
    shapes += [jax.ShapeDtypeStruct(x.shape, F32) for x in got[4:]]
    return pl.pallas_call(
        finish_kernel,
        out_shape=shapes,
        in_specs=[hbm] * 9,
        out_specs=[hbm] * 3 + [vmem] * 6 + [hbm] * 5,
        scratch_shapes=[pltpu.VMEM(x.shape, x.dtype) for x in got]
        + [pltpu.VMEM(x.shape, F32) for x in got[4:]]
        + [DMA((9 + got[1].shape[0],))] * 2,
        compiler_params=pltpu.CompilerParams(vmem_limit_bytes=VMEM_BYTES),
        name="casts",
    )(*got)


def solution(mesh):
    rows4 = P(None, "dp", "lat", None)
    vec = P("dp")
    mat = P("dp", None)
    n_dp, n_lat = mesh.shape["dp"], mesh.shape["lat"]
    body = fused if (n_dp, n_lat) == (8, 4) else shards
    return jax.shard_map(
        functools.partial(body, n_dp, n_lat),
        mesh=mesh,
        in_specs=(rows4, rows4, P(None, "dp"), rows4) + (vec,) * 6 + (mat,) * 5,
        out_specs=(rows4,) * 3 + (vec,) * 6 + (mat,) * 5,
        check_vma=False,
    )
```

```python
import functools
import types

import jax
import jax.numpy as jnp
from jax import lax
from jax.experimental import pallas as pl
from jax.experimental.pallas import tpu as pltpu
from jax.sharding import PartitionSpec as P

HEADS = 8
HEAD = 64
VIS = 256
EPS = 1e-05
F32 = jnp.float32
B16 = jnp.bfloat16
MESH = pl.DeviceIdType.MESH
DMA = pltpu.SemaphoreType.DMA
VMEM_BYTES = 62 << 20


def exchange_kernel(axis, n, modes, *refs):
    count = len(modes)
    ins, outs = refs[:count], refs[count : 2 * count]
    send, recv, own = refs[2 * count :]
    me = lax.axis_index(axis)
    barrier = pltpu.get_barrier_semaphore()
    for k in range(1, n):
        pl.semaphore_signal(
            barrier, inc=1, device_id={axis: lax.rem(me + k, n)}, device_id_type=MESH
        )
    pl.semaphore_wait(barrier, n - 1)
    copies = []
    for k in range(1, n):
        peer = lax.rem(me + k, n)
        for i in range(count):
            source = ins[i] if modes[i] == "gather" else ins[i].at[peer]
            copy = pltpu.make_async_remote_copy(
                source,
                outs[i].at[me],
                send.at[i, k],
                recv.at[i, k],
                device_id={axis: peer},
                device_id_type=MESH,
            )
            copy.start()
            copies.append(copy)
    for i in range(count):
        source = ins[i] if modes[i] == "gather" else ins[i].at[me]
        copy = pltpu.make_async_copy(source, outs[i].at[me], own.at[i])
        copy.start()
        copies.append(copy)
    for copy in copies:
        copy.wait()


class Exchanges:
    def __init__(self, sizes):
        self.sizes = sizes
        self.used = 0

    def __call__(self, axis, arrays, modes):
        n = self.sizes[axis]
        count = len(arrays)
        outs = [
            jax.ShapeDtypeStruct(((n,) + a.shape) if m == "gather" else a.shape, a.dtype)
            for a, m in zip(arrays, modes)
        ]
        self.used += 1
        space = pl.BlockSpec(memory_space=pl.ANY)
        return pl.pallas_call(
            functools.partial(exchange_kernel, axis, n, modes),
            out_shape=outs,
            in_specs=[space] * count,
            out_specs=[space] * count,
            scratch_shapes=[DMA((count, n)), DMA((count, n)), DMA((count,))],
            compiler_params=pltpu.CompilerParams(collective_id=self.used, has_side_effects=True),
            name="exchange_%d" % self.used,
        )(*arrays)


def norm_parts(x):
    mean = jnp.mean(x, -1, keepdims=True)
    cent = x - mean
    factor = lax.rsqrt(jnp.mean(cent * cent, -1, keepdims=True) + EPS)
    return cent * factor, factor


def norm_back(grad, unit, factor, gain):
    scaled = grad * gain
    inner = jnp.mean(scaled * unit, -1, keepdims=True)
    d_input = factor * (scaled - jnp.mean(scaled, -1, keepdims=True) - unit * inner)
    return d_input, jnp.sum(grad * unit, 0), jnp.sum(grad, 0)


def mm(a, b):
    return lax.dot_general(a, b, (((1,), (0,)), ((), ())), preferred_element_type=F32)


def mm_nt(a, b):
    return lax.dot_general(a, b, (((1,), (1,)), ((), ())), preferred_element_type=F32)


def mm_tn(a, b):
    return lax.dot_general(a, b, (((0,), (0,)), ((), ())), preferred_element_type=F32)


def shards(n_dp, n_lat, media, latents, counts, cotangent, g_m, b_m, g_l, b_l, g_f, b_f, wq, wkv, wo, wup, wdown):
    ex = Exchanges({"dp": n_dp, "lat": n_lat})
    micro, per, rows, width = media.shape
    nq = latents.shape[2]
    S = micro * per
    inner = wq.shape[1]
    ff = wup.shape[1]
    ff_part = ff // n_dp
    d_part = width // n_dp
    lat_at = lax.axis_index("lat")
    med = media.reshape(S * rows, width)
    lat = latents.reshape(S * nq, width).astype(F32)
    cot = cotangent.reshape(S * nq, width)
    count = counts.reshape(S)

    small = jnp.stack([g_m, b_m, g_l, b_l, g_f, b_f], 0)
    small_all, wq_all, wkv_all, wo_all = ex("dp", [small, wq, wkv, wo], ["gather"] * 4)
    params = jnp.transpose(small_all, (1, 0, 2)).reshape(6, width).astype(F32)
    wq_all = wq_all.reshape(width, inner)
    wkv_all = wkv_all.reshape(width, 2 * inner)
    wo_all = wo_all.reshape(inner, width)
    wup_cols = jnp.transpose(wup.reshape(d_part, n_dp, ff_part), (1, 0, 2))
    cot_all, wup_s = ex("dp", [cot, wup_cols], ["gather", "swap"])
    cot_all = cot_all.reshape(-1, width)
    wup_s = wup_s.reshape(width, ff_part)

    med_unit, med_factor = norm_parts(med.astype(F32))
    med_norm = (med_unit * params[0] + params[1]).astype(B16)
    lat_unit, lat_factor = norm_parts(lat)
    lat_norm = (lat_unit * params[2] + params[3]).astype(B16)
    query = (mm(lat_norm, wq_all) * 0.125).astype(B16)
    (query_all,) = ex("lat", [query], ["gather"])
    kv_med = mm(med_norm, wkv_all).astype(B16)
    kv_lat = mm(lat_norm, wkv_all).astype(B16)
    keyval = jnp.concatenate(
        [kv_med.reshape(S, rows, 2 * inner), kv_lat.reshape(S, nq, 2 * inner)], 1
    )
    kc = rows + nq
    keys = keyval[:, :, :inner].reshape(S, kc, HEADS, HEAD)
    values = keyval[:, :, inner:].reshape(S, kc, HEADS, HEAD)
    heads_q = query_all.reshape(n_lat, S, nq, HEADS, HEAD)
    slot = (lat_at * rows + lax.iota(jnp.int32, rows)) // VIS
    live = jnp.concatenate(
        [slot[None, :] < count[:, None], jnp.ones((S, nq), dtype=bool)], 1
    )
    score = jnp.einsum("zsqhd,skhd->shzqk", heads_q, keys, preferred_element_type=F32)
    score = jnp.where(live[:, None, None, None, :], score, -1e30)
    top = jnp.max(score, -1)
    p = jnp.exp(score - top[..., None])
    total = jnp.sum(p, -1)
    part = jnp.einsum("shzqk,skhd->zsqhd", p.astype(B16), values, preferred_element_type=F32)
    scale = jnp.transpose(1.0 / total, (2, 0, 3, 1))[..., None]
    part = (part * scale).astype(B16).reshape(n_lat, S * nq, inner)
    stats = jnp.stack([top, total], 0).reshape(2 * S * HEADS, n_lat * nq)
    part_all, stats_all = ex("lat", [part, stats], ["swap", "gather"])
    stats_all = stats_all.reshape(n_lat, 2, S, HEADS, n_lat, nq)
    tops, totals = stats_all[:, 0], stats_all[:, 1]
    top_max = jnp.max(tops, 0)
    weight = totals * jnp.exp(tops - top_max)
    whole = jnp.sum(weight, 0)
    lse = top_max + jnp.log(whole)
    weight = lax.dynamic_index_in_dim(weight / whole, lat_at, 3, keepdims=False)
    weight = jnp.transpose(weight, (0, 1, 3, 2)).reshape(n_lat, S * nq, HEADS, 1)
    attended_f = jnp.sum(part_all.reshape(n_lat, S * nq, HEADS, HEAD).astype(F32) * weight, 0)
    attended = attended_f.reshape(S * nq, inner).astype(B16)

    hidden = lat + mm(attended, wo_all)
    ffn_unit, ffn_factor = norm_parts(hidden)
    ff_norm = (ffn_unit * params[4] + params[5]).astype(B16)
    (ffn_all,) = ex("dp", [ff_norm], ["gather"])
    ffn_all = ffn_all.reshape(-1, width)
    up = mm(ffn_all, wup_s)
    act_f, pull = jax.vjp(lambda v: jax.nn.gelu(v, approximate=False), up)
    act = act_f.astype(B16)
    d_act = mm_nt(cot_all, wdown)
    d_up = pull(d_act)[0].astype(B16)
    out_part = mm(act, wdown).astype(B16).reshape(n_dp, S * nq, width)
    d_ffn_part = mm_nt(d_up, wup_s).astype(B16).reshape(n_dp, S * nq, width)
    d_ffn_all, out_all = ex("dp", [d_ffn_part, out_part], ["swap", "swap"])
    latents_out = (hidden + jnp.sum(out_all.astype(F32), 0)).astype(B16)
    d_ffn = jnp.sum(d_ffn_all.astype(F32), 0)
    grad_down = mm_tn(act, cot_all)
    grad_up = mm_tn(ffn_all, d_up)
    d_h, grad_gf, grad_bf = norm_back(d_ffn, ffn_unit, ffn_factor, params[4])
    d_hidden = cot.astype(F32) + d_h
    d_attn = d_hidden.astype(B16)
    grad_out = mm_tn(attended, d_attn)
    d_att = mm_nt(d_attn, wo_all).astype(B16)
    delta = jnp.sum(
        (d_att.astype(F32) * attended_f.reshape(S * nq, inner)).reshape(S * nq, HEADS, HEAD), -1
    )
    d_att_all, delta_all = ex("lat", [d_att, delta.T], ["gather", "gather"])
    d_att_h = d_att_all.reshape(n_lat, S, nq, HEADS, HEAD)
    delta_h = jnp.transpose(delta_all.reshape(n_lat, HEADS, S, nq), (2, 1, 0, 3))[..., None]
    prob = jnp.exp(score - lse[..., None])
    d_prob = jnp.einsum("zsqhd,skhd->shzqk", d_att_h, values, preferred_element_type=F32)
    d_score = (prob * (d_prob - delta_h)).astype(B16)
    dq_part = jnp.einsum("shzqk,skhd->zsqhd", d_score, keys, preferred_element_type=F32)
    (dq_all,) = ex("lat", [dq_part.astype(B16).reshape(n_lat, S * nq, inner)], ["swap"])
    d_keys = jnp.einsum("shzqk,zsqhd->skhd", d_score, heads_q, preferred_element_type=F32)
    d_values = jnp.einsum(
        "shzqk,zsqhd->skhd", prob.astype(B16), d_att_h, preferred_element_type=F32
    )
    d_kv = jnp.concatenate(
        [d_keys.reshape(S, kc, inner), d_values.reshape(S, kc, inner)], -1
    ).astype(B16)
    d_kv_med = d_kv[:, :rows].reshape(S * rows, 2 * inner)
    d_kv_lat = d_kv[:, rows:].reshape(S * nq, 2 * inner)
    grad_kv = mm_tn(med_norm, d_kv_med) + mm_tn(lat_norm, d_kv_lat)
    d_mnorm = mm_nt(d_kv_med, wkv_all)
    d_media, grad_gm, grad_bm = norm_back(d_mnorm, med_unit, med_factor, params[0])
    dq = (jnp.sum(dq_all.astype(F32), 0) * 0.125).astype(B16)
    grad_q = mm_tn(lat_norm, dq)
    d_lnorm = mm_nt(dq, wq_all) + mm_nt(d_kv_lat, wkv_all)
    d_latn, grad_gl, grad_bl = norm_back(d_lnorm, lat_unit, lat_factor, params[2])
    latent_grad = (d_hidden + d_latn).astype(B16)

    smalls = jnp.stack([grad_gm, grad_bm, grad_gl, grad_bl, grad_gf, grad_bf], 0)
    smalls = jnp.transpose(smalls.reshape(6, n_dp, d_part), (1, 0, 2))
    small_s, q_s, kv_s, o_s, up_s = ex(
        "dp",
        [
            smalls,
            grad_q.astype(B16).reshape(n_dp, d_part, inner),
            grad_kv.astype(B16).reshape(n_dp, d_part, 2 * inner),
            grad_out.astype(B16).reshape(n_dp, inner // n_dp, width),
            grad_up.astype(B16).reshape(n_dp, d_part, ff_part),
        ],
        ["swap"] * 5,
    )
    small_s = jnp.sum(small_s, 0)
    q_s = jnp.sum(q_s.astype(F32), 0)
    kv_s = jnp.sum(kv_s.astype(F32), 0)
    o_s = jnp.sum(o_s.astype(F32), 0)
    up_s = jnp.transpose(up_s, (1, 0, 2)).reshape(d_part, ff)
    pieces = [q_s, kv_s, o_s, up_s, grad_down]
    cut = [x.astype(B16).reshape(n_lat, x.shape[0] // n_lat, x.shape[1]) for x in pieces]
    got = ex("lat", cut + [small_s], ["swap"] * 5 + ["gather"])
    small_s = jnp.sum(got[5], 0)
    summed = [jnp.sum(x.astype(F32), 0).astype(B16) for x in got[:5]]
    full = ex("lat", summed, ["gather"] * 5)
    grads = [x.reshape(y.shape).astype(F32) for x, y in zip(full, pieces)]
    return (
        latents_out.reshape(latents.shape),
        d_media.astype(B16).reshape(media.shape),
        latent_grad.reshape(latents.shape),
        *[small_s[i] for i in range(6)],
        *grads,
    )


PROB_SPLIT = 4
ROWS_STEP = 160
NORMS = (3, 6)
SEND_A = (0, 1)
SEND_B = (2, 3)
SEND_C = ()
SEND_D = ()
HOP1, HOP2 = 2, 4
HOPS_DEXT = (0, 1)
HOPS_MID = (2,)
HOPS_ATT = ()
HOPS_KV = ((1, 3), (3, 4))
HOPS_Q = (5, 6)
HOPS_MED = ((1, 7), (4, 8), (6, 9))
MED_SPLIT = 4
HOP_END = 10

NT, NN, TN = (((1,), (1,)), ((), ())), (((1,), (0,)), ((), ())), (((0,), (0,)), ((), ()))


def dot(a, b, form):
    return lax.dot_general(a, b, form, preferred_element_type=F32)


def centred(x):
    mean = jnp.mean(x, -1, keepdims=True)
    cent = x - mean
    factor = lax.rsqrt(jnp.mean(cent * cent, -1, keepdims=True) + EPS)
    return cent * factor, factor


def back(grad, unit, factor, gain):
    scaled = grad * gain
    inner = jnp.mean(scaled * unit, -1, keepdims=True)
    return factor * (scaled - jnp.mean(scaled, -1, keepdims=True) - unit * inner)


def fused_kernel(geo, refs):
    S, R, Q, D, I, NC, NZ = geo
    KR = R + Q
    B = S * Q
    G = 2
    W = I // G
    HG = HEADS // G
    r = refs
    me = lax.axis_index("dp")
    z = lax.axis_index("lat")
    chip = me // 2
    core = lax.rem(me, 2)
    sib = me + 1 - 2 * core
    other = 1 - core

    def chip_to(k):
        return lax.rem(chip + k, NC)

    def chip_from(k):
        return lax.rem(chip + NC - k, NC)

    def z_to(k):
        return lax.rem(z + k, NZ)

    def z_from(k):
        return lax.rem(z + NZ - k, NZ)

    quads = range(1, NC)
    planes = range(1, NZ)
    used = [0, 0]

    def local(src, dst):
        sem = r.lsem.at[used[0]]
        used[0] += 1
        copy = pltpu.make_async_copy(src, dst, sem)
        copy.start()
        return copy

    def remote(src, dst, **where):
        at = used[1]
        used[1] += 1
        copy = pltpu.make_async_remote_copy(
            src, dst, r.ssem.at[at], r.rsem.at[at], device_id=where, device_id_type=MESH
        )
        copy.start()
        return copy

    class Planned:
        def __init__(self, make):
            at = used[1]
            used[1] += 1

            def build():
                src, dst, where = make()
                return pltpu.make_async_remote_copy(
                    src, dst, r.ssem.at[at], r.rsem.at[at], device_id=where, device_id_type=MESH
                )

            self.build = build

        def start(self):
            self.build().start()

        def wait(self):
            self.build().wait()

        def wait_send(self):
            self.build().wait_send()

        def wait_recv(self):
            self.build().wait_recv()

    class Spread:
        def __init__(self, src_for, dst_at):
            self.dst_at = dst_at
            self.far = [remote(src_for(chip_to(k)), dst_at(me), dp=2 * chip_to(k) + core) for k in quads]
            self.near = remote(src_for(chip), dst_at(me), dp=sib)
            self.own = local(src_for(chip), dst_at(me))

        def forward(self):
            self.passed = []
            for k in quads:
                self.far[k - 1].wait_recv()
                slot = self.dst_at(2 * chip_from(k) + core)
                self.passed.append(remote(slot, slot, dp=sib))

        def finish(self):
            self.own.wait()
            self.near.wait()
            for copy in self.far:
                copy.wait_send()
            for copy in self.passed:
                copy.wait()

    side = chip + 1 - 2 * lax.rem(chip, 2)
    ahead = chip + 2 - 4 * (chip // 2)
    cross = 3 - chip

    class Relay(Spread):
        def __init__(self, src_for, dst_at):
            self.dst_at = dst_at
            self.own = local(src_for(chip), dst_at(me))
            self.far = [remote(src_for(t), dst_at(me), dp=2 * t + core) for t in (side, ahead)]
            self.near = remote(src_for(chip), dst_at(me), dp=sib)
            self.half = dst_at(me).shape[0] // 2

        def forward(self):
            self.passed = []
            h = self.half
            for k, (source, target, at) in enumerate(((side, ahead, 0), (ahead, side, h))):
                self.far[k].wait_recv()
                slot = self.dst_at(2 * source + core)
                part = slot.at[at : at + h]
                self.passed.append(remote(part, part, dp=2 * target + core))
                self.passed.append(remote(slot, slot, dp=sib))

        def forward2(self):
            h = self.half
            self.late = []
            slot = self.dst_at(2 * cross + core)
            for k, at in ((0, 0), (2, h)):
                self.passed[k].wait_recv()
                part = slot.at[at : at + h]
                self.late.append(remote(part, part, dp=sib))

        def finish(self):
            self.own.wait()
            self.near.wait()
            for copy in self.far:
                copy.wait_send()
            for k in (0, 2):
                self.passed[k].wait_send()
            for copy in (self.passed[1], self.passed[3], *self.late):
                copy.wait()

    def to_quad(src_for, dst):
        return [remote(src_for(chip_to(k)), dst, dp=2 * chip_to(k) + core) for k in quads]

    def to_planes(src_for, dst):
        return [remote(src_for(z_to(k)), dst, lat=z_to(k)) for k in planes]

    def wait_all(copies):
        for copy in copies:
            copy.wait()

    class Line:
        def __init__(self, ref, part):
            def flow(p, way):
                return Planned(lambda: (ref.at[p, part], ref.at[p, part], {"lat": jnp.clip(z + way, 0, NZ - 1)}))

            self.up = [flow(p, 1) for p in range(NZ - 1)]
            self.down = [flow(p, -1) for p in range(1, NZ)]

        def flows(self):
            for p in range(NZ - 1):
                yield p, 1, self.up[p]
            for p in range(1, NZ):
                yield p, -1, self.down[p - 1]

        def send(self):
            for p, _, copy in self.flows():
                pl.when(z == p)(copy.start)

        def step(self, far):
            for p, way, copy in self.flows():
                at = p + way * far
                if 0 <= at < NZ:
                    last = at == (NZ - 1 if way > 0 else 0)

                    @pl.when(z == at)
                    def _():
                        copy.wait_recv()
                        if not last:
                            copy.start()

        def finish(self):
            for p, way, copy in self.flows():
                sends = jnp.logical_and(z >= p, z < NZ - 1) if way > 0 else jnp.logical_and(z <= p, z > 0)
                pl.when(sends)(copy.wait_send)

    class Meet:
        def __init__(self, own, got, cross, out, root):
            self.own, self.got, self.crossed, self.out, self.root = own, got, cross, out, root
            peer = 3 - root
            self.up = Planned(lambda: (own, got, {"lat": 1 + z // 2}))
            self.over = Planned(lambda: (own, cross, {"lat": root}))
            self.near = Planned(lambda: (own, out, {"lat": 3 * (root - 1)}))
            self.back = Planned(lambda: (own, out, {"lat": peer}))
            self.far = Planned(lambda: (out, out, {"lat": 3 * (peer - 1)}))
            self.lsem = r.lsem.at[used[0]]
            used[0] += 1

        def send(self):
            @pl.when(jnp.logical_or(z == 0, z == NZ - 1))
            def _():
                self.up.start()

        def merge(self):
            @pl.when(z == 3 - self.root)
            def _():
                self.up.wait_recv()
                self.own[...] = (self.own[...].astype(F32) + self.got[...].astype(F32)).astype(B16)
                self.over.start()

        def total(self):
            @pl.when(z == self.root)
            def _():
                self.up.wait_recv()
                both = self.own[...].astype(F32) + self.got[...].astype(F32)
                self.over.wait_recv()
                self.own[...] = (both + self.crossed[...].astype(F32)).astype(B16)
                self.near.start()
                self.back.start()
                pltpu.make_async_copy(self.own, self.out, self.lsem).start()

        def relay(self):
            @pl.when(z == 3 - self.root)
            def _():
                self.back.wait_recv()
                self.far.start()

        def finish(self):
            root, peer = self.root, 3 - self.root

            @pl.when(jnp.logical_or(z == 0, z == NZ - 1))
            def _():
                self.up.wait_send()

            @pl.when(z == 3 * (root - 1))
            def _():
                self.near.wait_recv()

            @pl.when(z == 3 * (peer - 1))
            def _():
                self.far.wait_recv()

            @pl.when(z == peer)
            def _():
                self.over.wait_send()
                self.far.wait_send()

            @pl.when(z == root)
            def _():
                self.near.wait_send()
                self.back.wait_send()
                pltpu.make_async_copy(self.own, self.out, self.lsem).wait()

    barrier = pltpu.get_barrier_semaphore()
    for k in quads:
        pl.semaphore_signal(barrier, inc=1, device_id={"dp": 2 * chip_to(k) + core}, device_id_type=MESH)
    pl.semaphore_signal(barrier, inc=1, device_id={"dp": sib}, device_id_type=MESH)
    for k in planes:
        pl.semaphore_signal(barrier, inc=1, device_id={"lat": z_to(k)}, device_id_type=MESH)
    pl.semaphore_wait(barrier, NC - 1 + 1 + NZ - 1)

    def whole(ref):
        return lambda _: ref

    def rows_at(ref):
        return lambda d: ref.at[d]

    def cols_at(ref, at, size):
        return lambda d: ref.at[d, :, at : at + size]

    part_rows = D // (2 * NC)
    per_slot = NC

    def up_at(d):
        at = pl.multiple_of(lax.rem(d, per_slot) * part_rows, part_rows)
        return r.ffw.at[2 + d // per_slot, pl.ds(at, part_rows)]

    span = r.wup.shape[1] // NC

    def down_matrix():
        return r.ffw[0:2].reshape(span, D)

    def up_matrix():
        return r.ffw[2:4].reshape(D, span)

    g_small = Spread(whole(r.small), rows_at(r.small_all))
    g_wq = Spread(whole(r.wq), rows_at(r.wq_all))
    lat_in = local(r.lat, r.lat_v)
    cot_in = local(r.cot, r.cot4.at[chip])
    slots = r.med.shape[0]

    def med_copy(s):
        slot = lax.rem(s, slots)
        return pltpu.make_async_copy(r.media.at[s], r.med.at[slot], r.dsem.at[slot])

    def med_first():
        for s in range(slots):
            med_copy(jnp.int32(s)).start()

    def med_next(s):
        @pl.when(s + slots < S)
        def _():
            med_copy(s + slots).start()

    med_first()
    g_small.forward()
    g_small.finish()
    params = r.params
    for d in range(2 * NC):
        params[0:6, d * part_rows : (d + 1) * part_rows] = r.small_all[d].astype(F32)

    def param(i):
        return params[i : i + 1, :]

    lat_in.wait()
    unit, _ = centred(r.lat_v[...].astype(F32))
    r.latn[...] = (unit * param(2) + param(3)).astype(B16)
    rb = ROWS_STEP

    def norm_sample(s, carry):
        slot = lax.rem(s, slots)
        med_copy(s).wait()

        def part(i, inner):
            x = r.med[slot, pl.ds(pl.multiple_of(i * rb, rb), rb), :].astype(F32)
            u, _ = centred(x)
            row = pl.multiple_of(s * KR + i * rb, 16)
            r.X[pl.ds(row, rb), :] = (u * param(0) + param(1)).astype(B16)
            return inner

        lax.fori_loop(0, R // rb, part, 0)
        row = pl.multiple_of(s * KR + R, 16)
        at = pl.multiple_of(s * Q, 16)
        r.X[pl.ds(row, Q), :] = r.latn[pl.ds(at, Q), :]
        med_next(s)
        return carry

    def up_slice(k):
        return r.wup.at[:, pl.ds(pl.multiple_of(k * span, 128), span)]

    def key_cols(s, carry):
        rows = pl.ds(pl.multiple_of(s * KR, 16), KR)
        r.KV[rows, 0:I] = dot(r.X[rows, :], r.wkv_all[:, :, 0:I].reshape(D, I), NN).astype(B16)
        return carry

    def value_cols(s, carry):
        rows = pl.ds(pl.multiple_of(s * KR, 16), KR)
        r.KV[rows, I : 2 * I] = dot(r.X[rows, :], r.wkv_all[:, :, I : 2 * I].reshape(D, I), NN).astype(B16)
        return carry

    first, second = NORMS
    lax.fori_loop(0, first, norm_sample, 0)
    g_key = Relay(lambda _: r.wkv.at[:, 0:I], cols_at(r.wkv_all, 0, I))
    g_wq.forward()
    g_val = Relay(lambda _: r.wkv.at[:, I : 2 * I], cols_at(r.wkv_all, I, I))
    g_wq.finish()
    query = dot(r.latn[...], r.wq_all[...].reshape(D, I), NN) * 0.125
    r.q_all[z] = query.astype(B16).reshape(S, Q, I)
    q_out = to_planes(lambda _: r.q_all.at[z], r.q_all.at[z])
    lax.fori_loop(first, second, norm_sample, 0)
    g_key.forward()
    g_wo = Relay(whole(r.wo), rows_at(r.wo_all))
    lax.fori_loop(second, S, norm_sample, 0)
    med_first()
    g_key.forward2()
    g_val.forward()
    g_up = Spread(up_slice, up_at)
    g_key.finish()
    lax.fori_loop(0, S, key_cols, 0)
    g_val.forward2()
    g_wo.forward()
    g_down = remote(r.wdown, r.ffw.at[core], dp=sib)
    g_down_own = local(r.wdown, r.ffw.at[core])
    g_val.finish()
    lax.fori_loop(0, S, value_cols, 0)
    g_wo.forward2()
    cot_in.wait()
    g_cot = to_quad(lambda _: r.cot, r.cot4.at[chip])
    wait_all(q_out)

    own_head = (
        lax.broadcasted_iota(jnp.int32, (HG * NZ * Q, W), 0) // (NZ * Q)
        == lax.broadcasted_iota(jnp.int32, (HG * NZ * Q, W), 1) // HEAD
    )
    r.mask[...] = own_head.astype(F32).astype(B16)

    def spread_heads(x):
        return jnp.concatenate([x] * HG, 0) * r.mask[...]

    def take_heads(x):
        low = lax.broadcasted_iota(jnp.int32, (NZ * Q, 2 * HEAD), 1) < HEAD
        cols = []
        for pair in range(HG // 2):
            block = x[:, pair * 2 * HEAD : (pair + 1) * 2 * HEAD]
            n = NZ * Q
            cols.append(
                jnp.where(low, block[2 * pair * n : (2 * pair + 1) * n], block[(2 * pair + 1) * n : (2 * pair + 2) * n])
            )
        return jnp.concatenate(cols, 1)

    def scores(s, g, qbig):
        rows = pl.ds(pl.multiple_of(s * KR, 16), KR)
        raw = dot(r.KV[rows, g * W : (g + 1) * W], qbig, NT)
        row = lax.broadcasted_iota(jnp.int32, raw.shape, 0)
        live = jnp.logical_or(row >= R, row + z * R < r.counts[s // r.counts.shape[1], lax.rem(s, r.counts.shape[1])] * VIS)
        return jnp.where(live, raw, -1e30)

    def queries(s, g):
        return spread_heads(r.q_all[:, s, :, g * W : (g + 1) * W].reshape(NZ * Q, W))

    def attend(s, carry):
        rows = pl.ds(pl.multiple_of(s * KR, 16), KR)
        for g in range(G):
            score = scores(s, g, queries(s, g))
            top = jnp.max(score, 0, keepdims=True)
            grown = jnp.exp(score - top)
            total = jnp.sum(grown, 0, keepdims=True)
            r.lse[z, pl.ds(g * S + s, 1), :] = top + jnp.log(total)
            prob = (grown * (1.0 / total)).astype(B16)
            part = dot(prob, r.KV[rows, I + g * W : I + (g + 1) * W], TN)
            r.o_send[:, s, :, g * W : (g + 1) * W] = take_heads(part).astype(B16).reshape(NZ, Q, W)

        @pl.when(s == S // 2)
        def _():
            for copy in o_out[: NZ - 1]:
                copy.start()

        return carry

    def half(n):
        return slice(n * (S // 2), (n + 1) * (S // 2))

    def plan(make):
        return [Planned(functools.partial(make, k, n)) for n in range(2) for k in planes]

    o_out = plan(lambda k, n: (r.o_send.at[z_to(k), half(n)], r.o_recv.at[z, half(n)], {"lat": z_to(k)}))
    lax.fori_loop(0, S, attend, 0)
    lse_out = to_planes(lambda _: r.lse.at[z], r.lse.at[z])
    for copy in o_out[NZ - 1 :]:
        copy.start()
    wait_all(lse_out)
    every = r.lse[...]
    top = jnp.max(every, 0)
    lse_all = top + jnp.log(jnp.sum(jnp.exp(every - top[None]), 0))
    r.lse_all[...] = lse_all
    r.lse[...] = jnp.exp(every - lse_all[None])
    pick = (
        lax.rem(lax.broadcasted_iota(jnp.int32, (B, HG * NZ * Q), 1), NZ * Q)
        == lax.rem(lax.broadcasted_iota(jnp.int32, (B, HG * NZ * Q), 0), Q) + z * Q
    )
    for k in range(NZ):
        store = r.hidden if k < 2 else r.d_hidden
        for g in range(G):
            lanes = jnp.broadcast_to(
                r.lse[z_from(k), g * S : (g + 1) * S, :][:, None, :], (S, Q, HG * NZ * Q)
            ).reshape(B, HG * NZ * Q)
            lanes = jnp.where(pick, lanes, 0.0)
            coarse = lanes.astype(B16)
            fine = (lanes - coarse.astype(F32)).astype(B16)
            at = (k % 2) * I + g * W
            store[:, at : at + W] = dot(coarse, r.mask[...], NN) + dot(fine, r.mask[...], NN)
    g_up.forward()
    g_wo.finish()
    wait_all(o_out)
    att = r.hidden[:, 0:I] * r.o_send[z].astype(F32).reshape(B, I)
    for k in planes:
        store = r.hidden if k < 2 else r.d_hidden
        at = (k % 2) * I
        att = att + store[:, at : at + I] * r.o_recv[z_from(k)].astype(F32).reshape(B, I)
    r.att_f[...] = att
    r.att[...] = att.astype(B16)
    hidden = r.lat_v[...].astype(F32) + dot(r.att[...], r.wo_all[...].reshape(I, D), NN)
    r.hidden[...] = hidden
    unit, _ = centred(hidden)
    r.ffn4[chip] = (unit * param(4) + param(5)).astype(B16)
    f_out = to_quad(lambda _: r.ffn4.at[chip], r.ffn4.at[chip])

    def act_grad(b, carry):
        r.d_act[b] = dot(r.cot4[b], down_matrix(), NT)
        return carry

    wait_all(g_cot)
    g_down.wait()
    g_down_own.wait()
    g_up.finish()
    lax.fori_loop(0, NC, act_grad, 0)

    def feed(b):
        r.up[...] = dot(r.ffn4[b], up_matrix(), NN)

        def gelu_part(i, carry):
            rows = pl.ds(pl.multiple_of(i * 32, 32), 32)
            x = r.up[rows, :]
            cdf = 0.5 * (1.0 + lax.erf(x * 0.7071067811865476))
            pdf = jnp.exp(-0.5 * x * x) * 0.3989422804014327
            r.act[b, rows, :] = (x * cdf).astype(B16)
            r.d_up[b, rows, :] = (r.d_act[b, rows, :] * (cdf + x * pdf)).astype(B16)
            return carry

        lax.fori_loop(0, B // 32, gelu_part, 0)
        r.df_send[b] = dot(r.d_up[b], up_matrix(), NT).astype(B16)

    feed(chip)
    df_out = []
    for k in quads:
        f_out[k - 1].wait_recv()
        b = chip_from(k)
        feed(b)
        df_out.append(remote(r.df_send.at[b], r.df_recv.at[chip], dp=2 * b + core))

    own_span = span // 2
    act2 = r.act

    def grad_down(half_core):
        def body(i, carry):
            at = pl.multiple_of(half_core * own_span + i * 256, 256)
            value = dot(
                act2[:, :, pl.ds(at, 256)].reshape(NC * B, 256), r.cot4[...].reshape(NC * B, D), TN
            )
            r.gd[half_core, pl.ds(pl.multiple_of(i * 256, 256), 256), :] = value.astype(B16)
            return carry

        lax.fori_loop(0, own_span // 256, body, 0)

    grad_down(other)
    gd_out = remote(r.gd.at[other], r.gd_recv, dp=sib)
    grad_down(core)
    dw = D // NC
    hw = dw // 2

    def grad_up(i, carry):
        at = pl.multiple_of(i * dw, dw)
        value = dot(
            r.ffn4[:, :, pl.ds(at, dw)].reshape(NC * B, dw), r.d_up[...].reshape(NC * B, span), TN
        ).astype(B16)
        r.gu[0, i] = value[:hw]
        r.gu[1, i] = value[hw:]
        return carry

    lax.fori_loop(0, NC, grad_up, 0)
    gu_out = remote(r.gu.at[other], r.gu_recv, dp=sib)

    piece = own_span // NZ
    gd_out.wait()
    for j in range(NZ):
        rows = slice(j * piece, (j + 1) * piece)
        r.gd_sum[j] = (r.gd[core, rows, :].astype(F32) + r.gd_recv[rows, :].astype(F32)).astype(B16)

    meets = [
        Meet(r.gd_sum.at[j], r.z_got.at[j], r.z_cross.at[j // 2], r.gdown.at[j * piece : (j + 1) * piece, :], 1 + j % 2)
        for j in range(NZ)
    ]
    meets += [
        Meet(r.gu_quad.at[j], r.z_got.at[NZ + j], r.z_cross.at[(NZ + j) // 2], r.gup.at[:, j * span : (j + 1) * span], 1 + j % 2)
        for j in range(NC)
    ]
    for part_, got_, cross_, out_ in (
        (r.go_t, r.go_got, r.go_cross, r.gout),
        (r.gk_t, r.gk_got, r.gk_cross, r.gkv),
        (r.gq_t, r.gq_got, r.gq_cross, r.gquery),
    ):
        rows = part_.shape[1]
        meets += [
            Meet(part_.at[j], got_.at[j], cross_, out_.at[j * rows : (j + 1) * rows, :], 1 + j) for j in range(2)
        ]

    def hop(n):
        if 0 <= n < len(meets):
            meets[n].merge()
        if 0 <= n - HOP1 < len(meets):
            meets[n - HOP1].total()
        if 0 <= n - HOP2 < len(meets):
            meets[n - HOP2].relay()

    for n in SEND_A:
        meets[n].send()
    def down(i, carry):
        r.out_send[i] = dot(r.act[i], down_matrix(), NN).astype(B16)
        return carry

    lax.fori_loop(0, NC, down, 0)
    gu_out.wait()

    for copy in f_out:
        copy.wait_send()
    wait_all(df_out)
    d_ffn = r.df_send[chip].astype(F32)
    for k in quads:
        d_ffn = d_ffn + r.df_recv[chip_to(k)].astype(F32)
    unit, factor = centred(r.hidden[...])
    sums = r.sums
    sums[4:5, :] = jnp.sum(d_ffn * unit, 0, keepdims=True)
    sums[5:6, :] = jnp.sum(d_ffn, 0, keepdims=True)
    d_hidden = r.cot4[chip].astype(F32) + back(d_ffn, unit, factor, param(4))
    r.d_hidden[...] = d_hidden
    r.d_attn[...] = d_hidden.astype(B16)
    d_att = dot(r.d_attn[...], r.wo_all[...].reshape(I, D), NT).astype(B16)
    weighed = d_att.astype(F32) * r.att_f[...]
    lane = lax.broadcasted_iota(jnp.int32, (B, 128), 1)
    delta = jnp.zeros((B, 128), F32)
    low_lane = lax.broadcasted_iota(jnp.int32, (B, 128), 1) < HEAD
    for h in range(HEADS):
        block = weighed[:, (h // 2) * 128 : (h // 2) * 128 + 128]
        keep = low_lane if h % 2 == 0 else jnp.logical_not(low_lane)
        one = jnp.sum(jnp.where(keep, block, 0.0), -1, keepdims=True)
        delta = jnp.where(jnp.logical_or(lane == h, lane == HEADS + h), -one, delta)
    coarse = delta.astype(B16).astype(F32)
    ext = jnp.where(lane < HEADS, coarse, delta - coarse).astype(B16)
    r.d_ext[z, :, :, 0:I] = d_att.reshape(S, Q, I)
    r.d_ext[z, :, :, I : I + 128] = ext.reshape(S, Q, 128)
    line = [Line(r.d_ext, half(n)) for n in range(2)]
    for one in line:
        one.send()

    ow = I // NC
    oh = ow // 2
    for i in range(NC):
        value = dot(r.att[:, i * ow : (i + 1) * ow], r.d_attn[...], TN).astype(B16)
        r.go[0, i] = value[:oh]
        r.go[1, i] = value[oh:]
    go_out = remote(r.go.at[other], r.go_recv, dp=sib)

    def add_pair(dst, a, b, n):
        def body(i, carry):
            dst[i] = (a[i].astype(F32) + b[i].astype(F32)).astype(B16)
            return carry

        lax.fori_loop(0, n, body, 0)

    add_pair(r.gu_sum, r.gu.at[core], r.gu_recv, NC)
    guq_out = to_quad(lambda k: r.gu_sum.at[k], r.gu_quad.at[chip])
    for n in SEND_B:
        meets[n].send()

    def prob_at(s, g):
        lanes = pl.ds(pl.multiple_of(lax.rem(s, 2) * I + g * W, W), W)
        return r.ffw.at[s // 2, 0:KR, lanes]

    def probs(s, carry):
        for g in range(G):
            score = scores(s, g, queries(s, g))
            prob_at(s, g)[...] = jnp.exp(score - r.lse_all[pl.ds(g * S + s, 1), :]).astype(B16)
        return carry

    lax.fori_loop(0, PROB_SPLIT, probs, 0)
    line[0].step(1)
    lax.fori_loop(PROB_SPLIT, S, probs, 0)
    go_out.wait()
    add_pair(r.go_sum, r.go.at[core], r.go_recv, NC)

    def quad_total(own, got):
        total = own[chip].astype(F32)
        for k in quads:
            total = total + got[chip_to(k)].astype(F32)
        return total

    def split_total(dst, own, got):
        total = quad_total(own, got).astype(B16)
        rows = total.shape[0] // 2
        for j in range(2):
            dst[j] = total[j * rows : (j + 1) * rows]

    line[0].step(2)
    line[1].step(1)
    for n in HOPS_DEXT:
        hop(n)
    line[0].step(3)
    line[1].step(2)
    for n in SEND_C:
        meets[n].send()

    ones = jnp.ones((KR, 128), B16)
    lane_e = lax.broadcasted_iota(jnp.int32, (HG * NZ * Q, 128), 1)
    head_e = lax.broadcasted_iota(jnp.int32, (HG * NZ * Q, 128), 0) // (NZ * Q)
    for g in range(G):
        r.mask_e[g] = (
            jnp.logical_or(lane_e == head_e + g * HG, lane_e == head_e + g * HG + HEADS).astype(F32).astype(B16)
        )

    dq_out = plan(lambda k, n: (r.dq_send.at[z_to(k), half(n)], r.dq_recv.at[z, half(n)], {"lat": z_to(k)}))

    def attend_back(s, carry):
        rows = pl.ds(pl.multiple_of(s * KR, 16), KR)

        for g in range(G):
            qbig = queries(s, g)
            prob = prob_at(s, g)[...]
            dbig = spread_heads(r.d_ext[:, s, :, g * W : (g + 1) * W].reshape(NZ * Q, W))
            minus = r.d_ext[:, s, :, I : I + 128].reshape(NZ * Q, 128)
            minus = jnp.concatenate([minus] * HG, 0) * r.mask_e[g]
            d_prob = dot(r.KV[rows, I + g * W : I + (g + 1) * W], dbig, NT) + dot(ones, minus, NT)
            d_score = (prob.astype(F32) * d_prob).astype(B16)
            dq = dot(d_score, r.KV[rows, g * W : (g + 1) * W], TN)
            r.dq_send[:, s, :, g * W : (g + 1) * W] = take_heads(dq).astype(B16).reshape(NZ, Q, W)
            r.KV[rows, g * W : (g + 1) * W] = dot(d_score, qbig, NN).astype(B16)
            r.KV[rows, I + g * W : I + (g + 1) * W] = dot(prob, dbig, NN).astype(B16)
        return carry

    lax.fori_loop(0, S // 2, attend_back, 0)
    for copy in dq_out[: NZ - 1]:
        copy.start()
    goq_out = to_quad(lambda k: r.go_sum.at[k], r.go_quad.at[chip])
    out_out = to_quad(lambda k: r.out_send.at[k], r.out_recv.at[chip])
    for n in HOPS_MID:
        hop(n)
    line[1].step(3)
    for n in SEND_D:
        meets[n].send()
    lax.fori_loop(S // 2, S, attend_back, 0)
    for one in line:
        one.finish()
    for copy in dq_out[NZ - 1 :]:
        copy.start()
    wait_all(guq_out)
    r.gu_quad[chip] = r.gu_sum[chip]
    for n in range(NZ, NZ + NC):
        meets[n].send()
    for n in HOPS_ATT:
        hop(n)

    def kv_chip(i):
        return lax.rem(chip + 1 + i, NC)

    def kv_pair(i):
        return pltpu.make_async_remote_copy(
            r.gk.at[other, kv_chip(i)],
            r.gk_recv.at[kv_chip(i)],
            r.ksem.at[0, i],
            r.ksem.at[1, i],
            device_id={"dp": sib},
            device_id_type=MESH,
        )

    def kv_quad(i):
        return pltpu.make_async_remote_copy(
            r.gk_sum.at[kv_chip(i)],
            r.gk_quad.at[chip],
            r.ksem.at[2, i],
            r.ksem.at[3, i],
            device_id={"dp": 2 * kv_chip(i) + core},
            device_id_type=MESH,
        )

    def kv_add(i):
        kv_pair(i).wait()
        b = kv_chip(i)
        r.gk_sum[b] = (r.gk[core, b].astype(F32) + r.gk_recv[b].astype(F32)).astype(B16)

    def grad_kv(i, carry):
        b = kv_chip(i)
        value = dot(r.X[:, pl.ds(pl.multiple_of(b * dw, dw), dw)], r.KV[...], TN).astype(B16)
        r.gk[0, b] = value[:hw]
        r.gk[1, b] = value[hw:]
        kv_pair(i).start()

        @pl.when(i >= 1)
        def _():
            kv_add(i - 1)
            kv_quad(i - 1).start()

        for at, n in HOPS_KV:

            @pl.when(i == at)
            def _():
                hop(n)

        return carry

    lax.fori_loop(0, NC, grad_kv, 0)

    wait_all(goq_out)
    split_total(r.go_t, r.go_sum, r.go_quad)
    for n in (8, 9):
        meets[n].send()
    wait_all(dq_out)
    dq = r.dq_send[z].astype(F32)
    for k in planes:
        dq = dq + r.dq_recv[z_from(k)].astype(F32)
    r.dq[...] = (dq.reshape(B, I) * 0.125).astype(B16)
    for i in range(NC):
        value = dot(r.latn[:, i * dw : (i + 1) * dw], r.dq[...], TN).astype(B16)
        r.gq[0, i] = value[:hw]
        r.gq[1, i] = value[hw:]
    gqs_out = remote(r.gq.at[other], r.gq_recv, dp=sib)
    kv_add(NC - 1)
    gqs_out.wait()
    add_pair(r.gq_sum, r.gq.at[core], r.gq_recv, NC)
    gqq_out = to_quad(lambda k: r.gq_sum.at[k], r.gq_quad.at[chip])
    for n in HOPS_Q:
        hop(n)

    sums[0:1, :] = jnp.zeros((1, D), F32)
    sums[1:2, :] = jnp.zeros((1, D), F32)
    sums[6:8, :] = jnp.zeros((2, D), F32)

    def media_back(s, carry):
        slot = lax.rem(s, 2)
        held = lax.rem(s, slots)
        rows = pl.ds(pl.multiple_of(s * KR, 16), KR)
        med_copy(s).wait()
        r.dn[...] = dot(r.KV[rows, :], r.wkv_all[...].reshape(D, 2 * I), NT)
        r.d_lat[pl.ds(pl.multiple_of(s * Q, 8), Q), :] = r.dn[R:, :]

        @pl.when(s >= 2)
        def _():
            pltpu.make_async_copy(r.mg.at[slot], r.media_grad.at[s - 2], r.msem.at[slot]).wait()

        def part(i, inner):
            block = pl.ds(pl.multiple_of(i * rb, rb), rb)
            unit, factor = centred(r.med[held, block, :].astype(F32))
            grad = r.dn[block, :]
            sums[0:1, :] += jnp.sum(grad * unit, 0, keepdims=True)
            sums[1:2, :] += jnp.sum(grad, 0, keepdims=True)
            r.mg[slot, block, :] = back(grad, unit, factor, param(0)).astype(B16)
            return inner

        lax.fori_loop(0, R // rb, part, 0)
        pltpu.make_async_copy(r.mg.at[slot], r.media_grad.at[s], r.msem.at[slot]).start()
        med_next(s)
        for at, n in HOPS_MED:

            @pl.when(s == at)
            def _():
                hop(n)

        return carry

    lax.fori_loop(0, MED_SPLIT, media_back, 0)
    for i in range(NC - 1):
        kv_quad(i).wait()
    split_total(r.gk_t, r.gk_sum, r.gk_quad)
    wait_all(gqq_out)
    split_total(r.gq_t, r.gq_sum, r.gq_quad)
    for n in range(10, 14):
        meets[n].send()
    lax.fori_loop(MED_SPLIT, S, media_back, 0)

    d_latn = r.d_lat[...] + dot(r.dq[...], r.wq_all[...].reshape(D, I), NT)
    unit, factor = centred(r.lat_v[...].astype(F32))
    sums[2:3, :] = jnp.sum(d_latn * unit, 0, keepdims=True)
    sums[3:4, :] = jnp.sum(d_latn, 0, keepdims=True)
    r.stage[1] = (r.d_hidden[...] + back(d_latn, unit, factor, param(2))).astype(B16)
    put_lat = local(r.stage.at[1], r.latent_grad)

    sp = D // (2 * NC)
    for t in range(NC):
        for cc in range(2):
            d = 2 * t + cc
            r.sm[cc, t] = sums[:, d * sp : (d + 1) * sp]
    sm_out = remote(r.sm.at[other], r.sm_recv, dp=sib)
    hop(HOP_END)
    sm_out.wait()
    r.sm_sum[...] = r.sm[core] + r.sm_recv[...]
    smq_out = to_quad(lambda k: r.sm_sum.at[k], r.sm_quad.at[chip])
    hop(HOP_END + 1)
    wait_all(smq_out)
    r.sm_z[z] = quad_total(r.sm_sum, r.sm_quad)
    zs_out = to_planes(lambda _: r.sm_z.at[z], r.sm_z.at[z])
    hop(HOP_END + 2)
    wait_all(out_out)
    out = r.hidden[...] + r.out_send[chip].astype(F32)
    for k in quads:
        out = out + r.out_recv[chip_to(k)].astype(F32)
    r.stage[0] = out.astype(B16)
    put_out = local(r.stage.at[0], r.latents_out)
    for n in range(HOP_END + 3, len(meets) + HOP2):
        hop(n)
    wait_all(zs_out)
    r.sm_all[...] = jnp.sum(r.sm_z[...], 0)
    put_small = local(r.sm_all, r.gsmall)
    for meet in meets:
        meet.finish()
    put_small.wait()
    for slot in range(2):
        pltpu.make_async_copy(
            r.mg.at[slot], r.media_grad.at[S - 2 + slot], r.msem.at[slot]
        ).wait()
    put_out.wait()
    put_lat.wait()
    assert used[1] <= r.rsem.shape[0] and used[0] <= r.lsem.shape[0]


def fused(n_dp, n_lat, media, latents, counts, cotangent, g_m, b_m, g_l, b_l, g_f, b_f, wq, wkv, wo, wup, wdown):
    micro, per, R, D = media.shape
    Q = latents.shape[2]
    S = micro * per
    B = S * Q
    I = wq.shape[1]
    NC = n_dp // 2
    NZ = n_lat
    KR = R + Q
    span = wup.shape[1] // NC
    dp_rows = D // n_dp
    small = jnp.stack([g_m, b_m, g_l, b_l, g_f, b_f], 0)
    hbm = pl.BlockSpec(memory_space=pl.ANY)
    ins = dict(
        media=media.reshape(S, R, D),
        lat=latents.reshape(B, D),
        cot=cotangent.reshape(B, D),
        small=small,
        wq=wq,
        wkv=wkv,
        wo=wo,
        wup=wup,
        wdown=wdown,
        counts=counts,
    )
    in_specs = [hbm] * 9 + [pl.BlockSpec(memory_space=pltpu.SMEM)]
    outs = dict(
        latents_out=((B, D), B16),
        media_grad=((S, R, D), B16),
        latent_grad=((B, D), B16),
        gsmall=((8, dp_rows), F32),
        gquery=((dp_rows, I), B16),
        gkv=((dp_rows, 2 * I), B16),
        gout=((I // n_dp, D), B16),
        gup=((dp_rows, NC * span), B16),
        gdown=((span // 2, D), B16),
    )
    kv_rows = S * KR
    o_rows = I // n_dp
    buffers = dict(
        med=((4, R, D), B16),
        X=((kv_rows, D), B16),
        KV=((kv_rows, 2 * I), B16),
        small_all=((n_dp, 6, dp_rows), B16),
        params=((8, D), F32),
        wq_all=((n_dp, dp_rows, I), B16),
        wkv_all=((n_dp, dp_rows, 2 * I), B16),
        wo_all=((n_dp, o_rows, D), B16),
        ffw=((4, span // 2, D), B16),
        lat_v=((B, D), B16),
        latn=((B, D), B16),
        cot4=((NC, B, D), B16),
        q_all=((NZ, S, Q, I), B16),
        lse=((NZ, 2 * S, NZ * Q * HEADS // 2), F32),
        lse_all=((2 * S, NZ * Q * HEADS // 2), F32),
        mask=((NZ * Q * HEADS // 2, I // 2), B16),
        mask_e=((2, NZ * Q * HEADS // 2, 128), B16),
        o_send=((NZ, S, Q, I), B16),
        o_recv=((NZ, S, Q, I), B16),
        att_f=((B, I), F32),
        att=((B, I), B16),
        hidden=((B, D), F32),
        ffn4=((NC, B, D), B16),
        d_act=((NC, B, span), F32),
        up=((B, span), F32),
        act=((NC, B, span), B16),
        d_up=((NC, B, span), B16),
        df_send=((NC, B, D), B16),
        df_recv=((NC, B, D), B16),
        out_send=((NC, B, D), B16),
        out_recv=((NC, B, D), B16),
        gd=((2, span // 2, D), B16),
        gd_recv=((span // 2, D), B16),
        gd_sum=((NZ, span // 2 // NZ, D), B16),
        gu=((2, NC, dp_rows, span), B16),
        gu_recv=((NC, dp_rows, span), B16),
        gu_sum=((NC, dp_rows, span), B16),
        gu_quad=((NC, dp_rows, span), B16),
        z_got=((2 * NZ, dp_rows, span), B16),
        z_cross=((NZ, dp_rows, span), B16),
        d_hidden=((B, D), F32),
        d_attn=((B, D), B16),
        d_ext=((NZ, S, Q, I + 128), B16),
        dq_send=((NZ, S, Q, I), B16),
        dq_recv=((NZ, S, Q, I), B16),
        dq=((B, I), B16),
        d_lat=((B, D), F32),
        dn=((KR, D), F32),
        mg=((2, R, D), B16),
        stage=((2, B, D), B16),
        sums=((8, D), F32),
        sm=((2, NC, 8, dp_rows), F32),
        sm_recv=((NC, 8, dp_rows), F32),
        sm_sum=((NC, 8, dp_rows), F32),
        sm_quad=((NC, 8, dp_rows), F32),
        sm_z=((NZ, 8, dp_rows), F32),
        sm_all=((8, dp_rows), F32),
    )
    for letter, rows, cols in (("k", dp_rows, 2 * I), ("q", dp_rows, I), ("o", o_rows, D)):
        name = "g" + letter
        buffers[name] = ((2, NC, rows, cols), B16)
        for tail in ("_recv", "_sum", "_quad"):
            buffers[name + tail] = ((NC, rows, cols), B16)
        buffers[name + "_t"] = ((2, rows // 2, cols), B16)
        buffers[name + "_got"] = ((2, rows // 2, cols), B16)
        buffers[name + "_cross"] = ((rows // 2, cols), B16)
    same = dict(gk="gu", gu_sum="act", gd_sum="d_up", gk_sum="df_send", dq_send="o_send", d_lat="up", stage="ffn4")
    for name in same:
        del buffers[name]
    names = list(ins) + list(outs) + list(buffers) + ["lsem", "ssem", "rsem", "msem", "dsem", "ksem"]
    geo = (S, R, Q, D, I, NC, NZ)

    def body(*refs):
        table = dict(zip(names, refs))
        for name, base in same.items():
            table[name] = table[base]
        fused_kernel(geo, types.SimpleNamespace(**table))

    got = pl.pallas_call(
        body,
        out_shape=[jax.ShapeDtypeStruct(s, d) for s, d in outs.values()],
        in_specs=in_specs,
        out_specs=[hbm] * len(outs),
        scratch_shapes=[pltpu.VMEM(s, d) for s, d in buffers.values()]
        + [DMA((40,)), DMA((192,)), DMA((192,)), DMA((2,)), DMA((4,)), DMA((4, 4))],
        compiler_params=pltpu.CompilerParams(
            collective_id=1, has_side_effects=True, vmem_limit_bytes=VMEM_BYTES
        ),
        name="resampler",
    )(*ins.values())
    done = finish(got)
    return (
        done[0].reshape(latents.shape),
        done[1].reshape(media.shape),
        done[2].reshape(latents.shape),
        *done[3:9],
        *done[9:],
    )


def finish_kernel(*refs):
    ins, outs = refs[:9], refs[9:23]
    stage, casts = refs[23:32], refs[32:37]
    sem_in, sem_out = refs[37:]
    parts = ins[1].shape[0]

    def media(s, load):
        if load:
            return pltpu.make_async_copy(ins[1].at[s], stage[1].at[s], sem_in.at[9 + s])
        return pltpu.make_async_copy(stage[1].at[s], outs[1].at[s], sem_out.at[9 + s])

    loads = [pltpu.make_async_copy(ins[i], stage[i], sem_in.at[i]) for i in range(9) if i != 1]
    order = [7, 6, 3, 4, 5, 0, 1, 2]
    for s in range(parts // 2):
        media(s, True).start()
    for i in order[:2]:
        loads[i].start()
    for s in range(parts // 2, parts):
        media(s, True).start()
    for i in order[2:]:
        loads[i].start()
    for s in range(parts // 2):
        media(s, True).wait()
        media(s, False).start()
    stores = []

    def cast_one(i):
        loads[3 + i].wait()
        rows = stage[4 + i].shape[0]
        step = 32

        def cast(k, carry):
            block = pl.ds(pl.multiple_of(k * step, step), step)
            casts[i][block, :] = stage[4 + i][block, :].astype(F32)
            return carry

        lax.fori_loop(0, rows // step, cast, 0)
        copy = pltpu.make_async_copy(casts[i], outs[9 + i], sem_out.at[3 + i])
        copy.start()
        stores.append(copy)

    cast_one(4)
    cast_one(3)
    for s in range(parts // 2, parts):
        media(s, True).wait()
        media(s, False).start()
    for i in range(3):
        cast_one(i)
    for at, i in enumerate((0, 2)):
        loads[at].wait()
        copy = pltpu.make_async_copy(stage[i], outs[i], sem_out.at[i])
        copy.start()
        stores.append(copy)
    loads[2].wait()
    for i in range(6):
        outs[3 + i][...] = stage[3][i]
    for s in range(parts):
        media(s, False).wait()
    for copy in stores:
        copy.wait()


def finish(got):
    hbm = pl.BlockSpec(memory_space=pl.ANY)
    vmem = pl.BlockSpec(memory_space=pltpu.VMEM)
    shapes = [jax.ShapeDtypeStruct(x.shape, x.dtype) for x in got[:3]]
    shapes += [jax.ShapeDtypeStruct((got[3].shape[1],), F32)] * 6
    shapes += [jax.ShapeDtypeStruct(x.shape, F32) for x in got[4:]]
    return pl.pallas_call(
        finish_kernel,
        out_shape=shapes,
        in_specs=[hbm] * 9,
        out_specs=[hbm] * 3 + [vmem] * 6 + [hbm] * 5,
        scratch_shapes=[pltpu.VMEM(x.shape, x.dtype) for x in got]
        + [pltpu.VMEM(x.shape, F32) for x in got[4:]]
        + [DMA((9 + got[1].shape[0],))] * 2,
        compiler_params=pltpu.CompilerParams(vmem_limit_bytes=VMEM_BYTES),
        name="casts",
    )(*got)


def solution(mesh):
    rows4 = P(None, "dp", "lat", None)
    vec = P("dp")
    mat = P("dp", None)
    n_dp, n_lat = mesh.shape["dp"], mesh.shape["lat"]
    body = fused if (n_dp, n_lat) == (8, 4) else shards
    return jax.shard_map(
        functools.partial(body, n_dp, n_lat),
        mesh=mesh,
        in_specs=(rows4, rows4, P(None, "dp"), rows4) + (vec,) * 6 + (mat,) * 5,
        out_specs=(rows4,) * 3 + (vec,) * 6 + (mat,) * 5,
        check_vma=False,
    )
```

```python
import functools
import types

import jax
import jax.numpy as jnp
from jax import lax
from jax.experimental import pallas as pl
from jax.experimental.pallas import tpu as pltpu
from jax.sharding import PartitionSpec as P

HEADS = 8
HEAD = 64
VIS = 256
EPS = 1e-05
F32 = jnp.float32
B16 = jnp.bfloat16
MESH = pl.DeviceIdType.MESH
DMA = pltpu.SemaphoreType.DMA
VMEM_BYTES = 62 << 20


def exchange_kernel(axis, n, modes, *refs):
    count = len(modes)
    ins, outs = refs[:count], refs[count : 2 * count]
    send, recv, own = refs[2 * count :]
    me = lax.axis_index(axis)
    barrier = pltpu.get_barrier_semaphore()
    for k in range(1, n):
        pl.semaphore_signal(
            barrier, inc=1, device_id={axis: lax.rem(me + k, n)}, device_id_type=MESH
        )
    pl.semaphore_wait(barrier, n - 1)
    copies = []
    for k in range(1, n):
        peer = lax.rem(me + k, n)
        for i in range(count):
            source = ins[i] if modes[i] == "gather" else ins[i].at[peer]
            copy = pltpu.make_async_remote_copy(
                source,
                outs[i].at[me],
                send.at[i, k],
                recv.at[i, k],
                device_id={axis: peer},
                device_id_type=MESH,
            )
            copy.start()
            copies.append(copy)
    for i in range(count):
        source = ins[i] if modes[i] == "gather" else ins[i].at[me]
        copy = pltpu.make_async_copy(source, outs[i].at[me], own.at[i])
        copy.start()
        copies.append(copy)
    for copy in copies:
        copy.wait()


class Exchanges:
    def __init__(self, sizes):
        self.sizes = sizes
        self.used = 0

    def __call__(self, axis, arrays, modes):
        n = self.sizes[axis]
        count = len(arrays)
        outs = [
            jax.ShapeDtypeStruct(((n,) + a.shape) if m == "gather" else a.shape, a.dtype)
            for a, m in zip(arrays, modes)
        ]
        self.used += 1
        space = pl.BlockSpec(memory_space=pl.ANY)
        return pl.pallas_call(
            functools.partial(exchange_kernel, axis, n, modes),
            out_shape=outs,
            in_specs=[space] * count,
            out_specs=[space] * count,
            scratch_shapes=[DMA((count, n)), DMA((count, n)), DMA((count,))],
            compiler_params=pltpu.CompilerParams(collective_id=self.used, has_side_effects=True),
            name="exchange_%d" % self.used,
        )(*arrays)


def norm_parts(x):
    mean = jnp.mean(x, -1, keepdims=True)
    cent = x - mean
    factor = lax.rsqrt(jnp.mean(cent * cent, -1, keepdims=True) + EPS)
    return cent * factor, factor


def norm_back(grad, unit, factor, gain):
    scaled = grad * gain
    inner = jnp.mean(scaled * unit, -1, keepdims=True)
    d_input = factor * (scaled - jnp.mean(scaled, -1, keepdims=True) - unit * inner)
    return d_input, jnp.sum(grad * unit, 0), jnp.sum(grad, 0)


def mm(a, b):
    return lax.dot_general(a, b, (((1,), (0,)), ((), ())), preferred_element_type=F32)


def mm_nt(a, b):
    return lax.dot_general(a, b, (((1,), (1,)), ((), ())), preferred_element_type=F32)


def mm_tn(a, b):
    return lax.dot_general(a, b, (((0,), (0,)), ((), ())), preferred_element_type=F32)


def shards(n_dp, n_lat, media, latents, counts, cotangent, g_m, b_m, g_l, b_l, g_f, b_f, wq, wkv, wo, wup, wdown):
    ex = Exchanges({"dp": n_dp, "lat": n_lat})
    micro, per, rows, width = media.shape
    nq = latents.shape[2]
    S = micro * per
    inner = wq.shape[1]
    ff = wup.shape[1]
    ff_part = ff // n_dp
    d_part = width // n_dp
    lat_at = lax.axis_index("lat")
    med = media.reshape(S * rows, width)
    lat = latents.reshape(S * nq, width).astype(F32)
    cot = cotangent.reshape(S * nq, width)
    count = counts.reshape(S)

    small = jnp.stack([g_m, b_m, g_l, b_l, g_f, b_f], 0)
    small_all, wq_all, wkv_all, wo_all = ex("dp", [small, wq, wkv, wo], ["gather"] * 4)
    params = jnp.transpose(small_all, (1, 0, 2)).reshape(6, width).astype(F32)
    wq_all = wq_all.reshape(width, inner)
    wkv_all = wkv_all.reshape(width, 2 * inner)
    wo_all = wo_all.reshape(inner, width)
    wup_cols = jnp.transpose(wup.reshape(d_part, n_dp, ff_part), (1, 0, 2))
    cot_all, wup_s = ex("dp", [cot, wup_cols], ["gather", "swap"])
    cot_all = cot_all.reshape(-1, width)
    wup_s = wup_s.reshape(width, ff_part)

    med_unit, med_factor = norm_parts(med.astype(F32))
    med_norm = (med_unit * params[0] + params[1]).astype(B16)
    lat_unit, lat_factor = norm_parts(lat)
    lat_norm = (lat_unit * params[2] + params[3]).astype(B16)
    query = (mm(lat_norm, wq_all) * 0.125).astype(B16)
    (query_all,) = ex("lat", [query], ["gather"])
    kv_med = mm(med_norm, wkv_all).astype(B16)
    kv_lat = mm(lat_norm, wkv_all).astype(B16)
    keyval = jnp.concatenate(
        [kv_med.reshape(S, rows, 2 * inner), kv_lat.reshape(S, nq, 2 * inner)], 1
    )
    kc = rows + nq
    keys = keyval[:, :, :inner].reshape(S, kc, HEADS, HEAD)
    values = keyval[:, :, inner:].reshape(S, kc, HEADS, HEAD)
    heads_q = query_all.reshape(n_lat, S, nq, HEADS, HEAD)
    slot = (lat_at * rows + lax.iota(jnp.int32, rows)) // VIS
    live = jnp.concatenate(
        [slot[None, :] < count[:, None], jnp.ones((S, nq), dtype=bool)], 1
    )
    score = jnp.einsum("zsqhd,skhd->shzqk", heads_q, keys, preferred_element_type=F32)
    score = jnp.where(live[:, None, None, None, :], score, -1e30)
    top = jnp.max(score, -1)
    p = jnp.exp(score - top[..., None])
    total = jnp.sum(p, -1)
    part = jnp.einsum("shzqk,skhd->zsqhd", p.astype(B16), values, preferred_element_type=F32)
    scale = jnp.transpose(1.0 / total, (2, 0, 3, 1))[..., None]
    part = (part * scale).astype(B16).reshape(n_lat, S * nq, inner)
    stats = jnp.stack([top, total], 0).reshape(2 * S * HEADS, n_lat * nq)
    part_all, stats_all = ex("lat", [part, stats], ["swap", "gather"])
    stats_all = stats_all.reshape(n_lat, 2, S, HEADS, n_lat, nq)
    tops, totals = stats_all[:, 0], stats_all[:, 1]
    top_max = jnp.max(tops, 0)
    weight = totals * jnp.exp(tops - top_max)
    whole = jnp.sum(weight, 0)
    lse = top_max + jnp.log(whole)
    weight = lax.dynamic_index_in_dim(weight / whole, lat_at, 3, keepdims=False)
    weight = jnp.transpose(weight, (0, 1, 3, 2)).reshape(n_lat, S * nq, HEADS, 1)
    attended_f = jnp.sum(part_all.reshape(n_lat, S * nq, HEADS, HEAD).astype(F32) * weight, 0)
    attended = attended_f.reshape(S * nq, inner).astype(B16)

    hidden = lat + mm(attended, wo_all)
    ffn_unit, ffn_factor = norm_parts(hidden)
    ff_norm = (ffn_unit * params[4] + params[5]).astype(B16)
    (ffn_all,) = ex("dp", [ff_norm], ["gather"])
    ffn_all = ffn_all.reshape(-1, width)
    up = mm(ffn_all, wup_s)
    act_f, pull = jax.vjp(lambda v: jax.nn.gelu(v, approximate=False), up)
    act = act_f.astype(B16)
    d_act = mm_nt(cot_all, wdown)
    d_up = pull(d_act)[0].astype(B16)
    out_part = mm(act, wdown).astype(B16).reshape(n_dp, S * nq, width)
    d_ffn_part = mm_nt(d_up, wup_s).astype(B16).reshape(n_dp, S * nq, width)
    d_ffn_all, out_all = ex("dp", [d_ffn_part, out_part], ["swap", "swap"])
    latents_out = (hidden + jnp.sum(out_all.astype(F32), 0)).astype(B16)
    d_ffn = jnp.sum(d_ffn_all.astype(F32), 0)
    grad_down = mm_tn(act, cot_all)
    grad_up = mm_tn(ffn_all, d_up)
    d_h, grad_gf, grad_bf = norm_back(d_ffn, ffn_unit, ffn_factor, params[4])
    d_hidden = cot.astype(F32) + d_h
    d_attn = d_hidden.astype(B16)
    grad_out = mm_tn(attended, d_attn)
    d_att = mm_nt(d_attn, wo_all).astype(B16)
    delta = jnp.sum(
        (d_att.astype(F32) * attended_f.reshape(S * nq, inner)).reshape(S * nq, HEADS, HEAD), -1
    )
    d_att_all, delta_all = ex("lat", [d_att, delta.T], ["gather", "gather"])
    d_att_h = d_att_all.reshape(n_lat, S, nq, HEADS, HEAD)
    delta_h = jnp.transpose(delta_all.reshape(n_lat, HEADS, S, nq), (2, 1, 0, 3))[..., None]
    prob = jnp.exp(score - lse[..., None])
    d_prob = jnp.einsum("zsqhd,skhd->shzqk", d_att_h, values, preferred_element_type=F32)
    d_score = (prob * (d_prob - delta_h)).astype(B16)
    dq_part = jnp.einsum("shzqk,skhd->zsqhd", d_score, keys, preferred_element_type=F32)
    (dq_all,) = ex("lat", [dq_part.astype(B16).reshape(n_lat, S * nq, inner)], ["swap"])
    d_keys = jnp.einsum("shzqk,zsqhd->skhd", d_score, heads_q, preferred_element_type=F32)
    d_values = jnp.einsum(
        "shzqk,zsqhd->skhd", prob.astype(B16), d_att_h, preferred_element_type=F32
    )
    d_kv = jnp.concatenate(
        [d_keys.reshape(S, kc, inner), d_values.reshape(S, kc, inner)], -1
    ).astype(B16)
    d_kv_med = d_kv[:, :rows].reshape(S * rows, 2 * inner)
    d_kv_lat = d_kv[:, rows:].reshape(S * nq, 2 * inner)
    grad_kv = mm_tn(med_norm, d_kv_med) + mm_tn(lat_norm, d_kv_lat)
    d_mnorm = mm_nt(d_kv_med, wkv_all)
    d_media, grad_gm, grad_bm = norm_back(d_mnorm, med_unit, med_factor, params[0])
    dq = (jnp.sum(dq_all.astype(F32), 0) * 0.125).astype(B16)
    grad_q = mm_tn(lat_norm, dq)
    d_lnorm = mm_nt(dq, wq_all) + mm_nt(d_kv_lat, wkv_all)
    d_latn, grad_gl, grad_bl = norm_back(d_lnorm, lat_unit, lat_factor, params[2])
    latent_grad = (d_hidden + d_latn).astype(B16)

    smalls = jnp.stack([grad_gm, grad_bm, grad_gl, grad_bl, grad_gf, grad_bf], 0)
    smalls = jnp.transpose(smalls.reshape(6, n_dp, d_part), (1, 0, 2))
    small_s, q_s, kv_s, o_s, up_s = ex(
        "dp",
        [
            smalls,
            grad_q.astype(B16).reshape(n_dp, d_part, inner),
            grad_kv.astype(B16).reshape(n_dp, d_part, 2 * inner),
            grad_out.astype(B16).reshape(n_dp, inner // n_dp, width),
            grad_up.astype(B16).reshape(n_dp, d_part, ff_part),
        ],
        ["swap"] * 5,
    )
    small_s = jnp.sum(small_s, 0)
    q_s = jnp.sum(q_s.astype(F32), 0)
    kv_s = jnp.sum(kv_s.astype(F32), 0)
    o_s = jnp.sum(o_s.astype(F32), 0)
    up_s = jnp.transpose(up_s, (1, 0, 2)).reshape(d_part, ff)
    pieces = [q_s, kv_s, o_s, up_s, grad_down]
    cut = [x.astype(B16).reshape(n_lat, x.shape[0] // n_lat, x.shape[1]) for x in pieces]
    got = ex("lat", cut + [small_s], ["swap"] * 5 + ["gather"])
    small_s = jnp.sum(got[5], 0)
    summed = [jnp.sum(x.astype(F32), 0).astype(B16) for x in got[:5]]
    full = ex("lat", summed, ["gather"] * 5)
    grads = [x.reshape(y.shape).astype(F32) for x, y in zip(full, pieces)]
    return (
        latents_out.reshape(latents.shape),
        d_media.astype(B16).reshape(media.shape),
        latent_grad.reshape(latents.shape),
        *[small_s[i] for i in range(6)],
        *grads,
    )


PROB_SPLIT = 4
ROWS_STEP = 160
NORMS = (3, 6)
SEND_A = (0, 1)
SEND_B = (2, 3)
SEND_C = ()
SEND_D = ()
HOP1, HOP2 = 2, 4
HOPS_DEXT = (0, 1)
HOPS_MID = (2,)
HOPS_ATT = ()
HOPS_KV = ((1, 3), (3, 4))
HOPS_Q = (5, 6)
HOPS_MED = ((1, 7), (4, 8), (6, 9))
MED_SPLIT = 4
HOP_END = 10

NT, NN, TN = (((1,), (1,)), ((), ())), (((1,), (0,)), ((), ())), (((0,), (0,)), ((), ()))


def dot(a, b, form):
    return lax.dot_general(a, b, form, preferred_element_type=F32)


def centred(x):
    mean = jnp.mean(x, -1, keepdims=True)
    cent = x - mean
    factor = lax.rsqrt(jnp.mean(cent * cent, -1, keepdims=True) + EPS)
    return cent * factor, factor


def back(grad, unit, factor, gain):
    scaled = grad * gain
    inner = jnp.mean(scaled * unit, -1, keepdims=True)
    return factor * (scaled - jnp.mean(scaled, -1, keepdims=True) - unit * inner)


def fused_kernel(geo, refs):
    S, R, Q, D, I, NC, NZ = geo
    KR = R + Q
    per = refs.counts.shape[1]
    B = S * Q
    G = 2
    W = I // G
    HG = HEADS // G
    r = refs
    me = lax.axis_index("dp")
    z = lax.axis_index("lat")
    chip = me // 2
    core = lax.rem(me, 2)
    sib = me + 1 - 2 * core
    other = 1 - core

    def chip_to(k):
        return lax.rem(chip + k, NC)

    def chip_from(k):
        return lax.rem(chip + NC - k, NC)

    def z_to(k):
        return lax.rem(z + k, NZ)

    def z_from(k):
        return lax.rem(z + NZ - k, NZ)

    quads = range(1, NC)
    planes = range(1, NZ)
    used = [0, 0]

    def local(src, dst):
        sem = r.lsem.at[used[0]]
        used[0] += 1
        copy = pltpu.make_async_copy(src, dst, sem)
        copy.start()
        return copy

    def remote(src, dst, **where):
        at = used[1]
        used[1] += 1
        copy = pltpu.make_async_remote_copy(
            src, dst, r.ssem.at[at], r.rsem.at[at], device_id=where, device_id_type=MESH
        )
        copy.start()
        return copy

    class Planned:
        def __init__(self, make):
            at = used[1]
            used[1] += 1

            def build():
                src, dst, where = make()
                return pltpu.make_async_remote_copy(
                    src, dst, r.ssem.at[at], r.rsem.at[at], device_id=where, device_id_type=MESH
                )

            self.build = build

        def start(self):
            self.build().start()

        def wait(self):
            self.build().wait()

        def wait_send(self):
            self.build().wait_send()

        def wait_recv(self):
            self.build().wait_recv()

    class Spread:
        def __init__(self, src_for, dst_at):
            self.dst_at = dst_at
            self.far = [remote(src_for(chip_to(k)), dst_at(me), dp=2 * chip_to(k) + core) for k in quads]
            self.near = remote(src_for(chip), dst_at(me), dp=sib)
            self.own = local(src_for(chip), dst_at(me))

        def forward(self):
            self.passed = []
            for k in quads:
                self.far[k - 1].wait_recv()
                slot = self.dst_at(2 * chip_from(k) + core)
                self.passed.append(remote(slot, slot, dp=sib))

        def finish(self):
            self.own.wait()
            self.near.wait()
            for copy in self.far:
                copy.wait_send()
            for copy in self.passed:
                copy.wait()

    side = chip + 1 - 2 * lax.rem(chip, 2)
    ahead = chip + 2 - 4 * (chip // 2)
    cross = 3 - chip

    class Relay(Spread):
        def __init__(self, src_for, dst_at):
            self.dst_at = dst_at
            self.own = local(src_for(chip), dst_at(me))
            self.far = [remote(src_for(t), dst_at(me), dp=2 * t + core) for t in (side, ahead)]
            self.near = remote(src_for(chip), dst_at(me), dp=sib)
            self.half = dst_at(me).shape[0] // 2

        def forward(self):
            self.passed = []
            h = self.half
            for k, (source, target, at) in enumerate(((side, ahead, 0), (ahead, side, h))):
                self.far[k].wait_recv()
                slot = self.dst_at(2 * source + core)
                part = slot.at[at : at + h]
                self.passed.append(remote(part, part, dp=2 * target + core))
                self.passed.append(remote(slot, slot, dp=sib))

        def forward2(self):
            h = self.half
            self.late = []
            slot = self.dst_at(2 * cross + core)
            for k, at in ((0, 0), (2, h)):
                self.passed[k].wait_recv()
                part = slot.at[at : at + h]
                self.late.append(remote(part, part, dp=sib))

        def finish(self):
            self.own.wait()
            self.near.wait()
            for copy in self.far:
                copy.wait_send()
            for k in (0, 2):
                self.passed[k].wait_send()
            for copy in (self.passed[1], self.passed[3], *self.late):
                copy.wait()

    def to_quad(src_for, dst):
        return [remote(src_for(chip_to(k)), dst, dp=2 * chip_to(k) + core) for k in quads]

    def to_planes(src_for, dst):
        return [remote(src_for(z_to(k)), dst, lat=z_to(k)) for k in planes]

    def wait_all(copies):
        for copy in copies:
            copy.wait()

    class Line:
        def __init__(self, ref, part):
            def flow(p, way):
                return Planned(lambda: (ref.at[p, part], ref.at[p, part], {"lat": jnp.clip(z + way, 0, NZ - 1)}))

            self.up = [flow(p, 1) for p in range(NZ - 1)]
            self.down = [flow(p, -1) for p in range(1, NZ)]

        def flows(self):
            for p in range(NZ - 1):
                yield p, 1, self.up[p]
            for p in range(1, NZ):
                yield p, -1, self.down[p - 1]

        def send(self):
            for p, _, copy in self.flows():
                pl.when(z == p)(copy.start)

        def step(self, far):
            for p, way, copy in self.flows():
                at = p + way * far
                if 0 <= at < NZ:
                    last = at == (NZ - 1 if way > 0 else 0)

                    @pl.when(z == at)
                    def _():
                        copy.wait_recv()
                        if not last:
                            copy.start()

        def finish(self):
            for p, way, copy in self.flows():
                sends = jnp.logical_and(z >= p, z < NZ - 1) if way > 0 else jnp.logical_and(z <= p, z > 0)
                pl.when(sends)(copy.wait_send)

    class Meet:
        def __init__(self, own, got, cross, out, root):
            self.own, self.got, self.crossed, self.out, self.root = own, got, cross, out, root
            peer = 3 - root
            self.up = Planned(lambda: (own, got, {"lat": 1 + z // 2}))
            self.over = Planned(lambda: (own, cross, {"lat": root}))
            self.near = Planned(lambda: (own, out, {"lat": 3 * (root - 1)}))
            self.back = Planned(lambda: (own, out, {"lat": peer}))
            self.far = Planned(lambda: (out, out, {"lat": 3 * (peer - 1)}))
            self.lsem = r.lsem.at[used[0]]
            used[0] += 1

        def send(self):
            @pl.when(jnp.logical_or(z == 0, z == NZ - 1))
            def _():
                self.up.start()

        def merge(self):
            @pl.when(z == 3 - self.root)
            def _():
                self.up.wait_recv()
                self.own[...] = (self.own[...].astype(F32) + self.got[...].astype(F32)).astype(B16)
                self.over.start()

        def total(self):
            @pl.when(z == self.root)
            def _():
                self.up.wait_recv()
                both = self.own[...].astype(F32) + self.got[...].astype(F32)
                self.over.wait_recv()
                self.own[...] = (both + self.crossed[...].astype(F32)).astype(B16)
                self.near.start()
                self.back.start()
                pltpu.make_async_copy(self.own, self.out, self.lsem).start()

        def relay(self):
            @pl.when(z == 3 - self.root)
            def _():
                self.back.wait_recv()
                self.far.start()

        def finish(self):
            root, peer = self.root, 3 - self.root

            @pl.when(jnp.logical_or(z == 0, z == NZ - 1))
            def _():
                self.up.wait_send()

            @pl.when(z == 3 * (root - 1))
            def _():
                self.near.wait_recv()

            @pl.when(z == 3 * (peer - 1))
            def _():
                self.far.wait_recv()

            @pl.when(z == peer)
            def _():
                self.over.wait_send()
                self.far.wait_send()

            @pl.when(z == root)
            def _():
                self.near.wait_send()
                self.back.wait_send()
                pltpu.make_async_copy(self.own, self.out, self.lsem).wait()

    barrier = pltpu.get_barrier_semaphore()
    for k in quads:
        pl.semaphore_signal(barrier, inc=1, device_id={"dp": 2 * chip_to(k) + core}, device_id_type=MESH)
    pl.semaphore_signal(barrier, inc=1, device_id={"dp": sib}, device_id_type=MESH)
    for k in planes:
        pl.semaphore_signal(barrier, inc=1, device_id={"lat": z_to(k)}, device_id_type=MESH)
    pl.semaphore_wait(barrier, NC - 1 + 1 + NZ - 1)

    def whole(ref):
        return lambda _: ref

    def rows_at(ref):
        return lambda d: ref.at[d]

    def cols_at(ref, at, size):
        return lambda d: ref.at[d, :, at : at + size]

    part_rows = D // (2 * NC)
    per_slot = NC

    def up_at(d):
        at = pl.multiple_of(lax.rem(d, per_slot) * part_rows, part_rows)
        return r.ffw.at[2 + d // per_slot, pl.ds(at, part_rows)]

    span = r.wup.shape[1] // NC

    def down_matrix():
        return r.ffw[0:2].reshape(span, D)

    def up_matrix():
        return r.ffw[2:4].reshape(D, span)

    g_small = Spread(whole(r.small), rows_at(r.small_all))
    g_wq = Spread(whole(r.wq), rows_at(r.wq_all))
    lat_in = local(r.lat, r.lat_v)
    counts_in = local(r.counts, r.counts_s)
    cot_in = local(r.cot, r.cot4.at[chip])
    slots = r.med.shape[0]

    def med_copy(s):
        slot = lax.rem(s, slots)
        return pltpu.make_async_copy(r.media.at[s], r.med.at[slot], r.dsem.at[slot])

    def med_first():
        for s in range(slots):
            med_copy(jnp.int32(s)).start()

    def med_next(s):
        @pl.when(s + slots < S)
        def _():
            med_copy(s + slots).start()

    med_first()
    g_small.forward()
    g_small.finish()
    params = r.params
    for d in range(2 * NC):
        params[0:6, d * part_rows : (d + 1) * part_rows] = r.small_all[d].astype(F32)

    def param(i):
        return params[i : i + 1, :]

    lat_in.wait()
    unit, _ = centred(r.lat_v[...].astype(F32))
    r.latn[...] = (unit * param(2) + param(3)).astype(B16)
    rb = ROWS_STEP

    def norm_sample(s, carry):
        slot = lax.rem(s, slots)
        med_copy(s).wait()

        def part(i, inner):
            x = r.med[slot, pl.ds(pl.multiple_of(i * rb, rb), rb), :].astype(F32)
            u, _ = centred(x)
            row = pl.multiple_of(s * KR + i * rb, 16)
            r.X[pl.ds(row, rb), :] = (u * param(0) + param(1)).astype(B16)
            return inner

        lax.fori_loop(0, R // rb, part, 0)
        row = pl.multiple_of(s * KR + R, 16)
        at = pl.multiple_of(s * Q, 16)
        r.X[pl.ds(row, Q), :] = r.latn[pl.ds(at, Q), :]
        med_next(s)
        return carry

    def up_slice(k):
        return r.wup.at[:, pl.ds(pl.multiple_of(k * span, 128), span)]

    def key_cols(s, carry):
        rows = pl.ds(pl.multiple_of(s * KR, 16), KR)
        r.KV[rows, 0:I] = dot(r.X[rows, :], r.wkv_all[:, :, 0:I].reshape(D, I), NN).astype(B16)
        return carry

    def value_cols(s, carry):
        rows = pl.ds(pl.multiple_of(s * KR, 16), KR)
        r.KV[rows, I : 2 * I] = dot(r.X[rows, :], r.wkv_all[:, :, I : 2 * I].reshape(D, I), NN).astype(B16)
        return carry

    first, second = NORMS
    lax.fori_loop(0, first, norm_sample, 0)
    g_key = Relay(lambda _: r.wkv.at[:, 0:I], cols_at(r.wkv_all, 0, I))
    g_wq.forward()
    g_val = Relay(lambda _: r.wkv.at[:, I : 2 * I], cols_at(r.wkv_all, I, I))
    g_wq.finish()
    query = dot(r.latn[...], r.wq_all[...].reshape(D, I), NN) * 0.125
    r.q_all[z] = query.astype(B16).reshape(S, Q, I)
    q_out = to_planes(lambda _: r.q_all.at[z], r.q_all.at[z])
    lax.fori_loop(first, second, norm_sample, 0)
    g_key.forward()
    g_wo = Relay(whole(r.wo), rows_at(r.wo_all))
    lax.fori_loop(second, S, norm_sample, 0)
    med_first()
    g_key.forward2()
    g_val.forward()
    g_up = Spread(up_slice, up_at)
    g_key.finish()
    lax.fori_loop(0, S, key_cols, 0)
    g_val.forward2()
    g_wo.forward()
    g_down = remote(r.wdown, r.ffw.at[core], dp=sib)
    g_down_own = local(r.wdown, r.ffw.at[core])
    g_val.finish()
    lax.fori_loop(0, S, value_cols, 0)
    g_wo.forward2()
    cot_in.wait()
    g_cot = to_quad(lambda _: r.cot, r.cot4.at[chip])
    counts_in.wait()
    wait_all(q_out)

    own_head = (
        lax.broadcasted_iota(jnp.int32, (HG * NZ * Q, W), 0) // (NZ * Q)
        == lax.broadcasted_iota(jnp.int32, (HG * NZ * Q, W), 1) // HEAD
    )
    r.mask[...] = own_head.astype(F32).astype(B16)

    def spread_heads(x):
        return jnp.concatenate([x] * HG, 0) * r.mask[...]

    def take_heads(x):
        low = lax.broadcasted_iota(jnp.int32, (NZ * Q, 2 * HEAD), 1) < HEAD
        cols = []
        for pair in range(HG // 2):
            block = x[:, pair * 2 * HEAD : (pair + 1) * 2 * HEAD]
            n = NZ * Q
            cols.append(
                jnp.where(low, block[2 * pair * n : (2 * pair + 1) * n], block[(2 * pair + 1) * n : (2 * pair + 2) * n])
            )
        return jnp.concatenate(cols, 1)

    def scores(s, g, qbig):
        rows = pl.ds(pl.multiple_of(s * KR, 16), KR)
        raw = dot(r.KV[rows, g * W : (g + 1) * W], qbig, NT)
        row = lax.broadcasted_iota(jnp.int32, raw.shape, 0)
        live = jnp.logical_or(row >= R, row + z * R < r.counts_s[s // per, lax.rem(s, per)] * VIS)
        return jnp.where(live, raw, -1e30)

    def queries(s, g):
        return spread_heads(r.q_all[:, s, :, g * W : (g + 1) * W].reshape(NZ * Q, W))

    def attend(s, carry):
        rows = pl.ds(pl.multiple_of(s * KR, 16), KR)
        for g in range(G):
            score = scores(s, g, queries(s, g))
            top = jnp.max(score, 0, keepdims=True)
            grown = jnp.exp(score - top)
            total = jnp.sum(grown, 0, keepdims=True)
            r.lse[z, pl.ds(g * S + s, 1), :] = top + jnp.log(total)
            prob = (grown * (1.0 / total)).astype(B16)
            part = dot(prob, r.KV[rows, I + g * W : I + (g + 1) * W], TN)
            r.o_send[:, s, :, g * W : (g + 1) * W] = take_heads(part).astype(B16).reshape(NZ, Q, W)

        @pl.when(s == S // 2)
        def _():
            for copy in o_out[: NZ - 1]:
                copy.start()

        return carry

    def half(n):
        return slice(n * (S // 2), (n + 1) * (S // 2))

    def plan(make):
        return [Planned(functools.partial(make, k, n)) for n in range(2) for k in planes]

    o_out = plan(lambda k, n: (r.o_send.at[z_to(k), half(n)], r.o_recv.at[z, half(n)], {"lat": z_to(k)}))
    lax.fori_loop(0, S, attend, 0)
    lse_out = to_planes(lambda _: r.lse.at[z], r.lse.at[z])
    for copy in o_out[NZ - 1 :]:
        copy.start()
    wait_all(lse_out)
    every = r.lse[...]
    top = jnp.max(every, 0)
    lse_all = top + jnp.log(jnp.sum(jnp.exp(every - top[None]), 0))
    r.lse_all[...] = lse_all
    r.lse[...] = jnp.exp(every - lse_all[None])
    pick = (
        lax.rem(lax.broadcasted_iota(jnp.int32, (B, HG * NZ * Q), 1), NZ * Q)
        == lax.rem(lax.broadcasted_iota(jnp.int32, (B, HG * NZ * Q), 0), Q) + z * Q
    )
    for k in range(NZ):
        store = r.hidden if k < 2 else r.d_hidden
        for g in range(G):
            lanes = jnp.broadcast_to(
                r.lse[z_from(k), g * S : (g + 1) * S, :][:, None, :], (S, Q, HG * NZ * Q)
            ).reshape(B, HG * NZ * Q)
            lanes = jnp.where(pick, lanes, 0.0)
            coarse = lanes.astype(B16)
            fine = (lanes - coarse.astype(F32)).astype(B16)
            at = (k % 2) * I + g * W
            store[:, at : at + W] = dot(coarse, r.mask[...], NN) + dot(fine, r.mask[...], NN)
    g_up.forward()
    g_wo.finish()
    wait_all(o_out)
    att = r.hidden[:, 0:I] * r.o_send[z].astype(F32).reshape(B, I)
    for k in planes:
        store = r.hidden if k < 2 else r.d_hidden
        at = (k % 2) * I
        att = att + store[:, at : at + I] * r.o_recv[z_from(k)].astype(F32).reshape(B, I)
    r.att_f[...] = att
    r.att[...] = att.astype(B16)
    hidden = r.lat_v[...].astype(F32) + dot(r.att[...], r.wo_all[...].reshape(I, D), NN)
    r.hidden[...] = hidden
    unit, _ = centred(hidden)
    r.ffn4[chip] = (unit * param(4) + param(5)).astype(B16)
    f_out = to_quad(lambda _: r.ffn4.at[chip], r.ffn4.at[chip])

    def act_grad(b, carry):
        r.d_act[b] = dot(r.cot4[b], down_matrix(), NT)
        return carry

    wait_all(g_cot)
    g_down.wait()
    g_down_own.wait()
    g_up.finish()
    lax.fori_loop(0, NC, act_grad, 0)

    def feed(b):
        r.up[...] = dot(r.ffn4[b], up_matrix(), NN)

        def gelu_part(i, carry):
            rows = pl.ds(pl.multiple_of(i * 32, 32), 32)
            x = r.up[rows, :]
            cdf = 0.5 * (1.0 + lax.erf(x * 0.7071067811865476))
            pdf = jnp.exp(-0.5 * x * x) * 0.3989422804014327
            r.act[b, rows, :] = (x * cdf).astype(B16)
            r.d_up[b, rows, :] = (r.d_act[b, rows, :] * (cdf + x * pdf)).astype(B16)
            return carry

        lax.fori_loop(0, B // 32, gelu_part, 0)
        r.df_send[b] = dot(r.d_up[b], up_matrix(), NT).astype(B16)

    feed(chip)
    df_out = []
    for k in quads:
        f_out[k - 1].wait_recv()
        b = chip_from(k)
        feed(b)
        df_out.append(remote(r.df_send.at[b], r.df_recv.at[chip], dp=2 * b + core))

    own_span = span // 2
    act2 = r.act

    def grad_down(half_core):
        def body(i, carry):
            at = pl.multiple_of(half_core * own_span + i * 256, 256)
            value = dot(
                act2[:, :, pl.ds(at, 256)].reshape(NC * B, 256), r.cot4[...].reshape(NC * B, D), TN
            )
            r.gd[half_core, pl.ds(pl.multiple_of(i * 256, 256), 256), :] = value.astype(B16)
            return carry

        lax.fori_loop(0, own_span // 256, body, 0)

    grad_down(other)
    gd_out = remote(r.gd.at[other], r.gd_recv, dp=sib)
    grad_down(core)
    dw = D // NC
    hw = dw // 2

    def grad_up(i, carry):
        at = pl.multiple_of(i * dw, dw)
        value = dot(
            r.ffn4[:, :, pl.ds(at, dw)].reshape(NC * B, dw), r.d_up[...].reshape(NC * B, span), TN
        ).astype(B16)
        r.gu[0, i] = value[:hw]
        r.gu[1, i] = value[hw:]
        return carry

    lax.fori_loop(0, NC, grad_up, 0)
    gu_out = remote(r.gu.at[other], r.gu_recv, dp=sib)

    piece = own_span // NZ
    gd_out.wait()
    for j in range(NZ):
        rows = slice(j * piece, (j + 1) * piece)
        r.gd_sum[j] = (r.gd[core, rows, :].astype(F32) + r.gd_recv[rows, :].astype(F32)).astype(B16)

    meets = [
        Meet(r.gd_sum.at[j], r.z_got.at[j], r.z_cross.at[j // 2], r.gdown.at[j * piece : (j + 1) * piece, :], 1 + j % 2)
        for j in range(NZ)
    ]
    meets += [
        Meet(r.gu_quad.at[j], r.z_got.at[NZ + j], r.z_cross.at[(NZ + j) // 2], r.gup.at[:, j * span : (j + 1) * span], 1 + j % 2)
        for j in range(NC)
    ]
    for part_, got_, cross_, out_ in (
        (r.go_t, r.go_got, r.go_cross, r.gout),
        (r.gk_t, r.gk_got, r.gk_cross, r.gkv),
        (r.gq_t, r.gq_got, r.gq_cross, r.gquery),
    ):
        rows = part_.shape[1]
        meets += [
            Meet(part_.at[j], got_.at[j], cross_, out_.at[j * rows : (j + 1) * rows, :], 1 + j) for j in range(2)
        ]

    def hop(n):
        if 0 <= n < len(meets):
            meets[n].merge()
        if 0 <= n - HOP1 < len(meets):
            meets[n - HOP1].total()
        if 0 <= n - HOP2 < len(meets):
            meets[n - HOP2].relay()

    for n in SEND_A:
        meets[n].send()
    def down(i, carry):
        r.out_send[i] = dot(r.act[i], down_matrix(), NN).astype(B16)
        return carry

    lax.fori_loop(0, NC, down, 0)
    gu_out.wait()

    for copy in f_out:
        copy.wait_send()
    wait_all(df_out)
    d_ffn = r.df_send[chip].astype(F32)
    for k in quads:
        d_ffn = d_ffn + r.df_recv[chip_to(k)].astype(F32)
    unit, factor = centred(r.hidden[...])
    sums = r.sums
    sums[4:5, :] = jnp.sum(d_ffn * unit, 0, keepdims=True)
    sums[5:6, :] = jnp.sum(d_ffn, 0, keepdims=True)
    d_hidden = r.cot4[chip].astype(F32) + back(d_ffn, unit, factor, param(4))
    r.d_hidden[...] = d_hidden
    r.d_attn[...] = d_hidden.astype(B16)
    d_att = dot(r.d_attn[...], r.wo_all[...].reshape(I, D), NT).astype(B16)
    weighed = d_att.astype(F32) * r.att_f[...]
    lane = lax.broadcasted_iota(jnp.int32, (B, 128), 1)
    delta = jnp.zeros((B, 128), F32)
    low_lane = lax.broadcasted_iota(jnp.int32, (B, 128), 1) < HEAD
    for h in range(HEADS):
        block = weighed[:, (h // 2) * 128 : (h // 2) * 128 + 128]
        keep = low_lane if h % 2 == 0 else jnp.logical_not(low_lane)
        one = jnp.sum(jnp.where(keep, block, 0.0), -1, keepdims=True)
        delta = jnp.where(jnp.logical_or(lane == h, lane == HEADS + h), -one, delta)
    coarse = delta.astype(B16).astype(F32)
    ext = jnp.where(lane < HEADS, coarse, delta - coarse).astype(B16)
    r.d_ext[z, :, :, 0:I] = d_att.reshape(S, Q, I)
    r.d_ext[z, :, :, I : I + 128] = ext.reshape(S, Q, 128)
    line = [Line(r.d_ext, half(n)) for n in range(2)]
    for one in line:
        one.send()

    ow = I // NC
    oh = ow // 2
    for i in range(NC):
        value = dot(r.att[:, i * ow : (i + 1) * ow], r.d_attn[...], TN).astype(B16)
        r.go[0, i] = value[:oh]
        r.go[1, i] = value[oh:]
    go_out = remote(r.go.at[other], r.go_recv, dp=sib)

    def add_pair(dst, a, b, n):
        def body(i, carry):
            dst[i] = (a[i].astype(F32) + b[i].astype(F32)).astype(B16)
            return carry

        lax.fori_loop(0, n, body, 0)

    add_pair(r.gu_sum, r.gu.at[core], r.gu_recv, NC)
    guq_out = to_quad(lambda k: r.gu_sum.at[k], r.gu_quad.at[chip])
    for n in SEND_B:
        meets[n].send()

    def prob_at(s, g):
        lanes = pl.ds(pl.multiple_of(lax.rem(s, 2) * I + g * W, W), W)
        return r.ffw.at[s // 2, 0:KR, lanes]

    def probs(s, carry):
        for g in range(G):
            score = scores(s, g, queries(s, g))
            prob_at(s, g)[...] = jnp.exp(score - r.lse_all[pl.ds(g * S + s, 1), :]).astype(B16)
        return carry

    lax.fori_loop(0, PROB_SPLIT, probs, 0)
    line[0].step(1)
    lax.fori_loop(PROB_SPLIT, S, probs, 0)
    go_out.wait()
    add_pair(r.go_sum, r.go.at[core], r.go_recv, NC)

    def quad_total(own, got):
        total = own[chip].astype(F32)
        for k in quads:
            total = total + got[chip_to(k)].astype(F32)
        return total

    def split_total(dst, own, got):
        total = quad_total(own, got).astype(B16)
        rows = total.shape[0] // 2
        for j in range(2):
            dst[j] = total[j * rows : (j + 1) * rows]

    line[0].step(2)
    line[1].step(1)
    for n in HOPS_DEXT:
        hop(n)
    line[0].step(3)
    line[1].step(2)
    for n in SEND_C:
        meets[n].send()

    ones = jnp.ones((KR, 128), B16)
    lane_e = lax.broadcasted_iota(jnp.int32, (HG * NZ * Q, 128), 1)
    head_e = lax.broadcasted_iota(jnp.int32, (HG * NZ * Q, 128), 0) // (NZ * Q)
    for g in range(G):
        r.mask_e[g] = (
            jnp.logical_or(lane_e == head_e + g * HG, lane_e == head_e + g * HG + HEADS).astype(F32).astype(B16)
        )

    dq_out = plan(lambda k, n: (r.dq_send.at[z_to(k), half(n)], r.dq_recv.at[z, half(n)], {"lat": z_to(k)}))

    def attend_back(s, carry):
        rows = pl.ds(pl.multiple_of(s * KR, 16), KR)

        for g in range(G):
            qbig = queries(s, g)
            prob = prob_at(s, g)[...]
            dbig = spread_heads(r.d_ext[:, s, :, g * W : (g + 1) * W].reshape(NZ * Q, W))
            minus = r.d_ext[:, s, :, I : I + 128].reshape(NZ * Q, 128)
            minus = jnp.concatenate([minus] * HG, 0) * r.mask_e[g]
            d_prob = dot(r.KV[rows, I + g * W : I + (g + 1) * W], dbig, NT) + dot(ones, minus, NT)
            d_score = (prob.astype(F32) * d_prob).astype(B16)
            dq = dot(d_score, r.KV[rows, g * W : (g + 1) * W], TN)
            r.dq_send[:, s, :, g * W : (g + 1) * W] = take_heads(dq).astype(B16).reshape(NZ, Q, W)
            r.KV[rows, g * W : (g + 1) * W] = dot(d_score, qbig, NN).astype(B16)
            r.KV[rows, I + g * W : I + (g + 1) * W] = dot(prob, dbig, NN).astype(B16)
        return carry

    lax.fori_loop(0, S // 2, attend_back, 0)
    for copy in dq_out[: NZ - 1]:
        copy.start()
    goq_out = to_quad(lambda k: r.go_sum.at[k], r.go_quad.at[chip])
    out_out = to_quad(lambda k: r.out_send.at[k], r.out_recv.at[chip])
    for n in HOPS_MID:
        hop(n)
    line[1].step(3)
    for n in SEND_D:
        meets[n].send()
    lax.fori_loop(S // 2, S, attend_back, 0)
    for one in line:
        one.finish()
    for copy in dq_out[NZ - 1 :]:
        copy.start()
    wait_all(guq_out)
    r.gu_quad[chip] = r.gu_sum[chip]
    for n in range(NZ, NZ + NC):
        meets[n].send()
    for n in HOPS_ATT:
        hop(n)

    def kv_chip(i):
        return lax.rem(chip + 1 + i, NC)

    def kv_pair(i):
        return pltpu.make_async_remote_copy(
            r.gk.at[other, kv_chip(i)],
            r.gk_recv.at[kv_chip(i)],
            r.ksem.at[0, i],
            r.ksem.at[1, i],
            device_id={"dp": sib},
            device_id_type=MESH,
        )

    def kv_quad(i):
        return pltpu.make_async_remote_copy(
            r.gk_sum.at[kv_chip(i)],
            r.gk_quad.at[chip],
            r.ksem.at[2, i],
            r.ksem.at[3, i],
            device_id={"dp": 2 * kv_chip(i) + core},
            device_id_type=MESH,
        )

    def kv_add(i):
        kv_pair(i).wait()
        b = kv_chip(i)
        r.gk_sum[b] = (r.gk[core, b].astype(F32) + r.gk_recv[b].astype(F32)).astype(B16)

    def grad_kv(i, carry):
        b = kv_chip(i)
        value = dot(r.X[:, pl.ds(pl.multiple_of(b * dw, dw), dw)], r.KV[...], TN).astype(B16)
        r.gk[0, b] = value[:hw]
        r.gk[1, b] = value[hw:]
        kv_pair(i).start()

        @pl.when(i >= 1)
        def _():
            kv_add(i - 1)
            kv_quad(i - 1).start()

        for at, n in HOPS_KV:

            @pl.when(i == at)
            def _():
                hop(n)

        return carry

    lax.fori_loop(0, NC, grad_kv, 0)

    wait_all(goq_out)
    split_total(r.go_t, r.go_sum, r.go_quad)
    for n in (8, 9):
        meets[n].send()
    wait_all(dq_out)
    dq = r.dq_send[z].astype(F32)
    for k in planes:
        dq = dq + r.dq_recv[z_from(k)].astype(F32)
    r.dq[...] = (dq.reshape(B, I) * 0.125).astype(B16)
    for i in range(NC):
        value = dot(r.latn[:, i * dw : (i + 1) * dw], r.dq[...], TN).astype(B16)
        r.gq[0, i] = value[:hw]
        r.gq[1, i] = value[hw:]
    gqs_out = remote(r.gq.at[other], r.gq_recv, dp=sib)
    kv_add(NC - 1)
    gqs_out.wait()
    add_pair(r.gq_sum, r.gq.at[core], r.gq_recv, NC)
    gqq_out = to_quad(lambda k: r.gq_sum.at[k], r.gq_quad.at[chip])
    for n in HOPS_Q:
        hop(n)

    sums[0:1, :] = jnp.zeros((1, D), F32)
    sums[1:2, :] = jnp.zeros((1, D), F32)
    sums[6:8, :] = jnp.zeros((2, D), F32)

    def media_back(s, carry):
        slot = lax.rem(s, 2)
        held = lax.rem(s, slots)
        rows = pl.ds(pl.multiple_of(s * KR, 16), KR)
        med_copy(s).wait()
        r.dn[...] = dot(r.KV[rows, :], r.wkv_all[...].reshape(D, 2 * I), NT)
        r.d_lat[pl.ds(pl.multiple_of(s * Q, 8), Q), :] = r.dn[R:, :]

        @pl.when(s >= 2)
        def _():
            pltpu.make_async_copy(r.mg.at[slot], r.media_grad.at[s - 2], r.msem.at[slot]).wait()

        def part(i, inner):
            block = pl.ds(pl.multiple_of(i * rb, rb), rb)
            unit, factor = centred(r.med[held, block, :].astype(F32))
            grad = r.dn[block, :]
            sums[0:1, :] += jnp.sum(grad * unit, 0, keepdims=True)
            sums[1:2, :] += jnp.sum(grad, 0, keepdims=True)
            r.mg[slot, block, :] = back(grad, unit, factor, param(0)).astype(B16)
            return inner

        lax.fori_loop(0, R // rb, part, 0)
        pltpu.make_async_copy(r.mg.at[slot], r.media_grad.at[s], r.msem.at[slot]).start()
        med_next(s)
        for at, n in HOPS_MED:

            @pl.when(s == at)
            def _():
                hop(n)

        return carry

    lax.fori_loop(0, MED_SPLIT, media_back, 0)
    for i in range(NC - 1):
        kv_quad(i).wait()
    split_total(r.gk_t, r.gk_sum, r.gk_quad)
    wait_all(gqq_out)
    split_total(r.gq_t, r.gq_sum, r.gq_quad)
    for n in range(10, 14):
        meets[n].send()
    wait_all(out_out)
    out = r.hidden[...] + r.out_send[chip].astype(F32)
    for k in quads:
        out = out + r.out_recv[chip_to(k)].astype(F32)
    r.stage[0] = out.astype(B16)
    put_out = local(r.stage.at[0], r.latents_out)
    lax.fori_loop(MED_SPLIT, S, media_back, 0)

    d_latn = r.d_lat[...] + dot(r.dq[...], r.wq_all[...].reshape(D, I), NT)
    unit, factor = centred(r.lat_v[...].astype(F32))
    sums[2:3, :] = jnp.sum(d_latn * unit, 0, keepdims=True)
    sums[3:4, :] = jnp.sum(d_latn, 0, keepdims=True)
    r.stage[1] = (r.d_hidden[...] + back(d_latn, unit, factor, param(2))).astype(B16)
    put_lat = local(r.stage.at[1], r.latent_grad)

    sp = D // (2 * NC)
    for t in range(NC):
        for cc in range(2):
            d = 2 * t + cc
            r.sm[cc, t] = sums[:, d * sp : (d + 1) * sp]
    sm_out = remote(r.sm.at[other], r.sm_recv, dp=sib)
    hop(HOP_END)
    sm_out.wait()
    r.sm_sum[...] = r.sm[core] + r.sm_recv[...]
    smq_out = to_quad(lambda k: r.sm_sum.at[k], r.sm_quad.at[chip])
    hop(HOP_END + 1)
    wait_all(smq_out)
    r.sm_z[z] = quad_total(r.sm_sum, r.sm_quad)
    zs_out = to_planes(lambda _: r.sm_z.at[z], r.sm_z.at[z])
    hop(HOP_END + 2)
    for n in range(HOP_END + 3, len(meets) + HOP2):
        hop(n)
    wait_all(zs_out)
    r.sm_all[...] = jnp.sum(r.sm_z[...], 0)
    put_small = local(r.sm_all, r.gsmall)
    for meet in meets:
        meet.finish()
    put_small.wait()
    for slot in range(2):
        pltpu.make_async_copy(
            r.mg.at[slot], r.media_grad.at[S - 2 + slot], r.msem.at[slot]
        ).wait()
    put_out.wait()
    put_lat.wait()
    assert used[1] <= r.rsem.shape[0] and used[0] <= r.lsem.shape[0]


def fused(n_dp, n_lat, media, latents, counts, cotangent, g_m, b_m, g_l, b_l, g_f, b_f, wq, wkv, wo, wup, wdown):
    micro, per, R, D = media.shape
    Q = latents.shape[2]
    S = micro * per
    B = S * Q
    I = wq.shape[1]
    NC = n_dp // 2
    NZ = n_lat
    KR = R + Q
    span = wup.shape[1] // NC
    dp_rows = D // n_dp
    small = jnp.stack([g_m, b_m, g_l, b_l, g_f, b_f], 0)
    hbm = pl.BlockSpec(memory_space=pl.ANY)
    ins = dict(
        media=media.reshape(S, R, D),
        lat=latents.reshape(B, D),
        cot=cotangent.reshape(B, D),
        small=small,
        wq=wq,
        wkv=wkv,
        wo=wo,
        wup=wup,
        wdown=wdown,
        counts=counts,
    )
    in_specs = [hbm] * 10
    outs = dict(
        latents_out=((B, D), B16),
        media_grad=((S, R, D), B16),
        latent_grad=((B, D), B16),
        gsmall=((8, dp_rows), F32),
        gquery=((dp_rows, I), B16),
        gkv=((dp_rows, 2 * I), B16),
        gout=((I // n_dp, D), B16),
        gup=((dp_rows, NC * span), B16),
        gdown=((span // 2, D), B16),
    )
    kv_rows = S * KR
    o_rows = I // n_dp
    buffers = dict(
        med=((4, R, D), B16),
        X=((kv_rows, D), B16),
        KV=((kv_rows, 2 * I), B16),
        small_all=((n_dp, 6, dp_rows), B16),
        params=((8, D), F32),
        wq_all=((n_dp, dp_rows, I), B16),
        wkv_all=((n_dp, dp_rows, 2 * I), B16),
        wo_all=((n_dp, o_rows, D), B16),
        ffw=((4, span // 2, D), B16),
        lat_v=((B, D), B16),
        latn=((B, D), B16),
        cot4=((NC, B, D), B16),
        q_all=((NZ, S, Q, I), B16),
        lse=((NZ, 2 * S, NZ * Q * HEADS // 2), F32),
        lse_all=((2 * S, NZ * Q * HEADS // 2), F32),
        mask=((NZ * Q * HEADS // 2, I // 2), B16),
        mask_e=((2, NZ * Q * HEADS // 2, 128), B16),
        o_send=((NZ, S, Q, I), B16),
        o_recv=((NZ, S, Q, I), B16),
        att_f=((B, I), F32),
        att=((B, I), B16),
        hidden=((B, D), F32),
        ffn4=((NC, B, D), B16),
        d_act=((NC, B, span), F32),
        up=((B, span), F32),
        act=((NC, B, span), B16),
        d_up=((NC, B, span), B16),
        df_send=((NC, B, D), B16),
        df_recv=((NC, B, D), B16),
        out_send=((NC, B, D), B16),
        out_recv=((NC, B, D), B16),
        gd=((2, span // 2, D), B16),
        gd_recv=((span // 2, D), B16),
        gd_sum=((NZ, span // 2 // NZ, D), B16),
        gu=((2, NC, dp_rows, span), B16),
        gu_recv=((NC, dp_rows, span), B16),
        gu_sum=((NC, dp_rows, span), B16),
        gu_quad=((NC, dp_rows, span), B16),
        z_got=((2 * NZ, dp_rows, span), B16),
        z_cross=((NZ, dp_rows, span), B16),
        d_hidden=((B, D), F32),
        d_attn=((B, D), B16),
        d_ext=((NZ, S, Q, I + 128), B16),
        dq_send=((NZ, S, Q, I), B16),
        dq_recv=((NZ, S, Q, I), B16),
        dq=((B, I), B16),
        d_lat=((B, D), F32),
        dn=((KR, D), F32),
        mg=((2, R, D), B16),
        stage=((2, B, D), B16),
        sums=((8, D), F32),
        sm=((2, NC, 8, dp_rows), F32),
        sm_recv=((NC, 8, dp_rows), F32),
        sm_sum=((NC, 8, dp_rows), F32),
        sm_quad=((NC, 8, dp_rows), F32),
        sm_z=((NZ, 8, dp_rows), F32),
        sm_all=((8, dp_rows), F32),
    )
    for letter, rows, cols in (("k", dp_rows, 2 * I), ("q", dp_rows, I), ("o", o_rows, D)):
        name = "g" + letter
        buffers[name] = ((2, NC, rows, cols), B16)
        for tail in ("_recv", "_sum", "_quad"):
            buffers[name + tail] = ((NC, rows, cols), B16)
        buffers[name + "_t"] = ((2, rows // 2, cols), B16)
        buffers[name + "_got"] = ((2, rows // 2, cols), B16)
        buffers[name + "_cross"] = ((rows // 2, cols), B16)
    same = dict(gk="gu", gu_sum="act", gd_sum="d_up", gk_sum="df_send", dq_send="o_send", d_lat="up", stage="ffn4")
    for name in same:
        del buffers[name]
    names = list(ins) + list(outs) + list(buffers) + ["lsem", "ssem", "rsem", "msem", "dsem", "ksem", "counts_s"]
    geo = (S, R, Q, D, I, NC, NZ)

    def body(*refs):
        table = dict(zip(names, refs))
        for name, base in same.items():
            table[name] = table[base]
        fused_kernel(geo, types.SimpleNamespace(**table))

    got = pl.pallas_call(
        body,
        out_shape=[jax.ShapeDtypeStruct(s, d) for s, d in outs.values()],
        in_specs=in_specs,
        out_specs=[hbm] * len(outs),
        scratch_shapes=[pltpu.VMEM(s, d) for s, d in buffers.values()]
        + [DMA((40,)), DMA((192,)), DMA((192,)), DMA((2,)), DMA((4,)), DMA((4, 4)), pltpu.SMEM(counts.shape, jnp.int32)],
        compiler_params=pltpu.CompilerParams(
            collective_id=1, has_side_effects=True, vmem_limit_bytes=VMEM_BYTES
        ),
        name="resampler",
    )(*ins.values())
    done = finish(got)
    return (
        done[0].reshape(latents.shape),
        done[1].reshape(media.shape),
        done[2].reshape(latents.shape),
        *done[3:9],
        *done[9:],
    )


def finish_kernel(*refs):
    ins, outs = refs[:9], refs[9:23]
    stage, casts = refs[23:32], refs[32:37]
    sem_in, sem_out = refs[37:]
    parts = ins[1].shape[0]

    def media(s, load):
        if load:
            return pltpu.make_async_copy(ins[1].at[s], stage[1].at[s], sem_in.at[9 + s])
        return pltpu.make_async_copy(stage[1].at[s], outs[1].at[s], sem_out.at[9 + s])

    loads = [pltpu.make_async_copy(ins[i], stage[i], sem_in.at[i]) for i in range(9) if i != 1]
    order = [7, 6, 3, 4, 5, 0, 1, 2]
    for s in range(parts // 2):
        media(s, True).start()
    for i in order[:2]:
        loads[i].start()
    for s in range(parts // 2, parts):
        media(s, True).start()
    for i in order[2:]:
        loads[i].start()
    for s in range(parts // 2):
        media(s, True).wait()
        media(s, False).start()
    stores = []

    def cast_one(i):
        loads[3 + i].wait()
        rows = stage[4 + i].shape[0]
        step = 32

        def cast(k, carry):
            block = pl.ds(pl.multiple_of(k * step, step), step)
            casts[i][block, :] = stage[4 + i][block, :].astype(F32)
            return carry

        lax.fori_loop(0, rows // step, cast, 0)
        copy = pltpu.make_async_copy(casts[i], outs[9 + i], sem_out.at[3 + i])
        copy.start()
        stores.append(copy)

    cast_one(4)
    cast_one(3)
    for s in range(parts // 2, parts):
        media(s, True).wait()
        media(s, False).start()
    for i in range(3):
        cast_one(i)
    for at, i in enumerate((0, 2)):
        loads[at].wait()
        copy = pltpu.make_async_copy(stage[i], outs[i], sem_out.at[i])
        copy.start()
        stores.append(copy)
    loads[2].wait()
    for i in range(6):
        outs[3 + i][...] = stage[3][i]
    for s in range(parts):
        media(s, False).wait()
    for copy in stores:
        copy.wait()


def finish(got):
    hbm = pl.BlockSpec(memory_space=pl.ANY)
    vmem = pl.BlockSpec(memory_space=pltpu.VMEM)
    shapes = [jax.ShapeDtypeStruct(x.shape, x.dtype) for x in got[:3]]
    shapes += [jax.ShapeDtypeStruct((got[3].shape[1],), F32)] * 6
    shapes += [jax.ShapeDtypeStruct(x.shape, F32) for x in got[4:]]
    return pl.pallas_call(
        finish_kernel,
        out_shape=shapes,
        in_specs=[hbm] * 9,
        out_specs=[hbm] * 3 + [vmem] * 6 + [hbm] * 5,
        scratch_shapes=[pltpu.VMEM(x.shape, x.dtype) for x in got]
        + [pltpu.VMEM(x.shape, F32) for x in got[4:]]
        + [DMA((9 + got[1].shape[0],))] * 2,
        compiler_params=pltpu.CompilerParams(vmem_limit_bytes=VMEM_BYTES),
        name="casts",
    )(*got)


def solution(mesh):
    rows4 = P(None, "dp", "lat", None)
    vec = P("dp")
    mat = P("dp", None)
    n_dp, n_lat = mesh.shape["dp"], mesh.shape["lat"]
    body = fused if (n_dp, n_lat) == (8, 4) else shards
    return jax.shard_map(
        functools.partial(body, n_dp, n_lat),
        mesh=mesh,
        in_specs=(rows4, rows4, P(None, "dp"), rows4) + (vec,) * 6 + (mat,) * 5,
        out_specs=(rows4,) * 3 + (vec,) * 6 + (mat,) * 5,
        check_vma=False,
    )
```
